32 devices in a mesh: dp: 4 (over z), row: 4 (over x, core), col: 2 (over y).
Axes of the slice: x: 2, y: 2, z: 4, core: 2. Of those that a mesh axis runs over, the one named last changes fastest.
Arguments:
- tokens: bfloat16 [8, 4096, 1024], P('dp', ('row', 'col')), may hold values from -6 to 6
- cotangent: bfloat16 [8, 4096, 1024], P('dp', ('row', 'col')), may hold values from -6 to 6
- branch: int32 [8, 8], P('dp'), may hold values from 256 to 2048
- ln1_gain: float32 [1024], replicated, may hold values from 0.5 to 1.5
- ln1_bias: float32 [1024], replicated, may hold values from -1.2 to 1.2
- qkv_weight: bfloat16 [1024, 3, 1024], P('row', None, 'col'), may hold values from -0.1875 to 0.1875
- qv_bias: float32 [2, 1024], P(None, 'col'), may hold values from -1.2 to 1.2
- out_weight: bfloat16 [1024, 1024], P('col', 'row'), may hold values from -1.5 to 1.5
- out_bias: float32 [1024], replicated, may hold values from -1.2 to 1.2
- ln2_gain: float32 [1024], replicated, may hold values from 0.5 to 1.5
- ln2_bias: float32 [1024], replicated, may hold values from -1.2 to 1.2
- fc_weight: bfloat16 [1024, 4096], P('row', 'col'), may hold values from -0.1875 to 0.1875
- fc_bias: float32 [4096], P('col'), may hold values from -1.8 to 1.8
- proj_weight: bfloat16 [4096, 1024], P('col', 'row'), may hold values from -0.09375 to 0.09375
- proj_bias: float32 [1024], replicated, may hold values from -1.2 to 1.2
Outputs:
- block_out: bfloat16 [8, 4096, 1024], P('dp', ('row', 'col'))
- input_grad: float32 [8, 4096, 1024], P('dp', ('row', 'col'))
- d_ln1_gain: float32 [1024], replicated
- d_ln1_bias: float32 [1024], replicated
- d_qkv_weight: float32 [1024, 3, 1024], P(('dp', 'row'), None, 'col')
- d_qv_bias: float32 [2, 1024], replicated
- d_out_weight: float32 [1024, 1024], P('col', ('dp', 'row'))
- d_out_bias: float32 [1024], replicated
- d_ln2_gain: float32 [1024], replicated
- d_ln2_bias: float32 [1024], replicated
- d_fc_weight: float32 [1024, 4096], P(('dp', 'row'), 'col')
- d_fc_bias: float32 [4096], replicated
- d_proj_weight: float32 [4096, 1024], P('col', ('dp', 'row'))
- d_proj_bias: float32 [1024], replicated
The draws below stay inside these ranges and needn't reach their ends.
Inputs may be any that keep to these rules, and one draw needn't show every extreme that they name: branch[g, c] is the number of leading prompt tokens that continuation c of group g sees.
All inputs are finite; a program needn't handle non-finite values.
Results may differ from the reference program's by a relative error of at most 0.015.
Values may be sent and summed in bfloat16 or wider, within the bound.
No kernel may reach another device: no remote copies, remote signals or barrier semaphores. Data moves between devices by JAX's collectives and lax.ppermute only.
A program may use at most 328 MiB of HBM per device.

```python
import jax
import jax.numpy as jnp
from jax import lax

D = 1024
HEADS = 16
HEAD = 64
FF = 4096
PLEN = 2048
CLEN = 256
CONTS = 8
GROUP_TOK = 4096
GROUPS = 8


def plant(entries, stream_key, low, high):
    index_at = [jax.random.randint(jax.random.fold_in(stream_key, axis), (), 0, length) for axis, length in enumerate(entries.shape)]
    longest = entries.shape.index(max(entries.shape))
    neighbour = index_at[:longest] + [(index_at[longest] + 1) % entries.shape[longest]] + index_at[longest + 1:]
    return entries.at[tuple(index_at)].set(low).at[tuple(neighbour)].set(high)


def levels(stream_key, dims, split, least, top_value):
    def one(dim, parts):
        draws = jax.random.uniform(jax.random.fold_in(jax.random.fold_in(stream_key, 6), dim), (parts,), jnp.float32, least / len(split), top_value / len(split))
        return jnp.repeat(jnp.exp(draws), dims[dim] // parts).reshape((-1,) + (1,) * (len(dims) - dim - 1))

    loudness = one(*split[0])
    for cut in split[1:]:
        loudness = loudness * one(*cut)
    return loudness


def scatter_about(key, extent, scale, most, shards=(), kind=jnp.bfloat16):
    factor_of = levels(key, extent, shards, -0.22, 0.18) if shards else 1.0
    drawn = jax.random.normal(key, extent, jnp.float32) * scale * factor_of
    return jnp.minimum(jnp.maximum(drawn, -most), most).astype(kind)


def setup_inputs(seed: int = 0) -> dict:
    keys = jax.random.split(jax.random.key(seed), 16)
    return {
        "tokens": scatter_about(keys[0], (GROUPS, GROUP_TOK, D), 1.0, 6.0, ((0, 4), (1, 8))),
        "cotangent": scatter_about(keys[1], (GROUPS, GROUP_TOK, D), 1.0, 6.0, ((0, 4), (1, 8))),
        "branch": plant(jax.random.randint(keys[2], (GROUPS, CONTS), PLEN // 8, PLEN + 1), jax.random.fold_in(keys[2], 1), PLEN // 8, PLEN).astype(jnp.int32),
        "ln1_gain": jnp.clip(1.0 + 0.1 * jax.random.normal(keys[3], (D,), jnp.float32), 0.5, 1.5),
        "ln1_bias": scatter_about(keys[4], (D,), 0.2, 1.2, (), jnp.float32),
        "qkv_weight": scatter_about(keys[5], (D, 3, D), D ** -0.5, 0.1875, ((0, 4), (2, 2))),
        "qv_bias": scatter_about(keys[6], (2, D), 0.2, 1.2, ((1, 2),), jnp.float32),
        "out_weight": scatter_about(keys[7], (D, D), (D // 64) ** -0.5, 1.5, ((0, 2), (1, 4))),
        "out_bias": scatter_about(keys[8], (D,), 0.2, 1.2, (), jnp.float32),
        "ln2_gain": jnp.clip(1.0 + 0.1 * jax.random.normal(keys[9], (D,), jnp.float32), 0.5, 1.5),
        "ln2_bias": scatter_about(keys[10], (D,), 0.2, 1.2, (), jnp.float32),
        "fc_weight": scatter_about(keys[11], (D, FF), D ** -0.5, 0.1875, ((0, 4), (1, 2))),
        "fc_bias": scatter_about(keys[12], (FF,), 0.3, 1.8, ((0, 2),), jnp.float32),
        "proj_weight": scatter_about(keys[13], (FF, D), FF ** -0.5, 0.09375, ((0, 2), (1, 4))),
        "proj_bias": scatter_about(keys[14], (D,), 0.2, 1.2, (), jnp.float32),
    }


@jax.custom_vjp
def low(v):
    return lax.optimization_barrier(v.astype(jnp.bfloat16)).astype(jnp.float32)

@jax.custom_vjp
def low_back(v):
    return v

def low_keep(v):
    return (low(v), None)

def low_pass(kept, grad):
    return (grad,)

def back_keep(v):
    return (v, None)

def back_low(kept, grad):
    return (low(grad),)
low.defvjp(low_keep, low_pass)
low_back.defvjp(back_keep, back_low)
EPSILON = 1e-05
MASKED_SCORE = -1e+30
HIGHEST = lax.Precision.HIGHEST

def normalize(values, gain, shift):
    center = values - lax.optimization_barrier(jnp.mean(values, axis=-1, keepdims=True))
    spread = lax.optimization_barrier(jnp.mean(center * center, axis=-1, keepdims=True))
    return center * lax.rsqrt(spread + EPSILON) * gain + shift

def allowed_keys(row_pos, col_pos, branch_cut):
    row_seg = jnp.where(row_pos >= PLEN, (row_pos - PLEN) // CLEN, -1)
    col_seg = jnp.where(col_pos >= PLEN, (col_pos - PLEN) // CLEN, -1)
    picked = (row_seg[:, None] == jnp.arange(CONTS, dtype=jnp.int32)[None, :]).astype(jnp.int32)
    row_cut = lax.optimization_barrier(jnp.sum(picked * branch_cut[None, :], axis=1))
    causal = col_pos[None, :] <= row_pos[:, None]
    same_seq = col_seg[None, :] == row_seg[:, None]
    in_prefix = (row_seg[:, None] >= 0) & (col_seg[None, :] < 0) & (col_pos[None, :] < row_cut[:, None])
    return same_seq & causal | in_prefix

def attend_block(queries, key_rows, values, branch_cut, offset):
    row_pos = offset + jnp.arange(queries.shape[0], dtype=jnp.int32)
    col_pos = jnp.arange(key_rows.shape[0], dtype=jnp.int32)
    allowed = allowed_keys(row_pos, col_pos, branch_cut)
    scores = jnp.einsum('qhd,khd->hqk', queries, key_rows, precision=HIGHEST) * HEAD ** (-0.5)
    scores = low_back(scores)
    scores = jnp.where(allowed[None], scores, MASKED_SCORE)
    row_peak = lax.optimization_barrier(jnp.max(scores, axis=-1, keepdims=True))
    exponent = jnp.exp(scores - row_peak)
    probabilities = low(exponent / lax.optimization_barrier(jnp.sum(exponent, axis=-1, keepdims=True)))
    return jnp.einsum('hqk,khd->qhd', probabilities, values, precision=HIGHEST)

def forward(residual, branch_cut, params):
    ln1_gain, ln1_bias, qkv_weight, qv_bias, out_weight, out_bias, ln2_gain, ln2_bias, fc_weight, fc_bias, proj_weight, proj_bias = params
    row_total = residual.shape[0]
    normed = low(normalize(residual, ln1_gain, ln1_bias))
    bias_three = jnp.stack([qv_bias[0], jnp.zeros_like(qv_bias[0]), qv_bias[1]])
    projected = jnp.einsum('td,dsf->tsf', normed, qkv_weight, precision=HIGHEST) + bias_three[None]
    projected = low(low_back(projected))
    queries = projected[:, 0].reshape(row_total, HEADS, HEAD)
    key_rows = projected[:, 1].reshape(row_total, HEADS, HEAD)
    values = projected[:, 2].reshape(row_total, HEADS, HEAD)
    q_block = min(512, row_total)
    starts = jnp.arange(row_total // q_block, dtype=jnp.int32) * q_block
    blocked = queries.reshape(row_total // q_block, q_block, HEADS, HEAD)

    def one_block(block_item):
        return attend_block(block_item[0], key_rows, values, branch_cut, block_item[1])
    attended = lax.map(jax.checkpoint(one_block), (blocked, starts))
    attended = low(low_back(attended.reshape(row_total, HEADS * HEAD)))
    branch_out = low_back(jnp.dot(attended, out_weight, precision=HIGHEST) + out_bias)
    middle = residual + branch_out
    normed_two = low(normalize(middle, ln2_gain, ln2_bias))
    hidden = low_back(jnp.dot(normed_two, fc_weight, precision=HIGHEST) + fc_bias)
    active = low(jax.nn.gelu(hidden, approximate=True))
    return middle + low_back(jnp.dot(active, proj_weight, precision=HIGHEST) + proj_bias)

def reference(tokens, cotangent, branch, ln1_gain, ln1_bias, qkv_weight, qv_bias, out_weight, out_bias, ln2_gain, ln2_bias, fc_weight, fc_bias, proj_weight, proj_bias):
    params = tuple((tensor.astype(jnp.float32) for tensor in (ln1_gain, ln1_bias, qkv_weight, qv_bias, out_weight, out_bias, ln2_gain, ln2_bias, fc_weight, fc_bias, proj_weight, proj_bias)))

    def one_group(carry, group_item):
        group_tokens, group_cot, group_cut = group_item
        inputs = group_tokens.astype(jnp.float32)
        output, pull_back = jax.vjp(lambda resid_in, param_in: forward(resid_in, group_cut, param_in), inputs, params)
        grad_input, param_grads = pull_back(group_cot.astype(jnp.float32))
        carry = jax.tree.map(lambda total, extra: total + extra, carry, param_grads)
        return (carry, (output.astype(jnp.bfloat16), grad_input))
    zeros_init = jax.tree.map(jnp.zeros_like, params)
    grads, (block_out, input_grad) = lax.scan(one_group, zeros_init, (tokens, cotangent, branch))
    return (block_out, input_grad, grads[0], grads[1], grads[2], grads[3], grads[4], grads[5], grads[6], grads[7], grads[8], grads[9], grads[10], grads[11])
```

```python
import functools

import jax
import jax.numpy as jnp
from jax import lax
from jax.experimental import pallas as pl
from jax.experimental.pallas import tpu as pltpu
from jax.sharding import PartitionSpec as P

HEAD = 64
PLEN = 2048
CLEN = 256
CONTS = 8


EPSILON = 1e-05
MASKED_SCORE = -1e30
LOG2E = 1.4426950408889634
PAIR = 2 * HEAD
BQ = 256
BK = 512
BK_BACK = 512
HIDDEN_TILE = 512
VMEM_BYTES = 60 * 2**20
NT = (((1,), (1,)), ((), ()))
TN = (((0,), (0,)), ((), ()))
MESH_AXES = ("row", "col")


def normalize(values, gain, shift):
    center = values - jnp.mean(values, axis=-1, keepdims=True)
    spread = jnp.mean(center * center, axis=-1, keepdims=True)
    return center * lax.rsqrt(spread + EPSILON) * gain + shift


def gelu_tanh(values):
    return jax.nn.gelu(values, approximate=True)


def allowed_keys(row_pos, col_pos, branch_cut):
    row_seg = jnp.where(row_pos >= PLEN, (row_pos - PLEN) // CLEN, -1)
    col_seg = jnp.where(col_pos >= PLEN, (col_pos - PLEN) // CLEN, -1)
    picked = (row_seg[:, None] == jnp.arange(CONTS, dtype=jnp.int32)[None, :]).astype(jnp.int32)
    row_cut = jnp.sum(picked * branch_cut[None, :], axis=1)
    causal = col_pos[None, :] <= row_pos[:, None]
    same_seq = col_seg[None, :] == row_seg[:, None]
    in_prefix = (
        (row_seg[:, None] >= 0) & (col_seg[None, :] < 0) & (col_pos[None, :] < row_cut[:, None])
    )
    return same_seq & causal | in_prefix


def add_trees(first, second):
    return jax.tree.map(lambda total, extra: total + extra, first, second)


def gathered_body(
    tokens,
    cotangent,
    branch,
    ln1_gain,
    ln1_bias,
    qkv_weight,
    qv_bias,
    out_weight,
    out_bias,
    ln2_gain,
    ln2_bias,
    fc_weight,
    fc_bias,
    proj_weight,
    proj_bias,
):
    scale = HEAD ** (-0.5)
    width = tokens.shape[2]
    local_rows = tokens.shape[1]
    head_cols = qv_bias.shape[1]
    head_count = head_cols // HEAD
    ff_local = fc_bias.shape[0]
    col_count = lax.axis_size("col")
    row_count = lax.axis_size("row")
    row_rows = local_rows * col_count
    group_rows = row_rows * row_count
    q_block = min(512, row_rows)
    block_count = row_rows // q_block
    row_base = lax.axis_index("row") * row_rows
    col_index = lax.axis_index("col")
    bias_three = jnp.stack([qv_bias[0], jnp.zeros_like(qv_bias[0]), qv_bias[1]])
    key_pos = jnp.arange(group_rows, dtype=jnp.int32)
    block_starts = jnp.arange(block_count, dtype=jnp.int32) * q_block

    def spread_rows(values):
        return lax.all_gather(values, "col", axis=0, tiled=True)

    def spread_grads(values):
        return lax.all_gather(values, "col", axis=0, tiled=True)

    def sum_branch(values):
        return lax.psum_scatter(values, "col", scatter_dimension=0, tiled=True)

    def sum_inputs(values):
        return lax.psum_scatter(values, "col", scatter_dimension=0, tiled=True)

    kept_weights = (
        lax.all_gather(qkv_weight, "row", axis=0, tiled=True),
        lax.all_gather(out_weight, "row", axis=1, tiled=True),
        lax.all_gather(fc_weight, "row", axis=0, tiled=True),
        lax.all_gather(proj_weight, "row", axis=1, tiled=True),
    )

    def block_scores(queries3, keys3, offset, branch_cut):
        q_part = lax.dynamic_slice_in_dim(queries3, offset, q_block, 0)
        row_pos = row_base + offset + jnp.arange(q_block, dtype=jnp.int32)
        allowed = allowed_keys(row_pos, key_pos, branch_cut)
        scores = (
            jnp.einsum("qhd,khd->hqk", q_part, keys3, preferred_element_type=jnp.float32) * scale
        )
        return (q_part, jnp.where(allowed[None], scores, MASKED_SCORE))

    def micro_step(carry, micro_item):
        grads_acc, small_acc = carry
        tok_rows, cot_rows, branch_cut = micro_item
        w_qkv, w_out, w_fc, w_proj = kept_weights
        residual = tok_rows.astype(jnp.float32)
        normed = normalize(residual, ln1_gain, ln1_bias).astype(jnp.bfloat16)
        normed_all = spread_rows(normed)
        projected = jnp.einsum("td,dsf->tsf", normed_all, w_qkv, preferred_element_type=jnp.float32)
        projected = (projected + bias_three[None]).astype(jnp.bfloat16)
        key_rows, value_rows = (
            lax.all_gather(projected[:, 1], "row", axis=0, tiled=True),
            lax.all_gather(projected[:, 2], "row", axis=0, tiled=True),
        )
        queries3 = projected[:, 0].reshape(row_rows, head_count, HEAD)
        keys3 = key_rows.reshape(group_rows, head_count, HEAD)
        values3 = value_rows.reshape(group_rows, head_count, HEAD)

        def attend(offset):
            q_part, scores = block_scores(queries3, keys3, offset, branch_cut)
            row_peak = jnp.max(scores, axis=-1, keepdims=True)
            exponent = jnp.exp(scores - row_peak)
            row_total = jnp.sum(exponent, axis=-1, keepdims=True)
            probs_low = (exponent / row_total).astype(jnp.bfloat16)
            mixed_rows = jnp.einsum(
                "hqk,khd->qhd", probs_low, values3, preferred_element_type=jnp.float32
            )
            return (mixed_rows, (row_peak + jnp.log(row_total))[..., 0])

        attended, log_totals = lax.map(attend, block_starts)
        attended = attended.reshape(row_rows, head_cols).astype(jnp.bfloat16)
        branch_part = jnp.dot(attended, w_out, preferred_element_type=jnp.float32)
        middle = residual + sum_branch(branch_part) + out_bias
        normed_two = normalize(middle, ln2_gain, ln2_bias).astype(jnp.bfloat16)
        normed_two_all = spread_rows(normed_two)
        hidden = jnp.dot(normed_two_all, w_fc, preferred_element_type=jnp.float32) + fc_bias
        active = gelu_tanh(hidden).astype(jnp.bfloat16)
        ffn_part = jnp.dot(active, w_proj, preferred_element_type=jnp.float32)
        output_rows = (middle + sum_branch(ffn_part) + proj_bias).astype(jnp.bfloat16)
        cot_all = spread_grads(cot_rows)
        grad_proj = jnp.einsum("tf,td->fd", active, cot_all, preferred_element_type=jnp.float32)
        grad_proj_bias = jnp.sum(cot_rows.astype(jnp.float32), axis=0)
        grad_active = jnp.einsum("td,fd->tf", cot_all, w_proj, preferred_element_type=jnp.float32)
        grad_hidden = jax.vjp(gelu_tanh, hidden)[1](grad_active)[0].astype(jnp.bfloat16)
        grad_fc = jnp.einsum(
            "td,tf->df", normed_two_all, grad_hidden, preferred_element_type=jnp.float32
        )
        grad_fc_bias = jnp.sum(grad_hidden.astype(jnp.float32), axis=0)
        grad_normed_two = sum_inputs(
            jnp.einsum("tf,df->td", grad_hidden, w_fc, preferred_element_type=jnp.float32)
        )
        back_middle, grad_gain_two, grad_bias_two = jax.vjp(normalize, middle, ln2_gain, ln2_bias)[
            1
        ](grad_normed_two)
        grad_middle = cot_rows.astype(jnp.float32) + back_middle
        grad_out_rows = grad_middle.astype(jnp.bfloat16)
        grad_out_all = spread_grads(grad_out_rows)
        grad_out = jnp.einsum(
            "tc,td->cd", attended, grad_out_all, preferred_element_type=jnp.float32
        )
        grad_out_bias = jnp.sum(grad_out_rows.astype(jnp.float32), axis=0)
        grad_att = jnp.einsum("td,cd->tc", grad_out_all, w_out, preferred_element_type=jnp.float32)
        grad_att = grad_att.astype(jnp.bfloat16).reshape(row_rows, head_count, HEAD)

        def attend_back(acc_pair, block_item):
            offset, log_total = block_item
            grad_keys_acc, grad_values_acc = acc_pair
            q_part, scores = block_scores(queries3, keys3, offset, branch_cut)
            probs = jnp.exp(scores - log_total[..., None])
            probs_low = probs.astype(jnp.bfloat16)
            grad_part = lax.dynamic_slice_in_dim(grad_att, offset, q_block, 0)
            grad_values_acc = grad_values_acc + jnp.einsum(
                "hqk,qhd->khd", probs_low, grad_part, preferred_element_type=jnp.float32
            )
            grad_probs = jnp.einsum(
                "qhd,khd->hqk", grad_part, values3, preferred_element_type=jnp.float32
            )
            center = jnp.sum(grad_probs * probs, axis=-1, keepdims=True)
            grad_scores = (probs * (grad_probs - center)).astype(jnp.bfloat16)
            grad_keys_acc = (
                grad_keys_acc
                + jnp.einsum(
                    "hqk,qhd->khd", grad_scores, q_part, preferred_element_type=jnp.float32
                )
                * scale
            )
            grad_query = (
                jnp.einsum("hqk,khd->qhd", grad_scores, keys3, preferred_element_type=jnp.float32)
                * scale
            )
            return ((grad_keys_acc, grad_values_acc), grad_query)

        empty_keys = jnp.zeros((group_rows, head_count, HEAD), jnp.float32)
        (grad_keys, grad_values), grad_queries = lax.scan(
            attend_back, (empty_keys, empty_keys), (block_starts, log_totals)
        )
        own_keys, own_values = (
            lax.psum_scatter(
                grad_keys.reshape(group_rows, head_cols).astype(jnp.bfloat16),
                "row",
                scatter_dimension=0,
                tiled=True,
            ).astype(jnp.float32),
            lax.psum_scatter(
                grad_values.reshape(group_rows, head_cols).astype(jnp.bfloat16),
                "row",
                scatter_dimension=0,
                tiled=True,
            ).astype(jnp.float32),
        )
        grad_projected = jnp.stack(
            [grad_queries.reshape(row_rows, head_cols), own_keys, own_values], axis=1
        ).astype(jnp.bfloat16)
        grad_qkv = jnp.einsum(
            "td,tsf->dsf", normed_all, grad_projected, preferred_element_type=jnp.float32
        )
        grad_qkv_bias = jnp.sum(grad_projected.astype(jnp.float32), axis=0)
        grad_normed = sum_inputs(
            jnp.einsum("tsf,dsf->td", grad_projected, w_qkv, preferred_element_type=jnp.float32)
        )
        back_input, grad_gain_one, grad_bias_one = jax.vjp(normalize, residual, ln1_gain, ln1_bias)[
            1
        ](grad_normed)
        input_rows = grad_middle + back_input
        weight_terms = (grad_qkv, grad_out, grad_fc, grad_proj)
        small_terms = (
            grad_gain_one,
            grad_bias_one,
            grad_qkv_bias,
            grad_out_bias,
            grad_gain_two,
            grad_bias_two,
            grad_fc_bias,
            grad_proj_bias,
        )
        return (
            (add_trees(grads_acc, weight_terms), add_trees(small_acc, small_terms)),
            (output_rows, input_rows),
        )

    grads_init = (
        jnp.zeros((width, 3, head_cols), jnp.float32),
        jnp.zeros((head_cols, width), jnp.float32),
        jnp.zeros((width, ff_local), jnp.float32),
        jnp.zeros((ff_local, width), jnp.float32),
    )
    vector_zero = jnp.zeros((width,), jnp.float32)
    small_init = (
        vector_zero,
        vector_zero,
        jnp.zeros((3, head_cols), jnp.float32),
        vector_zero,
        vector_zero,
        vector_zero,
        jnp.zeros((ff_local,), jnp.float32),
        vector_zero,
    )
    (grads_acc, small_acc), (block_out, input_grad) = lax.scan(
        micro_step, (grads_init, small_init), (tokens, cotangent, branch)
    )
    (
        gain_one,
        bias_one,
        qkv_bias_acc,
        out_bias_acc,
        gain_two,
        bias_two,
        fc_bias_acc,
        proj_bias_acc,
    ) = small_acc
    qv_full = lax.dynamic_update_slice(
        jnp.zeros((2, width), jnp.float32),
        jnp.stack([qkv_bias_acc[0], qkv_bias_acc[2]]),
        (jnp.int32(0), col_index * head_cols),
    )
    fc_full = lax.dynamic_update_slice(
        jnp.zeros((ff_local * col_count,), jnp.float32), fc_bias_acc, (col_index * ff_local,)
    )
    summed = lax.psum(
        (gain_one, bias_one, qv_full, out_bias_acc, gain_two, bias_two, fc_full, proj_bias_acc),
        ("dp", "row", "col"),
    )
    return (
        block_out,
        input_grad,
        summed[0],
        summed[1],
        lax.psum_scatter(
            grads_acc[0].astype(jnp.bfloat16), ("dp", "row"), scatter_dimension=0, tiled=True
        ).astype(jnp.float32),
        summed[2],
        lax.psum_scatter(
            grads_acc[1].astype(jnp.bfloat16), ("dp", "row"), scatter_dimension=1, tiled=True
        ).astype(jnp.float32),
        summed[3],
        summed[4],
        summed[5],
        lax.psum_scatter(
            grads_acc[2].astype(jnp.bfloat16), ("dp", "row"), scatter_dimension=0, tiled=True
        ).astype(jnp.float32),
        summed[6],
        lax.psum_scatter(
            grads_acc[3].astype(jnp.bfloat16), ("dp", "row"), scatter_dimension=1, tiled=True
        ).astype(jnp.float32),
        summed[7],
    )


def dot(left, right):
    return jnp.dot(left, right, preferred_element_type=jnp.float32)


def dot_nt(left, right):
    return lax.dot_general(left, right, NT, preferred_element_type=jnp.float32)


def cost(flops, moved, exps=0):
    return pl.CostEstimate(flops=int(flops), bytes_accessed=int(moved), transcendentals=int(exps))


def params():
    return pltpu.CompilerParams(vmem_limit_bytes=VMEM_BYTES)


def fixed(shape):
    return pl.BlockSpec(shape, lambda *_: (0,) * len(shape), pipeline_mode=pl.Buffered(1))


def pair_rows(rows):
    low = lax.broadcasted_iota(jnp.int32, rows.shape, 1) < HEAD
    zero = jnp.zeros_like(rows)
    return jnp.concatenate([jnp.where(low, rows, zero), jnp.where(low, zero, rows)], axis=0)


def pick_lanes(stacked):
    half = stacked.shape[0] // 2
    low = lax.broadcasted_iota(jnp.int32, (half, stacked.shape[1]), 1) < HEAD
    return jnp.where(low, stacked[:half], stacked[half:])


def qkv_kernel(rows, groups, x_ref, w_ref, bias_ref, *out_refs):
    depth = w_ref.shape[3]
    for part in range(3):
        weight = w_ref[:, 0, part].reshape(rows * depth, 2 * PAIR)
        values = dot(x_ref[...], weight)
        if part != 1:
            values = values + bias_ref[0, 0 if part == 0 else 1]
        if part == 0:
            values = values * HEAD**-0.5
        values = values.astype(jnp.bfloat16)
        span = values.shape[0] // groups
        for g in range(groups):
            for half in range(2):
                out_refs[g][half, 0, :, part * PAIR : (part + 1) * PAIR] = values[
                    g * span : (g + 1) * span, half * PAIR : (half + 1) * PAIR
                ]


def project_qkv(normed, weight, bias, groups):
    rows, cols, _, depth, width = weight.shape
    tokens, model = normed.shape
    span = tokens // groups
    return pl.pallas_call(
        functools.partial(qkv_kernel, rows, groups),
        grid=(rows // 2, cols),
        in_specs=[
            fixed((tokens, model)),
            pl.BlockSpec((rows, 1, 3, depth, 2 * PAIR), lambda i, c: (0, c, 0, 0, i)),
            pl.BlockSpec((1, 2, 1, 2 * PAIR), lambda i, c: (c, 0, 0, i)),
        ],
        out_specs=[pl.BlockSpec((2, 1, span, 3 * PAIR), lambda i, c: (i, c, 0, 0))] * groups,
        out_shape=[jax.ShapeDtypeStruct((rows, cols, span, 3 * PAIR), jnp.bfloat16)] * groups,
        compiler_params=params(),
        cost_estimate=cost(6 * tokens * model * model, 8 * tokens * model + 6 * model * model),
        name="qkv",
    )(normed, weight, bias)


def attend_kernel(
    bk, cut_ref, qkv_ref, o_ref, lse_ref, s_ref, own_ref, value_ref, peak_ref, acc_ref
):
    i = pl.program_id(0)
    prompt_blocks = PLEN // BQ

    @pl.when(i == 0)
    def _():
        value_ref[:, :PAIR] = qkv_ref[:, 2 * PAIR : 3 * PAIR]
        value_ref[:, PAIR:] = jnp.ones((value_ref.shape[0], PAIR), value_ref.dtype)

    start = pl.multiple_of(i * BQ, BQ)
    queries = pair_rows(qkv_ref[pl.ds(start, BQ), 0:PAIR])
    limit = jnp.where(i < prompt_blocks, start, cut_ref[jnp.maximum(i - prompt_blocks, 0)])
    full = limit // bk
    rest = limit - full * bk

    def scores(first, count):
        keys = qkv_ref[pl.ds(pl.multiple_of(first, BQ), count), PAIR : 2 * PAIR]
        return dot_nt(queries, keys) * LOG2E

    def lane_peak(values):
        return functools.reduce(
            jnp.maximum, [values[:, at : at + 128] for at in range(0, values.shape[1], 128)]
        )

    own = scores(start, BQ)
    row = lax.broadcasted_iota(jnp.int32, own.shape, 0) & (BQ - 1)
    own = jnp.where(lax.broadcasted_iota(jnp.int32, own.shape, 1) <= row, own, MASKED_SCORE)
    own_ref[...] = own
    peak_ref[...] = lane_peak(own)

    def score_step(j, none):
        values = scores(j * bk, bk)
        s_ref[j] = values
        peak_ref[...] = jnp.maximum(peak_ref[...], lane_peak(values))
        return none

    lax.fori_loop(0, full, score_step, 0)

    @pl.when(rest > 0)
    def _():
        values = scores(full * bk, bk)
        seen = lax.broadcasted_iota(jnp.int32, values.shape, 1) < rest
        values = jnp.where(seen, values, MASKED_SCORE)
        s_ref[full] = values
        peak_ref[...] = jnp.maximum(peak_ref[...], lane_peak(values))

    peak = jnp.max(peak_ref[...], axis=1, keepdims=True)
    probs = jnp.exp2(own_ref[...] - peak).astype(jnp.bfloat16)
    acc_ref[...] = dot(probs, value_ref[pl.ds(start, BQ), :])

    def value_step(j, none):
        probs = jnp.exp2(s_ref[j] - peak).astype(jnp.bfloat16)
        acc_ref[...] += dot(probs, value_ref[pl.ds(pl.multiple_of(j * bk, bk), bk), :])
        return none

    lax.fori_loop(0, full + jnp.where(rest > 0, 1, 0), value_step, 0)
    total = acc_ref[:, PAIR:]
    o_ref[...] = pick_lanes(acc_ref[:, :PAIR] / total).astype(o_ref.dtype)
    lse_ref[0] = jnp.transpose(peak + jnp.log2(total))[:8]


def attend(cut, qkv):
    tokens = qkv.shape[0]
    blocks = tokens // BQ
    pairs = 2 * tokens * tokens // 4
    return pl.pallas_call(
        functools.partial(attend_kernel, BK),
        grid=(blocks,),
        in_specs=[pl.BlockSpec(memory_space=pltpu.SMEM), fixed((tokens, 3 * PAIR))],
        out_specs=[
            pl.BlockSpec((BQ, PAIR), lambda i: (i, 0)),
            pl.BlockSpec((1, 8, 2 * BQ), lambda i: (i, 0, 0)),
        ],
        out_shape=[
            jax.ShapeDtypeStruct((tokens, PAIR), jnp.bfloat16),
            jax.ShapeDtypeStruct((blocks, 8, 2 * BQ), jnp.float32),
        ],
        scratch_shapes=[
            pltpu.VMEM((PLEN // BK, 2 * BQ, BK), jnp.float32),
            pltpu.VMEM((2 * BQ, BQ), jnp.float32),
            pltpu.VMEM((tokens, 2 * PAIR), jnp.bfloat16),
            pltpu.VMEM((2 * BQ, PAIR), jnp.float32),
            pltpu.VMEM((2 * BQ, 2 * PAIR), jnp.float32),
        ],
        compiler_params=params(),
        cost_estimate=cost(8 * 2 * pairs * 256, 2 * tokens * 4 * PAIR, pairs),
        name="attend",
    )(cut, qkv)


def attend_back_kernel(
    bk, cut_ref, qkv_ref, o_ref, do_ref, lse_ref, out_ref, dk_ref, dv_ref, dq_ref
):
    i = pl.program_id(0)
    prompt_blocks = PLEN // BQ

    @pl.when(i == 0)
    def _():
        dk_ref[...] = jnp.zeros_like(dk_ref)
        dv_ref[...] = jnp.zeros_like(dv_ref)

    start = pl.multiple_of(i * BQ, BQ)
    queries = pair_rows(qkv_ref[pl.ds(start, BQ), 0:PAIR])
    grad = do_ref[pl.ds(start, BQ), :]
    grads = pair_rows(grad)
    mixed = jnp.transpose(
        grad.astype(jnp.float32) * o_ref[pl.ds(start, BQ), :].astype(jnp.float32)
    )
    center = jnp.concatenate(
        [
            jnp.sum(mixed[:HEAD], axis=0, keepdims=True),
            jnp.sum(mixed[HEAD:], axis=0, keepdims=True),
        ],
        axis=1,
    )
    log_total = lse_ref[0, 0:1, :]
    limit = jnp.where(i < prompt_blocks, start, cut_ref[jnp.maximum(i - prompt_blocks, 0)])
    full = limit // bk
    rest = limit - full * bk

    def block(first, count, keep, begin):
        at = pl.ds(pl.multiple_of(first, BQ), count)
        keys = qkv_ref[at, PAIR : 2 * PAIR]
        values = qkv_ref[at, 2 * PAIR : 3 * PAIR]
        probs = jnp.exp2(dot_nt(keys, queries) * LOG2E - log_total)
        if keep is not None:
            probs = jnp.where(keep(probs.shape), probs, 0.0)
        dv_ref[at, :] += dot(probs.astype(jnp.bfloat16), grads)
        grad_probs = dot_nt(values, grads)
        grad_scores = (probs * (grad_probs - center)).astype(jnp.bfloat16)
        dk_ref[at, :] += dot(grad_scores, queries)
        part = lax.dot_general(keys, grad_scores, TN, preferred_element_type=jnp.float32)
        dq_ref[...] = part if begin else dq_ref[...] + part

    def causal(shape):
        key = lax.broadcasted_iota(jnp.int32, shape, 0)
        query = lax.broadcasted_iota(jnp.int32, shape, 1) & (BQ - 1)
        return key <= query

    block(start, BQ, causal, True)

    def step(j, none):
        block(j * bk, bk, None, False)
        return none

    lax.fori_loop(0, full, step, 0)

    @pl.when(rest > 0)
    def _():
        block(full * bk, bk, lambda s: lax.broadcasted_iota(jnp.int32, s, 0) < rest, False)

    grad_query = pick_lanes(jnp.transpose(dq_ref[...])) * HEAD**-0.5
    out_ref[pl.ds(start, BQ), 0:PAIR] = grad_query.astype(out_ref.dtype)

    @pl.when(i == pl.num_programs(0) - 1)
    def _():
        out_ref[:, PAIR : 2 * PAIR] = dk_ref[...].astype(out_ref.dtype)
        out_ref[:, 2 * PAIR : 3 * PAIR] = dv_ref[...].astype(out_ref.dtype)


def attend_back(cut, qkv, att, grad_att, log_totals):
    tokens = qkv.shape[0]
    pairs = 2 * tokens * tokens // 4
    return pl.pallas_call(
        functools.partial(attend_back_kernel, BK_BACK),
        grid=(tokens // BQ,),
        in_specs=[
            pl.BlockSpec(memory_space=pltpu.SMEM),
            fixed((tokens, 3 * PAIR)),
            fixed((tokens, PAIR)),
            fixed((tokens, PAIR)),
            pl.BlockSpec((1, 8, 2 * BQ), lambda i: (i, 0, 0)),
        ],
        out_specs=fixed((tokens, 3 * PAIR)),
        out_shape=jax.ShapeDtypeStruct((tokens, 3 * PAIR), jnp.bfloat16),
        scratch_shapes=[
            pltpu.VMEM((tokens, PAIR), jnp.float32),
            pltpu.VMEM((tokens, PAIR), jnp.float32),
            pltpu.VMEM((PAIR, 2 * BQ), jnp.float32),
        ],
        compiler_params=params(),
        cost_estimate=cost(10 * 2 * pairs * 256, 2 * tokens * 8 * PAIR, pairs),
        name="attend_back",
    )(cut, qkv, att, grad_att, log_totals)


def centered(values):
    center = values - jnp.mean(values, axis=-1, keepdims=True)
    spread = jnp.mean(center * center, axis=-1, keepdims=True)
    inverse = lax.rsqrt(spread + EPSILON)
    return center * inverse, inverse


def norm_back(grad, gain, unit, inverse):
    scaled = grad * gain
    mean_one = jnp.mean(scaled, axis=-1, keepdims=True)
    mean_two = jnp.mean(scaled * unit, axis=-1, keepdims=True)
    return (scaled - mean_one - unit * mean_two) * inverse


def middle_kernel(
    rows, cols, tok_ref, att_ref, w_ref, vec_ref, middle_ref, normed_ref, turned_ref
):
    parts = []
    for c in range(cols):
        parts.append(jnp.concatenate([att_ref[r, c] for r in range(rows)], axis=1))
    pieces = []
    for r in range(rows):
        total = dot(parts[0], w_ref[r, 0])
        for c in range(1, cols):
            total = total + dot(parts[c], w_ref[r, c])
        pieces.append(total)
    middle = tok_ref[0].astype(jnp.float32) + jnp.concatenate(pieces, axis=1) + vec_ref[0:1]
    middle_ref[...] = middle
    normed = (centered(middle)[0] * vec_ref[1:2] + vec_ref[2:3]).astype(jnp.bfloat16)
    normed_ref[...] = normed
    turned_ref[...] = jnp.transpose(normed)


def project_out(tokens, att, weight, vectors, g):
    rows, cols, span, _ = att.shape
    model = tokens.shape[2]
    tile = min(256, span)
    return pl.pallas_call(
        functools.partial(middle_kernel, rows, cols),
        grid=(span // tile,),
        in_specs=[
            pl.BlockSpec((1, tile, model), lambda i: (g, i, 0)),
            pl.BlockSpec((rows, cols, tile, PAIR), lambda i: (0, 0, i, 0)),
            fixed(weight.shape),
            fixed(vectors.shape),
        ],
        out_specs=[
            pl.BlockSpec((tile, model), lambda i: (i, 0)),
            pl.BlockSpec((tile, model), lambda i: (i, 0)),
            pl.BlockSpec((model, tile), lambda i: (0, i)),
        ],
        out_shape=[
            jax.ShapeDtypeStruct((span, model), jnp.float32),
            jax.ShapeDtypeStruct((span, model), jnp.bfloat16),
            jax.ShapeDtypeStruct((model, span), jnp.bfloat16),
        ],
        compiler_params=params(),
        cost_estimate=cost(2 * span * model * model, 2 * model * model + 12 * span * model),
        name="out_norm",
    )(tokens, att, weight, vectors)


def hidden_kernel(rows, dps, groups, *refs):
    normed_refs = refs[:groups]
    turned_refs = refs[groups : 2 * groups]
    middle_refs = refs[2 * groups : 3 * groups]
    (cot_ref, cot_turned_ref, fc_ref, fc_bias_ref, proj_ref, proj_bias_ref) = refs[
        3 * groups : 3 * groups + 6
    ]
    (out_ref, back_ref, grad_fc_ref, grad_proj_ref, bias_ref) = refs[
        3 * groups + 6 : 3 * groups + 11
    ]
    normed_all, turned_all, out_acc, back_acc = refs[3 * groups + 11 :]
    step = pl.program_id(0) * pl.num_programs(1) + pl.program_id(1)
    last = pl.num_programs(0) * pl.num_programs(1) - 1
    span = normed_refs[0].shape[0]
    model = normed_all.shape[1]
    depth = model // rows
    tile = fc_ref.shape[3]

    @pl.when(step == 0)
    def _():
        for g in range(groups):
            normed_all[g * span : (g + 1) * span, :] = normed_refs[g][...]
            turned_all[:, g * span : (g + 1) * span] = turned_refs[g][...]

    fc_weight = fc_ref[:, 0].reshape(model, tile)
    hidden = dot(normed_all[...], fc_weight) + fc_bias_ref[0]
    root = 0.7978845608028654
    square = hidden * hidden
    inner = jnp.tanh(hidden * (root + (root * 0.044715) * square))
    plus = 0.5 + 0.5 * inner
    active = (hidden * plus).astype(jnp.bfloat16)
    slope = plus + hidden * (0.5 - 0.5 * inner * inner) * (root + (3 * root * 0.044715) * square)
    cot = cot_ref[...]
    grad_active = None
    for r in range(rows):
        part = dot_nt(cot[:, r * depth : (r + 1) * depth], proj_ref[r, 0])
        grad_active = part if grad_active is None else grad_active + part
    grad_hidden = grad_active * slope
    grad_low = grad_hidden.astype(jnp.bfloat16)
    bias_ref[0] = jnp.sum(grad_low.astype(jnp.float32), axis=0, keepdims=True)
    grad_fc = dot(turned_all[...], grad_low).astype(jnp.bfloat16)
    grad_proj = dot(cot_turned_ref[...], active).astype(jnp.bfloat16)
    cut = model // (rows * dps)
    for r in range(rows):
        for d in range(dps):
            at = (d * rows + r) * cut
            grad_fc_ref[r, 0, d] = grad_fc[at : at + cut]
            grad_proj_ref[r, 0, d] = grad_proj[at : at + cut]
    for r in range(rows):
        lanes = slice(r * depth, (r + 1) * depth)
        forward = dot(active, proj_ref[r, 0])
        backward = dot_nt(grad_low, fc_ref[r, 0])

        @pl.when(step == 0)
        def _():
            out_acc[:, lanes] = forward
            back_acc[:, lanes] = backward

        @pl.when(step > 0)
        def _():
            out_acc[:, lanes] += forward
            back_acc[:, lanes] += backward

    @pl.when(step == last)
    def _():
        for g in range(groups):
            at = slice(g * span, (g + 1) * span)
            out_ref[g] = (middle_refs[g][...] + out_acc[at] + proj_bias_ref[...]).astype(
                out_ref.dtype
            )
            back_ref[g] = back_acc[at]


def feed_forward(normed, turned, middle, cot, cot_turned, fc, fc_bias, proj, proj_bias, dps):
    groups = len(normed)
    span, model = normed[0].shape
    tokens = groups * span
    rows, cols, depth, local = fc.shape
    tile = min(HIDDEN_TILE, local)
    cut = model // (rows * dps)
    grad_spec = pl.BlockSpec((rows, 1, dps, cut, tile), lambda c, i: (0, c, 0, 0, i))
    grad_shape = jax.ShapeDtypeStruct((rows, cols, dps, cut, local), jnp.bfloat16)
    return pl.pallas_call(
        functools.partial(hidden_kernel, rows, dps, groups),
        grid=(cols, local // tile),
        in_specs=[fixed((span, model))] * groups
        + [fixed((model, span))] * groups
        + [fixed((span, model))] * groups
        + [
            fixed((tokens, model)),
            fixed((model, tokens)),
            pl.BlockSpec((rows, 1, depth, tile), lambda c, i: (0, c, 0, i)),
            pl.BlockSpec((1, 1, tile), lambda c, i: (c, 0, i)),
            pl.BlockSpec((rows, 1, tile, depth), lambda c, i: (0, c, i, 0)),
            fixed((1, model)),
        ],
        out_specs=[
            fixed((groups, span, model)),
            fixed((groups, span, model)),
            grad_spec,
            grad_spec,
            pl.BlockSpec((1, 1, tile), lambda c, i: (c, 0, i)),
        ],
        out_shape=[
            jax.ShapeDtypeStruct((groups, span, model), jnp.bfloat16),
            jax.ShapeDtypeStruct((groups, span, model), jnp.float32),
            grad_shape,
            grad_shape,
            jax.ShapeDtypeStruct((cols, 1, local), jnp.float32),
        ],
        scratch_shapes=[
            pltpu.VMEM((tokens, model), jnp.bfloat16),
            pltpu.VMEM((model, tokens), jnp.bfloat16),
            pltpu.VMEM((tokens, model), jnp.float32),
            pltpu.VMEM((tokens, model), jnp.float32),
        ],
        compiler_params=params(),
        cost_estimate=cost(
            12 * tokens * model * cols * local, 8 * model * cols * local, tokens * cols * local
        ),
        name="feed_forward",
    )(*normed, *turned, *middle, cot, cot_turned, fc, fc_bias, proj, proj_bias)


def middle_back_kernel(
    rows, cols, grad_ref, middle_ref, cot_ref, w_ref, vec_ref, dx_ref, turned_ref, datt_ref, sum_ref
):
    grad = grad_ref[0]
    unit, inverse = centered(middle_ref[...])
    total = cot_ref[0].astype(jnp.float32) + norm_back(grad, vec_ref[1:2], unit, inverse)
    dx_ref[...] = total
    low = total.astype(jnp.bfloat16)
    turned_ref[...] = jnp.transpose(low)
    depth = w_ref.shape[3]
    for c in range(cols):
        part = dot_nt(low[:, :depth], w_ref[0, c])
        for r in range(1, rows):
            part = part + dot_nt(low[:, r * depth : (r + 1) * depth], w_ref[r, c])
        part = part.astype(jnp.bfloat16)
        for r in range(rows):
            datt_ref[r, c] = part[:, r * PAIR : (r + 1) * PAIR]

    @pl.when(pl.program_id(0) == 0)
    def _():
        sum_ref[...] = jnp.zeros_like(sum_ref)

    sum_ref[0:1] += jnp.sum(grad * unit, axis=0, keepdims=True)
    sum_ref[1:2] += jnp.sum(grad, axis=0, keepdims=True)
    sum_ref[2:3] += jnp.sum(low.astype(jnp.float32), axis=0, keepdims=True)


def middle_back(grad, middle, cot, weight, vectors, g):
    span, model = middle.shape
    rows, cols = weight.shape[:2]
    tile = min(256, span)
    return pl.pallas_call(
        functools.partial(middle_back_kernel, rows, cols),
        grid=(span // tile,),
        in_specs=[
            pl.BlockSpec((1, tile, model), lambda i: (g, i, 0)),
            pl.BlockSpec((tile, model), lambda i: (i, 0)),
            pl.BlockSpec((1, tile, model), lambda i: (g, i, 0)),
            fixed(weight.shape),
            fixed(vectors.shape),
        ],
        out_specs=[
            pl.BlockSpec((tile, model), lambda i: (i, 0)),
            pl.BlockSpec((model, tile), lambda i: (0, i)),
            pl.BlockSpec((rows, cols, tile, PAIR), lambda i: (0, 0, i, 0)),
            pl.BlockSpec((8, model), lambda i: (0, 0)),
        ],
        out_shape=[
            jax.ShapeDtypeStruct((span, model), jnp.float32),
            jax.ShapeDtypeStruct((model, span), jnp.bfloat16),
            jax.ShapeDtypeStruct((rows, cols, span, PAIR), jnp.bfloat16),
            jax.ShapeDtypeStruct((8, model), jnp.float32),
        ],
        compiler_params=params(),
        cost_estimate=cost(2 * span * model * model, 2 * model * model + 18 * span * model),
        name="out_norm_back",
    )(grad, middle, cot, weight, vectors)


def out_grad_kernel(rows, dps, groups, *refs):
    out_ref = refs[2 * groups]
    total = None
    for g in range(groups):
        att = jnp.concatenate([refs[groups + g][r, 0] for r in range(rows)], axis=1)
        part = dot(refs[g][...], att)
        total = part if total is None else total + part
    total = total.astype(jnp.bfloat16)
    cut = out_ref.shape[3]
    for r in range(rows):
        for d in range(dps):
            at = (d * rows + r) * cut
            out_ref[r, 0, d] = total[at : at + cut]


def out_grad(turned, att, dps):
    groups = len(turned)
    model, span = turned[0].shape
    rows, cols = att[0].shape[:2]
    cut = model // (rows * dps)
    return pl.pallas_call(
        functools.partial(out_grad_kernel, rows, dps, groups),
        grid=(cols,),
        in_specs=[fixed((model, span))] * groups
        + [pl.BlockSpec((rows, 1, span, PAIR), lambda c: (0, c, 0, 0))] * groups,
        out_specs=pl.BlockSpec((rows, 1, dps, cut, rows * PAIR), lambda c: (0, c, 0, 0, 0)),
        out_shape=jax.ShapeDtypeStruct((rows, cols, dps, cut, rows * PAIR), jnp.bfloat16),
        compiler_params=params(),
        cost_estimate=cost(2 * groups * span * model * model, 2 * model * model),
        name="out_grad",
    )(*turned, *att)


def input_kernel(rows, dps, groups, *refs):
    grad_refs = refs[:groups]
    dx_refs = refs[groups : 2 * groups]
    (turned_ref, tok_ref, w_ref, gain_ref) = refs[2 * groups : 2 * groups + 4]
    (out_ref, grad_ref, bias_ref, sum_ref) = refs[2 * groups + 4 : 2 * groups + 8]
    acc = refs[2 * groups + 8]
    step = pl.program_id(0) * pl.num_programs(1) + pl.program_id(1)
    last = pl.num_programs(0) * pl.num_programs(1) - 1
    span = dx_refs[0].shape[0]
    depth = w_ref.shape[3]
    cut = grad_ref.shape[4]
    grads = []
    for part in range(3):
        lanes = slice(part * PAIR, (part + 1) * PAIR)
        grads.append(
            jnp.concatenate(
                [
                    jnp.concatenate([ref[half, 0, :, lanes] for half in range(2)], axis=1)
                    for ref in grad_refs
                ],
                axis=0,
            )
        )
    for part in range(3):
        weight_grad = dot(turned_ref[...], grads[part]).astype(jnp.bfloat16)
        for r in range(rows):
            for d in range(dps):
                at = (d * rows + r) * cut
                grad_ref[r, 0, d, part] = weight_grad[at : at + cut]
        bias_ref[0, part] = jnp.sum(grads[part].astype(jnp.float32), axis=0, keepdims=True)
    for r in range(rows):
        lanes = slice(r * depth, (r + 1) * depth)
        piece = dot_nt(grads[0], w_ref[r, 0, 0])
        for part in range(1, 3):
            piece = piece + dot_nt(grads[part], w_ref[r, 0, part])

        @pl.when(step == 0)
        def _():
            acc[:, lanes] = piece

        @pl.when(step > 0)
        def _():
            acc[:, lanes] += piece

    @pl.when(step == last)
    def _():
        gain_sum = None
        for g in range(groups):
            grad = acc[g * span : (g + 1) * span]
            unit, inverse = centered(tok_ref[g].astype(jnp.float32))
            out_ref[g] = dx_refs[g][...] + norm_back(grad, gain_ref[...], unit, inverse)
            gains = jnp.sum(grad * unit, axis=0, keepdims=True)
            shifts = jnp.sum(grad, axis=0, keepdims=True)
            gain_sum = gains if gain_sum is None else gain_sum + gains
            shift_sum = shifts if g == 0 else shift_sum + shifts
        sum_ref[0:1] = gain_sum
        sum_ref[1:2] = shift_sum


def input_back(grads, dx, normed_turned, tokens, weight, gain, dps):
    groups = len(grads)
    rows, cols, _, depth, width = weight.shape
    span, model = dx[0].shape
    cut = model // (rows * dps)
    count = groups * span
    return pl.pallas_call(
        functools.partial(input_kernel, rows, dps, groups),
        grid=(rows // 2, cols),
        in_specs=[pl.BlockSpec((2, 1, span, 3 * PAIR), lambda i, c: (i, c, 0, 0))] * groups
        + [fixed((span, model))] * groups
        + [
            fixed((model, count)),
            fixed((groups, span, model)),
            pl.BlockSpec((rows, 1, 3, depth, 2 * PAIR), lambda i, c: (0, c, 0, 0, i)),
            fixed((1, model)),
        ],
        out_specs=[
            fixed((groups, span, model)),
            pl.BlockSpec((rows, 1, dps, 3, cut, 2 * PAIR), lambda i, c: (0, c, 0, 0, 0, i)),
            pl.BlockSpec((1, 3, 1, 2 * PAIR), lambda i, c: (c, 0, 0, i)),
            fixed((8, model)),
        ],
        out_shape=[
            jax.ShapeDtypeStruct((groups, span, model), jnp.float32),
            jax.ShapeDtypeStruct((rows, cols, dps, 3, cut, width), jnp.bfloat16),
            jax.ShapeDtypeStruct((cols, 3, 1, width), jnp.float32),
            jax.ShapeDtypeStruct((8, model), jnp.float32),
        ],
        scratch_shapes=[pltpu.VMEM((count, model), jnp.float32)],
        compiler_params=params(),
        cost_estimate=cost(12 * count * model * model, 12 * model * model + 20 * count * model),
        name="input_back",
    )(*grads, *dx, normed_turned, tokens, weight, gain)


def head_body(
    tokens,
    cotangent,
    branch,
    ln1_gain,
    ln1_bias,
    qkv_weight,
    qv_bias,
    out_weight,
    out_bias,
    ln2_gain,
    ln2_bias,
    fc_weight,
    fc_bias,
    proj_weight,
    proj_bias,
):
    groups, span, model = tokens.shape
    rows = lax.axis_size("row")
    cols = lax.axis_size("col")
    dps = lax.axis_size("dp")
    members = rows * cols
    count = groups * span
    head_cols = qv_bias.shape[1]
    hidden_cols = fc_bias.shape[0]

    def spread(shard):
        whole = lax.all_gather(shard, MESH_AXES, axis=0, tiled=False)
        return whole.reshape((rows, cols) + shard.shape)

    def swap(blocks):
        return lax.all_to_all(blocks, MESH_AXES, 0, 0, tiled=True)

    def collect(partial):
        partial = partial.reshape((members,) + partial.shape[2:])
        partial = lax.psum_scatter(partial, MESH_AXES, scatter_dimension=0, tiled=True)
        partial = lax.psum_scatter(partial, "dp", scatter_dimension=1, tiled=True)
        return partial.reshape(partial.shape[2:]).astype(jnp.float32)

    w_qkv = spread(jnp.transpose(qkv_weight, (1, 0, 2)))
    biases = lax.all_gather(jnp.concatenate([qv_bias.reshape(-1), fc_bias]), "col", axis=0)
    w_out = spread(out_weight)
    w_fc = spread(fc_weight)
    w_proj = spread(proj_weight)
    qv_full = biases[:, : 2 * head_cols].reshape(cols, 2, 1, head_cols)
    fc_full = biases[:, 2 * head_cols :].reshape(cols, 1, hidden_cols)

    residual = tokens.astype(jnp.float32)
    normed = normalize(residual, ln1_gain, ln1_bias).astype(jnp.bfloat16).reshape(count, model)
    normed_turned = normed.T
    cot_flat = cotangent.reshape(count, model)
    cot_turned = cot_flat.T
    proj_bias_sum = jnp.sum(cot_flat.astype(jnp.float32), axis=0)

    blocks = project_qkv(normed, w_qkv, qv_full, groups)
    vectors = jnp.stack([out_bias, ln2_gain, ln2_bias] + [out_bias] * 5)
    gains = jnp.stack([ln2_gain] * 8)
    qkv, att, att_own, log_totals, middle, normed_two, turned_two = [], [], [], [], [], [], []
    for g in range(groups):
        received = swap(blocks[g].reshape(members, span, 3 * PAIR))
        qkv.append(received.reshape(members * span, 3 * PAIR))
    for g in range(groups):
        mixed, totals = attend(branch[g], qkv[g])
        att_own.append(mixed)
        log_totals.append(totals)
        att.append(swap(mixed.reshape(members, span, PAIR)).reshape(rows, cols, span, PAIR))
    for g in range(groups):
        mid, low, turned = project_out(tokens, att[g], w_out, vectors, g)
        middle.append(mid)
        normed_two.append(low)
        turned_two.append(turned)
    block_out, grad_two, grad_fc, grad_proj, fc_bias_sum = feed_forward(
        normed_two,
        turned_two,
        middle,
        cot_flat,
        cot_turned,
        w_fc,
        fc_full,
        w_proj,
        proj_bias[None],
        dps,
    )
    d_fc = collect(grad_fc)
    d_proj = collect(grad_proj).T
    dx, dx_turned, grad_att, sums_two = [], [], [], []
    for g in range(groups):
        total, turned, datt, sums = middle_back(
            grad_two, middle[g], cotangent, w_out, gains, g
        )
        dx.append(total)
        dx_turned.append(turned)
        sums_two.append(sums)
        grad_att.append(
            swap(datt.reshape(members, span, PAIR)).reshape(members * span, PAIR)
        )
    d_out = collect(out_grad(dx_turned, att, dps)).T
    grads = []
    for g in range(groups):
        grad = attend_back(branch[g], qkv[g], att_own[g], grad_att[g], log_totals[g])
        grads.append(
            swap(grad.reshape(members, span, 3 * PAIR)).reshape(rows, cols, span, 3 * PAIR)
        )
    input_grad, grad_qkv, qkv_bias_sum, sums_one = input_back(
        grads, dx, normed_turned, tokens, w_qkv, ln1_gain[None], dps
    )
    d_qkv = jnp.transpose(collect(grad_qkv), (1, 0, 2))
    sums_two = functools.reduce(jnp.add, sums_two)
    bias_rows = jnp.transpose(qkv_bias_sum[:, :, 0], (1, 0, 2)).reshape(3, cols * head_cols)
    small = (
        sums_one[0],
        sums_one[1],
        bias_rows[0],
        bias_rows[2],
        sums_two[2],
        sums_two[0],
        sums_two[1],
        fc_bias_sum.reshape(-1),
        proj_bias_sum,
    )
    ends = []
    for item in small:
        ends.append((ends[-1] if ends else 0) + item.shape[0])
    packed = lax.psum(jnp.concatenate(small), ("dp",) + MESH_AXES)
    (s_gain1, s_bias1, s_q, s_v, s_out, s_gain2, s_bias2, s_fc, s_proj) = jnp.split(
        packed, ends[:-1]
    )
    return (
        block_out,
        input_grad,
        s_gain1,
        s_bias1,
        d_qkv,
        jnp.stack([s_q, s_v]),
        d_out,
        s_out,
        s_gain2,
        s_bias2,
        d_fc,
        s_fc,
        d_proj,
        s_proj,
    )


def by_heads(mesh):
    rows, cols = mesh.shape["row"], mesh.shape["col"]

    def body(tokens, cotangent, branch, ln1_gain, ln1_bias, qkv_weight, *rest):
        width = qkv_weight.shape[2] * cols
        whole = tokens.shape[1] * rows * cols
        fits = width == rows * cols * PAIR and rows % 2 == 0
        fits = fits and whole == PLEN + CONTS * CLEN and tokens.shape[1] % BQ == 0
        chosen = head_body if fits else gathered_body
        return chosen(tokens, cotangent, branch, ln1_gain, ln1_bias, qkv_weight, *rest)

    return body


def solution(mesh):
    placed = (
        P("dp", ("row", "col"), None),
        P("dp", ("row", "col"), None),
        P("dp", None),
        P(),
        P(),
        P("row", None, "col"),
        P(None, "col"),
        P("col", "row"),
        P(),
        P(),
        P(),
        P("row", "col"),
        P("col"),
        P("col", "row"),
        P(),
    )
    return jax.shard_map(
        by_heads(mesh),
        mesh=mesh,
        in_specs=placed,
        out_specs=(
            P("dp", ("row", "col"), None),
            P("dp", ("row", "col"), None),
            P(),
            P(),
            P(("dp", "row"), None, "col"),
            P(),
            P("col", ("dp", "row")),
            P(),
            P(),
            P(),
            P(("dp", "row"), "col"),
            P(),
            P("col", ("dp", "row")),
            P(),
        ),
        check_vma=False,
    )
```

```python
import functools

import jax
import jax.numpy as jnp
from jax import lax
from jax.experimental import pallas as pl
from jax.experimental.pallas import tpu as pltpu
from jax.sharding import PartitionSpec as P

HEAD = 64
PLEN = 2048
CLEN = 256
CONTS = 8


EPSILON = 1e-05
MASKED_SCORE = -1e30
LOG2E = 1.4426950408889634
PAIR = 2 * HEAD
BQ = 256
BK = 512
BK_BACK = 512
HIDDEN_TILE = 512
NT = (((1,), (1,)), ((), ()))
TN = (((0,), (0,)), ((), ()))
MESH_AXES = ("row", "col")


def normalize(values, gain, shift):
    center = values - jnp.mean(values, axis=-1, keepdims=True)
    spread = jnp.mean(center * center, axis=-1, keepdims=True)
    return center * lax.rsqrt(spread + EPSILON) * gain + shift


def gelu_tanh(values):
    return jax.nn.gelu(values, approximate=True)


def allowed_keys(row_pos, col_pos, branch_cut):
    row_seg = jnp.where(row_pos >= PLEN, (row_pos - PLEN) // CLEN, -1)
    col_seg = jnp.where(col_pos >= PLEN, (col_pos - PLEN) // CLEN, -1)
    picked = (row_seg[:, None] == jnp.arange(CONTS, dtype=jnp.int32)[None, :]).astype(jnp.int32)
    row_cut = jnp.sum(picked * branch_cut[None, :], axis=1)
    causal = col_pos[None, :] <= row_pos[:, None]
    same_seq = col_seg[None, :] == row_seg[:, None]
    in_prefix = (
        (row_seg[:, None] >= 0) & (col_seg[None, :] < 0) & (col_pos[None, :] < row_cut[:, None])
    )
    return same_seq & causal | in_prefix


def add_trees(first, second):
    return jax.tree.map(lambda total, extra: total + extra, first, second)


def gathered_body(
    tokens,
    cotangent,
    branch,
    ln1_gain,
    ln1_bias,
    qkv_weight,
    qv_bias,
    out_weight,
    out_bias,
    ln2_gain,
    ln2_bias,
    fc_weight,
    fc_bias,
    proj_weight,
    proj_bias,
):
    scale = HEAD ** (-0.5)
    width = tokens.shape[2]
    local_rows = tokens.shape[1]
    head_cols = qv_bias.shape[1]
    head_count = head_cols // HEAD
    ff_local = fc_bias.shape[0]
    col_count = lax.axis_size("col")
    row_count = lax.axis_size("row")
    row_rows = local_rows * col_count
    group_rows = row_rows * row_count
    q_block = min(512, row_rows)
    block_count = row_rows // q_block
    row_base = lax.axis_index("row") * row_rows
    col_index = lax.axis_index("col")
    bias_three = jnp.stack([qv_bias[0], jnp.zeros_like(qv_bias[0]), qv_bias[1]])
    key_pos = jnp.arange(group_rows, dtype=jnp.int32)
    block_starts = jnp.arange(block_count, dtype=jnp.int32) * q_block

    def spread_rows(values):
        return lax.all_gather(values, "col", axis=0, tiled=True)

    def spread_grads(values):
        return lax.all_gather(values, "col", axis=0, tiled=True)

    def sum_branch(values):
        return lax.psum_scatter(values, "col", scatter_dimension=0, tiled=True)

    def sum_inputs(values):
        return lax.psum_scatter(values, "col", scatter_dimension=0, tiled=True)

    kept_weights = (
        lax.all_gather(qkv_weight, "row", axis=0, tiled=True),
        lax.all_gather(out_weight, "row", axis=1, tiled=True),
        lax.all_gather(fc_weight, "row", axis=0, tiled=True),
        lax.all_gather(proj_weight, "row", axis=1, tiled=True),
    )

    def block_scores(queries3, keys3, offset, branch_cut):
        q_part = lax.dynamic_slice_in_dim(queries3, offset, q_block, 0)
        row_pos = row_base + offset + jnp.arange(q_block, dtype=jnp.int32)
        allowed = allowed_keys(row_pos, key_pos, branch_cut)
        scores = (
            jnp.einsum("qhd,khd->hqk", q_part, keys3, preferred_element_type=jnp.float32) * scale
        )
        return (q_part, jnp.where(allowed[None], scores, MASKED_SCORE))

    def micro_step(carry, micro_item):
        grads_acc, small_acc = carry
        tok_rows, cot_rows, branch_cut = micro_item
        w_qkv, w_out, w_fc, w_proj = kept_weights
        residual = tok_rows.astype(jnp.float32)
        normed = normalize(residual, ln1_gain, ln1_bias).astype(jnp.bfloat16)
        normed_all = spread_rows(normed)
        projected = jnp.einsum("td,dsf->tsf", normed_all, w_qkv, preferred_element_type=jnp.float32)
        projected = (projected + bias_three[None]).astype(jnp.bfloat16)
        key_rows, value_rows = (
            lax.all_gather(projected[:, 1], "row", axis=0, tiled=True),
            lax.all_gather(projected[:, 2], "row", axis=0, tiled=True),
        )
        queries3 = projected[:, 0].reshape(row_rows, head_count, HEAD)
        keys3 = key_rows.reshape(group_rows, head_count, HEAD)
        values3 = value_rows.reshape(group_rows, head_count, HEAD)

        def attend(offset):
            q_part, scores = block_scores(queries3, keys3, offset, branch_cut)
            row_peak = jnp.max(scores, axis=-1, keepdims=True)
            exponent = jnp.exp(scores - row_peak)
            row_total = jnp.sum(exponent, axis=-1, keepdims=True)
            probs_low = (exponent / row_total).astype(jnp.bfloat16)
            mixed_rows = jnp.einsum(
                "hqk,khd->qhd", probs_low, values3, preferred_element_type=jnp.float32
            )
            return (mixed_rows, (row_peak + jnp.log(row_total))[..., 0])

        attended, log_totals = lax.map(attend, block_starts)
        attended = attended.reshape(row_rows, head_cols).astype(jnp.bfloat16)
        branch_part = jnp.dot(attended, w_out, preferred_element_type=jnp.float32)
        middle = residual + sum_branch(branch_part) + out_bias
        normed_two = normalize(middle, ln2_gain, ln2_bias).astype(jnp.bfloat16)
        normed_two_all = spread_rows(normed_two)
        hidden = jnp.dot(normed_two_all, w_fc, preferred_element_type=jnp.float32) + fc_bias
        active = gelu_tanh(hidden).astype(jnp.bfloat16)
        ffn_part = jnp.dot(active, w_proj, preferred_element_type=jnp.float32)
        output_rows = (middle + sum_branch(ffn_part) + proj_bias).astype(jnp.bfloat16)
        cot_all = spread_grads(cot_rows)
        grad_proj = jnp.einsum("tf,td->fd", active, cot_all, preferred_element_type=jnp.float32)
        grad_proj_bias = jnp.sum(cot_rows.astype(jnp.float32), axis=0)
        grad_active = jnp.einsum("td,fd->tf", cot_all, w_proj, preferred_element_type=jnp.float32)
        grad_hidden = jax.vjp(gelu_tanh, hidden)[1](grad_active)[0].astype(jnp.bfloat16)
        grad_fc = jnp.einsum(
            "td,tf->df", normed_two_all, grad_hidden, preferred_element_type=jnp.float32
        )
        grad_fc_bias = jnp.sum(grad_hidden.astype(jnp.float32), axis=0)
        grad_normed_two = sum_inputs(
            jnp.einsum("tf,df->td", grad_hidden, w_fc, preferred_element_type=jnp.float32)
        )
        back_middle, grad_gain_two, grad_bias_two = jax.vjp(normalize, middle, ln2_gain, ln2_bias)[
            1
        ](grad_normed_two)
        grad_middle = cot_rows.astype(jnp.float32) + back_middle
        grad_out_rows = grad_middle.astype(jnp.bfloat16)
        grad_out_all = spread_grads(grad_out_rows)
        grad_out = jnp.einsum(
            "tc,td->cd", attended, grad_out_all, preferred_element_type=jnp.float32
        )
        grad_out_bias = jnp.sum(grad_out_rows.astype(jnp.float32), axis=0)
        grad_att = jnp.einsum("td,cd->tc", grad_out_all, w_out, preferred_element_type=jnp.float32)
        grad_att = grad_att.astype(jnp.bfloat16).reshape(row_rows, head_count, HEAD)

        def attend_back(acc_pair, block_item):
            offset, log_total = block_item
            grad_keys_acc, grad_values_acc = acc_pair
            q_part, scores = block_scores(queries3, keys3, offset, branch_cut)
            probs = jnp.exp(scores - log_total[..., None])
            probs_low = probs.astype(jnp.bfloat16)
            grad_part = lax.dynamic_slice_in_dim(grad_att, offset, q_block, 0)
            grad_values_acc = grad_values_acc + jnp.einsum(
                "hqk,qhd->khd", probs_low, grad_part, preferred_element_type=jnp.float32
            )
            grad_probs = jnp.einsum(
                "qhd,khd->hqk", grad_part, values3, preferred_element_type=jnp.float32
            )
            center = jnp.sum(grad_probs * probs, axis=-1, keepdims=True)
            grad_scores = (probs * (grad_probs - center)).astype(jnp.bfloat16)
            grad_keys_acc = (
                grad_keys_acc
                + jnp.einsum(
                    "hqk,qhd->khd", grad_scores, q_part, preferred_element_type=jnp.float32
                )
                * scale
            )
            grad_query = (
                jnp.einsum("hqk,khd->qhd", grad_scores, keys3, preferred_element_type=jnp.float32)
                * scale
            )
            return ((grad_keys_acc, grad_values_acc), grad_query)

        empty_keys = jnp.zeros((group_rows, head_count, HEAD), jnp.float32)
        (grad_keys, grad_values), grad_queries = lax.scan(
            attend_back, (empty_keys, empty_keys), (block_starts, log_totals)
        )
        own_keys, own_values = (
            lax.psum_scatter(
                grad_keys.reshape(group_rows, head_cols).astype(jnp.bfloat16),
                "row",
                scatter_dimension=0,
                tiled=True,
            ).astype(jnp.float32),
            lax.psum_scatter(
                grad_values.reshape(group_rows, head_cols).astype(jnp.bfloat16),
                "row",
                scatter_dimension=0,
                tiled=True,
            ).astype(jnp.float32),
        )
        grad_projected = jnp.stack(
            [grad_queries.reshape(row_rows, head_cols), own_keys, own_values], axis=1
        ).astype(jnp.bfloat16)
        grad_qkv = jnp.einsum(
            "td,tsf->dsf", normed_all, grad_projected, preferred_element_type=jnp.float32
        )
        grad_qkv_bias = jnp.sum(grad_projected.astype(jnp.float32), axis=0)
        grad_normed = sum_inputs(
            jnp.einsum("tsf,dsf->td", grad_projected, w_qkv, preferred_element_type=jnp.float32)
        )
        back_input, grad_gain_one, grad_bias_one = jax.vjp(normalize, residual, ln1_gain, ln1_bias)[
            1
        ](grad_normed)
        input_rows = grad_middle + back_input
        weight_terms = (grad_qkv, grad_out, grad_fc, grad_proj)
        small_terms = (
            grad_gain_one,
            grad_bias_one,
            grad_qkv_bias,
            grad_out_bias,
            grad_gain_two,
            grad_bias_two,
            grad_fc_bias,
            grad_proj_bias,
        )
        return (
            (add_trees(grads_acc, weight_terms), add_trees(small_acc, small_terms)),
            (output_rows, input_rows),
        )

    grads_init = (
        jnp.zeros((width, 3, head_cols), jnp.float32),
        jnp.zeros((head_cols, width), jnp.float32),
        jnp.zeros((width, ff_local), jnp.float32),
        jnp.zeros((ff_local, width), jnp.float32),
    )
    vector_zero = jnp.zeros((width,), jnp.float32)
    small_init = (
        vector_zero,
        vector_zero,
        jnp.zeros((3, head_cols), jnp.float32),
        vector_zero,
        vector_zero,
        vector_zero,
        jnp.zeros((ff_local,), jnp.float32),
        vector_zero,
    )
    (grads_acc, small_acc), (block_out, input_grad) = lax.scan(
        micro_step, (grads_init, small_init), (tokens, cotangent, branch)
    )
    (
        gain_one,
        bias_one,
        qkv_bias_acc,
        out_bias_acc,
        gain_two,
        bias_two,
        fc_bias_acc,
        proj_bias_acc,
    ) = small_acc
    qv_full = lax.dynamic_update_slice(
        jnp.zeros((2, width), jnp.float32),
        jnp.stack([qkv_bias_acc[0], qkv_bias_acc[2]]),
        (jnp.int32(0), col_index * head_cols),
    )
    fc_full = lax.dynamic_update_slice(
        jnp.zeros((ff_local * col_count,), jnp.float32), fc_bias_acc, (col_index * ff_local,)
    )
    summed = lax.psum(
        (gain_one, bias_one, qv_full, out_bias_acc, gain_two, bias_two, fc_full, proj_bias_acc),
        ("dp", "row", "col"),
    )
    return (
        block_out,
        input_grad,
        summed[0],
        summed[1],
        lax.psum_scatter(
            grads_acc[0].astype(jnp.bfloat16), ("dp", "row"), scatter_dimension=0, tiled=True
        ).astype(jnp.float32),
        summed[2],
        lax.psum_scatter(
            grads_acc[1].astype(jnp.bfloat16), ("dp", "row"), scatter_dimension=1, tiled=True
        ).astype(jnp.float32),
        summed[3],
        summed[4],
        summed[5],
        lax.psum_scatter(
            grads_acc[2].astype(jnp.bfloat16), ("dp", "row"), scatter_dimension=0, tiled=True
        ).astype(jnp.float32),
        summed[6],
        lax.psum_scatter(
            grads_acc[3].astype(jnp.bfloat16), ("dp", "row"), scatter_dimension=1, tiled=True
        ).astype(jnp.float32),
        summed[7],
    )


def dot(left, right):
    return jnp.dot(left, right, preferred_element_type=jnp.float32)


def dot_nt(left, right):
    return lax.dot_general(left, right, NT, preferred_element_type=jnp.float32)


def cost(flops, moved, exps=0):
    return pl.CostEstimate(flops=int(flops), bytes_accessed=int(moved), transcendentals=int(exps))


def params(mebibytes):
    return pltpu.CompilerParams(vmem_limit_bytes=mebibytes * 2**20)


def fixed(shape):
    return pl.BlockSpec(shape, lambda *_: (0,) * len(shape), pipeline_mode=pl.Buffered(1))


def pair_rows(rows):
    low = lax.broadcasted_iota(jnp.int32, rows.shape, 1) < HEAD
    zero = jnp.zeros_like(rows)
    return jnp.concatenate([jnp.where(low, rows, zero), jnp.where(low, zero, rows)], axis=0)


def pick_lanes(stacked):
    half = stacked.shape[0] // 2
    low = lax.broadcasted_iota(jnp.int32, (half, stacked.shape[1]), 1) < HEAD
    return jnp.where(low, stacked[:half], stacked[half:])


def qkv_kernel(rows, groups, x_ref, w_ref, bias_ref, *out_refs):
    depth = w_ref.shape[3]
    for part in range(3):
        weight = w_ref[:, 0, part].reshape(rows * depth, 2 * PAIR)
        values = dot(x_ref[...], weight)
        if part != 1:
            values = values + bias_ref[0, 0 if part == 0 else 1]
        if part == 0:
            values = values * HEAD**-0.5
        values = values.astype(jnp.bfloat16)
        span = values.shape[0] // groups
        for g in range(groups):
            for half in range(2):
                out_refs[g][half, 0, :, part * PAIR : (part + 1) * PAIR] = values[
                    g * span : (g + 1) * span, half * PAIR : (half + 1) * PAIR
                ]


def project_qkv(normed, weight, bias, groups):
    rows, cols, _, depth, width = weight.shape
    tokens, model = normed.shape
    span = tokens // groups
    return pl.pallas_call(
        functools.partial(qkv_kernel, rows, groups),
        grid=(rows // 2, cols),
        in_specs=[
            fixed((tokens, model)),
            pl.BlockSpec((rows, 1, 3, depth, 2 * PAIR), lambda i, c: (0, c, 0, 0, i)),
            pl.BlockSpec((1, 2, 1, 2 * PAIR), lambda i, c: (c, 0, 0, i)),
        ],
        out_specs=[pl.BlockSpec((2, 1, span, 3 * PAIR), lambda i, c: (i, c, 0, 0))] * groups,
        out_shape=[jax.ShapeDtypeStruct((rows, cols, span, 3 * PAIR), jnp.bfloat16)] * groups,
        compiler_params=params(24),
        cost_estimate=cost(6 * tokens * model * model, 8 * tokens * model + 6 * model * model),
        name="qkv",
    )(normed, weight, bias)


def attend_kernel(
    bk, cut_ref, qkv_ref, o_ref, lse_ref, s_ref, own_ref, value_ref, peak_ref, acc_ref
):
    i = pl.program_id(0)
    prompt_blocks = PLEN // BQ

    @pl.when(i == 0)
    def _():
        value_ref[:, :PAIR] = qkv_ref[:, 2 * PAIR : 3 * PAIR]
        value_ref[:, PAIR:] = jnp.ones((value_ref.shape[0], PAIR), value_ref.dtype)

    start = pl.multiple_of(i * BQ, BQ)
    queries = pair_rows(qkv_ref[pl.ds(start, BQ), 0:PAIR])
    limit = jnp.where(i < prompt_blocks, start, cut_ref[jnp.maximum(i - prompt_blocks, 0)])
    full = limit // bk
    rest = limit - full * bk

    def scores(first, count):
        keys = qkv_ref[pl.ds(pl.multiple_of(first, BQ), count), PAIR : 2 * PAIR]
        return dot_nt(queries, keys) * LOG2E

    def lane_peak(values):
        return functools.reduce(
            jnp.maximum, [values[:, at : at + 128] for at in range(0, values.shape[1], 128)]
        )

    own = scores(start, BQ)
    row = lax.broadcasted_iota(jnp.int32, own.shape, 0) & (BQ - 1)
    own = jnp.where(lax.broadcasted_iota(jnp.int32, own.shape, 1) <= row, own, MASKED_SCORE)
    own_ref[...] = own
    peak_ref[...] = lane_peak(own)

    def score_step(j, none):
        values = scores(j * bk, bk)
        s_ref[j] = values
        peak_ref[...] = jnp.maximum(peak_ref[...], lane_peak(values))
        return none

    lax.fori_loop(0, full, score_step, 0)

    @pl.when(rest > 0)
    def _():
        values = scores(full * bk, bk)
        seen = lax.broadcasted_iota(jnp.int32, values.shape, 1) < rest
        values = jnp.where(seen, values, MASKED_SCORE)
        s_ref[full] = values
        peak_ref[...] = jnp.maximum(peak_ref[...], lane_peak(values))

    peak = jnp.max(peak_ref[...], axis=1, keepdims=True)
    probs = jnp.exp2(own_ref[...] - peak).astype(jnp.bfloat16)
    acc_ref[...] = dot(probs, value_ref[pl.ds(start, BQ), :])

    def value_step(j, none):
        probs = jnp.exp2(s_ref[j] - peak).astype(jnp.bfloat16)
        acc_ref[...] += dot(probs, value_ref[pl.ds(pl.multiple_of(j * bk, bk), bk), :])
        return none

    lax.fori_loop(0, full + jnp.where(rest > 0, 1, 0), value_step, 0)
    total = acc_ref[:, PAIR:]
    o_ref[...] = pick_lanes(acc_ref[:, :PAIR] / total).astype(o_ref.dtype)
    lse_ref[0] = jnp.transpose(peak + jnp.log2(total))[:8]


def attend(cut, qkv):
    tokens = qkv.shape[0]
    blocks = tokens // BQ
    pairs = 2 * tokens * tokens // 4
    return pl.pallas_call(
        functools.partial(attend_kernel, BK),
        grid=(blocks,),
        in_specs=[pl.BlockSpec(memory_space=pltpu.SMEM), fixed((tokens, 3 * PAIR))],
        out_specs=[
            pl.BlockSpec((BQ, PAIR), lambda i: (i, 0)),
            pl.BlockSpec((1, 8, 2 * BQ), lambda i: (i, 0, 0)),
        ],
        out_shape=[
            jax.ShapeDtypeStruct((tokens, PAIR), jnp.bfloat16),
            jax.ShapeDtypeStruct((blocks, 8, 2 * BQ), jnp.float32),
        ],
        scratch_shapes=[
            pltpu.VMEM((PLEN // BK, 2 * BQ, BK), jnp.float32),
            pltpu.VMEM((2 * BQ, BQ), jnp.float32),
            pltpu.VMEM((tokens, 2 * PAIR), jnp.bfloat16),
            pltpu.VMEM((2 * BQ, PAIR), jnp.float32),
            pltpu.VMEM((2 * BQ, 2 * PAIR), jnp.float32),
        ],
        compiler_params=params(24),
        cost_estimate=cost(8 * 2 * pairs * 256, 2 * tokens * 4 * PAIR, pairs),
        name="attend",
    )(cut, qkv)


def attend_back_kernel(
    bk, cut_ref, qkv_ref, o_ref, do_ref, lse_ref, out_ref, dk_ref, dv_ref, dq_ref
):
    i = pl.program_id(0)
    prompt_blocks = PLEN // BQ

    @pl.when(i == 0)
    def _():
        dk_ref[...] = jnp.zeros_like(dk_ref)
        dv_ref[...] = jnp.zeros_like(dv_ref)

    start = pl.multiple_of(i * BQ, BQ)
    queries = pair_rows(qkv_ref[pl.ds(start, BQ), 0:PAIR])
    grad = do_ref[pl.ds(start, BQ), :]
    grads = pair_rows(grad)
    mixed = jnp.transpose(
        grad.astype(jnp.float32) * o_ref[pl.ds(start, BQ), :].astype(jnp.float32)
    )
    center = jnp.concatenate(
        [
            jnp.sum(mixed[:HEAD], axis=0, keepdims=True),
            jnp.sum(mixed[HEAD:], axis=0, keepdims=True),
        ],
        axis=1,
    )
    log_total = lse_ref[0, 0:1, :]
    limit = jnp.where(i < prompt_blocks, start, cut_ref[jnp.maximum(i - prompt_blocks, 0)])
    full = limit // bk
    rest = limit - full * bk

    def block(first, count, keep, begin):
        at = pl.ds(pl.multiple_of(first, BQ), count)
        keys = qkv_ref[at, PAIR : 2 * PAIR]
        values = qkv_ref[at, 2 * PAIR : 3 * PAIR]
        probs = jnp.exp2(dot_nt(keys, queries) * LOG2E - log_total)
        if keep is not None:
            probs = jnp.where(keep(probs.shape), probs, 0.0)
        dv_ref[at, :] += dot(probs.astype(jnp.bfloat16), grads)
        grad_probs = dot_nt(values, grads)
        grad_scores = (probs * (grad_probs - center)).astype(jnp.bfloat16)
        dk_ref[at, :] += dot(grad_scores, queries)
        part = lax.dot_general(keys, grad_scores, TN, preferred_element_type=jnp.float32)
        dq_ref[...] = part if begin else dq_ref[...] + part

    def causal(shape):
        key = lax.broadcasted_iota(jnp.int32, shape, 0)
        query = lax.broadcasted_iota(jnp.int32, shape, 1) & (BQ - 1)
        return key <= query

    block(start, BQ, causal, True)

    def step(j, none):
        block(j * bk, bk, None, False)
        return none

    lax.fori_loop(0, full, step, 0)

    @pl.when(rest > 0)
    def _():
        block(full * bk, bk, lambda s: lax.broadcasted_iota(jnp.int32, s, 0) < rest, False)

    grad_query = pick_lanes(jnp.transpose(dq_ref[...])) * HEAD**-0.5
    out_ref[pl.ds(start, BQ), 0:PAIR] = grad_query.astype(out_ref.dtype)

    @pl.when(i == pl.num_programs(0) - 1)
    def _():
        out_ref[:, PAIR : 2 * PAIR] = dk_ref[...].astype(out_ref.dtype)
        out_ref[:, 2 * PAIR : 3 * PAIR] = dv_ref[...].astype(out_ref.dtype)


def attend_back(cut, qkv, att, grad_att, log_totals):
    tokens = qkv.shape[0]
    pairs = 2 * tokens * tokens // 4
    return pl.pallas_call(
        functools.partial(attend_back_kernel, BK_BACK),
        grid=(tokens // BQ,),
        in_specs=[
            pl.BlockSpec(memory_space=pltpu.SMEM),
            fixed((tokens, 3 * PAIR)),
            fixed((tokens, PAIR)),
            fixed((tokens, PAIR)),
            pl.BlockSpec((1, 8, 2 * BQ), lambda i: (i, 0, 0)),
        ],
        out_specs=fixed((tokens, 3 * PAIR)),
        out_shape=jax.ShapeDtypeStruct((tokens, 3 * PAIR), jnp.bfloat16),
        scratch_shapes=[
            pltpu.VMEM((tokens, PAIR), jnp.float32),
            pltpu.VMEM((tokens, PAIR), jnp.float32),
            pltpu.VMEM((PAIR, 2 * BQ), jnp.float32),
        ],
        compiler_params=params(32),
        cost_estimate=cost(10 * 2 * pairs * 256, 2 * tokens * 8 * PAIR, pairs),
        name="attend_back",
    )(cut, qkv, att, grad_att, log_totals)


def centered(values):
    center = values - jnp.mean(values, axis=-1, keepdims=True)
    spread = jnp.mean(center * center, axis=-1, keepdims=True)
    inverse = lax.rsqrt(spread + EPSILON)
    return center * inverse, inverse


def norm_back(grad, gain, unit, inverse):
    scaled = grad * gain
    mean_one = jnp.mean(scaled, axis=-1, keepdims=True)
    mean_two = jnp.mean(scaled * unit, axis=-1, keepdims=True)
    return (scaled - mean_one - unit * mean_two) * inverse


def middle_kernel(
    rows, cols, tok_ref, att_ref, w_ref, vec_ref, middle_ref, normed_ref, turned_ref
):
    parts = []
    for c in range(cols):
        parts.append(jnp.concatenate([att_ref[r, c] for r in range(rows)], axis=1))
    pieces = []
    for r in range(rows):
        total = dot(parts[0], w_ref[r, 0])
        for c in range(1, cols):
            total = total + dot(parts[c], w_ref[r, c])
        pieces.append(total)
    middle = tok_ref[0].astype(jnp.float32) + jnp.concatenate(pieces, axis=1) + vec_ref[0:1]
    middle_ref[...] = middle
    normed = (centered(middle)[0] * vec_ref[1:2] + vec_ref[2:3]).astype(jnp.bfloat16)
    normed_ref[...] = normed
    turned_ref[...] = jnp.transpose(normed)


def project_out(tokens, att, weight, vectors, g):
    rows, cols, span, _ = att.shape
    model = tokens.shape[2]
    tile = min(256, span)
    return pl.pallas_call(
        functools.partial(middle_kernel, rows, cols),
        grid=(span // tile,),
        in_specs=[
            pl.BlockSpec((1, tile, model), lambda i: (g, i, 0)),
            pl.BlockSpec((rows, cols, tile, PAIR), lambda i: (0, 0, i, 0)),
            fixed(weight.shape),
            fixed(vectors.shape),
        ],
        out_specs=[
            pl.BlockSpec((tile, model), lambda i: (i, 0)),
            pl.BlockSpec((tile, model), lambda i: (i, 0)),
            pl.BlockSpec((model, tile), lambda i: (0, i)),
        ],
        out_shape=[
            jax.ShapeDtypeStruct((span, model), jnp.float32),
            jax.ShapeDtypeStruct((span, model), jnp.bfloat16),
            jax.ShapeDtypeStruct((model, span), jnp.bfloat16),
        ],
        compiler_params=params(24),
        cost_estimate=cost(2 * span * model * model, 2 * model * model + 12 * span * model),
        name="out_norm",
    )(tokens, att, weight, vectors)


def hidden_kernel(rows, dps, groups, first, *refs):
    normed_refs = refs[:groups]
    turned_refs = refs[groups : 2 * groups]
    cot_ref, cot_turned_ref, w_ref, fc_bias_ref = refs[2 * groups : 2 * groups + 4]
    if first:
        middle_refs = refs[2 * groups + 4 : 3 * groups + 4]
        out_acc, back_acc, grad_ref, bias_ref, sems = refs[3 * groups + 4 :]
    else:
        (prev_out_ref, prev_back_ref, proj_bias_ref) = refs[2 * groups + 4 : 2 * groups + 7]
        out_ref, back_acc, grad_ref, bias_ref, out_acc, sems = refs[2 * groups + 7 :]
    step = pl.program_id(0) * pl.num_programs(1) + pl.program_id(1)
    last = pl.num_programs(0) * pl.num_programs(1) - 1
    span, model = normed_refs[0].shape
    tile = w_ref.shape[4]
    if first:
        copies = [
            pltpu.make_async_copy(
                middle_refs[g], out_acc.at[pl.ds(g * span, span)], sems.at[g]
            )
            for g in range(groups)
        ]
    else:
        copies = [
            pltpu.make_async_copy(prev_out_ref, out_acc, sems.at[0]),
            pltpu.make_async_copy(prev_back_ref, back_acc, sems.at[1]),
        ]

    @pl.when(step == 0)
    def _():
        for copy in copies:
            copy.start()
        if first:
            back_acc[...] = jnp.zeros_like(back_acc)

    fc_weight = w_ref[:, 0, 0].reshape(model, tile)
    proj_turned = w_ref[:, 0, 1].reshape(model, tile)
    root = 0.7978845608028654
    actives, lows = [], []
    for g in range(groups):
        hidden = dot(normed_refs[g][...], fc_weight) + fc_bias_ref[0]
        square = hidden * hidden
        inner = jnp.tanh(hidden * (root + (root * 0.044715) * square))
        plus = 0.5 + 0.5 * inner
        actives.append((hidden * plus).astype(jnp.bfloat16))
        bend = 0.5 - 0.5 * inner * inner
        slope = plus + hidden * bend * (root + (3 * root * 0.044715) * square)
        grad_active = dot(cot_ref[g * span : (g + 1) * span], proj_turned)
        lows.append((grad_active * slope).astype(jnp.bfloat16))
    bias_ref[0] = functools.reduce(
        jnp.add, [jnp.sum(low.astype(jnp.float32), axis=0, keepdims=True) for low in lows]
    )
    low_all = jnp.concatenate(lows, axis=0)
    active_all = jnp.concatenate(actives, axis=0)
    turned_all = jnp.concatenate([ref[...] for ref in turned_refs], axis=1)
    cut = model // (rows * dps)
    for which, weight_grad in enumerate(
        (dot(turned_all, low_all), dot(cot_turned_ref[...], active_all))
    ):
        weight_grad = weight_grad.astype(jnp.bfloat16)
        for r in range(rows):
            for d in range(dps):
                at = (d * rows + r) * cut
                grad_ref[r, 0, d, which] = weight_grad[at : at + cut]

    @pl.when(step == 0)
    def _():
        for copy in copies:
            copy.wait()

    out_acc[...] += dot_nt(active_all, proj_turned)
    back_acc[...] += dot_nt(low_all, fc_weight)
    if not first:

        @pl.when(step == last)
        def _():
            for g in range(groups):
                at = slice(g * span, (g + 1) * span)
                out_ref[g] = (out_acc[at] + proj_bias_ref[...]).astype(out_ref.dtype)


def feed_forward(first, normed, turned, cot, cot_turned, weight, fc_bias, rest, dps):
    groups = len(normed)
    span, model = normed[0].shape
    tokens = groups * span
    rows, cols, _, depth, local = weight.shape
    tile = min(HIDDEN_TILE, local)
    cut = model // (rows * dps)
    acc_shape = jax.ShapeDtypeStruct((tokens, model), jnp.float32)
    anywhere = pl.BlockSpec(memory_space=pl.ANY)
    if first:
        rest_specs = [anywhere] * groups
        out_spec, out_shape = fixed((tokens, model)), acc_shape
        scratch = [pltpu.SemaphoreType.DMA((groups,))]
    else:
        rest_specs = [anywhere, anywhere, fixed((1, model))]
        out_spec = fixed((groups, span, model))
        out_shape = jax.ShapeDtypeStruct((groups, span, model), jnp.bfloat16)
        scratch = [pltpu.VMEM((tokens, model), jnp.float32), pltpu.SemaphoreType.DMA((2,))]
    return pl.pallas_call(
        functools.partial(hidden_kernel, rows, dps, groups, first),
        grid=(cols, local // tile),
        in_specs=[fixed((span, model))] * groups
        + [fixed((model, span))] * groups
        + [
            fixed((tokens, model)),
            fixed((model, tokens)),
            pl.BlockSpec((rows, 1, 2, depth, tile), lambda c, i: (0, c, 0, 0, i)),
            pl.BlockSpec((1, 1, tile), lambda c, i: (c, 0, i)),
        ]
        + rest_specs,
        out_specs=[
            out_spec,
            fixed((tokens, model)),
            pl.BlockSpec((rows, 1, dps, 2, cut, tile), lambda c, i: (0, c, 0, 0, 0, i)),
            pl.BlockSpec((1, 1, tile), lambda c, i: (c, 0, i)),
        ],
        out_shape=[
            out_shape,
            acc_shape,
            jax.ShapeDtypeStruct((rows, cols, dps, 2, cut, local), jnp.bfloat16),
            jax.ShapeDtypeStruct((cols, 1, local), jnp.float32),
        ],
        scratch_shapes=scratch,
        compiler_params=params(60),
        cost_estimate=cost(
            12 * tokens * model * cols * local, 8 * model * cols * local, tokens * cols * local
        ),
        name="feed_forward_first" if first else "feed_forward_second",
    )(*normed, *turned, cot, cot_turned, weight, fc_bias, *rest)


def middle_back_kernel(
    rows, cols, grad_ref, middle_ref, cot_ref, w_ref, vec_ref, dx_ref, turned_ref, datt_ref, sum_ref
):
    grad = grad_ref[0]
    unit, inverse = centered(middle_ref[...])
    total = cot_ref[0].astype(jnp.float32) + norm_back(grad, vec_ref[1:2], unit, inverse)
    dx_ref[...] = total
    low = total.astype(jnp.bfloat16)
    turned_ref[...] = jnp.transpose(low)
    depth = w_ref.shape[3]
    for c in range(cols):
        part = dot_nt(low[:, :depth], w_ref[0, c])
        for r in range(1, rows):
            part = part + dot_nt(low[:, r * depth : (r + 1) * depth], w_ref[r, c])
        part = part.astype(jnp.bfloat16)
        for r in range(rows):
            datt_ref[r, c] = part[:, r * PAIR : (r + 1) * PAIR]

    @pl.when(pl.program_id(0) == 0)
    def _():
        sum_ref[...] = jnp.zeros_like(sum_ref)

    sum_ref[0:1] += jnp.sum(grad * unit, axis=0, keepdims=True)
    sum_ref[1:2] += jnp.sum(grad, axis=0, keepdims=True)
    sum_ref[2:3] += jnp.sum(low.astype(jnp.float32), axis=0, keepdims=True)


def middle_back(grad, middle, cot, weight, vectors, g):
    span, model = middle.shape
    rows, cols = weight.shape[:2]
    tile = min(256, span)
    return pl.pallas_call(
        functools.partial(middle_back_kernel, rows, cols),
        grid=(span // tile,),
        in_specs=[
            pl.BlockSpec((1, tile, model), lambda i: (g, i, 0)),
            pl.BlockSpec((tile, model), lambda i: (i, 0)),
            pl.BlockSpec((1, tile, model), lambda i: (g, i, 0)),
            fixed(weight.shape),
            fixed(vectors.shape),
        ],
        out_specs=[
            pl.BlockSpec((tile, model), lambda i: (i, 0)),
            pl.BlockSpec((model, tile), lambda i: (0, i)),
            pl.BlockSpec((rows, cols, tile, PAIR), lambda i: (0, 0, i, 0)),
            pl.BlockSpec((8, model), lambda i: (0, 0)),
        ],
        out_shape=[
            jax.ShapeDtypeStruct((span, model), jnp.float32),
            jax.ShapeDtypeStruct((model, span), jnp.bfloat16),
            jax.ShapeDtypeStruct((rows, cols, span, PAIR), jnp.bfloat16),
            jax.ShapeDtypeStruct((8, model), jnp.float32),
        ],
        compiler_params=params(24),
        cost_estimate=cost(2 * span * model * model, 2 * model * model + 18 * span * model),
        name="out_norm_back",
    )(grad, middle, cot, weight, vectors)


def out_grad_kernel(rows, dps, groups, *refs):
    out_ref = refs[2 * groups]
    total = None
    for g in range(groups):
        att = jnp.concatenate([refs[groups + g][r, 0] for r in range(rows)], axis=1)
        part = dot(refs[g][...], att)
        total = part if total is None else total + part
    total = total.astype(jnp.bfloat16)
    cut = out_ref.shape[3]
    for r in range(rows):
        for d in range(dps):
            at = (d * rows + r) * cut
            out_ref[r, 0, d] = total[at : at + cut]


def out_grad(turned, att, dps):
    groups = len(turned)
    model, span = turned[0].shape
    rows, cols = att[0].shape[:2]
    cut = model // (rows * dps)
    return pl.pallas_call(
        functools.partial(out_grad_kernel, rows, dps, groups),
        grid=(cols,),
        in_specs=[fixed((model, span))] * groups
        + [pl.BlockSpec((rows, 1, span, PAIR), lambda c: (0, c, 0, 0))] * groups,
        out_specs=pl.BlockSpec((rows, 1, dps, cut, rows * PAIR), lambda c: (0, c, 0, 0, 0)),
        out_shape=jax.ShapeDtypeStruct((rows, cols, dps, cut, rows * PAIR), jnp.bfloat16),
        compiler_params=params(24),
        cost_estimate=cost(2 * groups * span * model * model, 2 * model * model),
        name="out_grad",
    )(*turned, *att)


def qkv_grad_kernel(rows, dps, turned_ref, dqkv_ref, *refs):
    grad_ref, bias_ref = refs[-2:]
    cut = grad_ref.shape[4]
    for part in range(3):
        lanes = slice(part * PAIR, (part + 1) * PAIR)
        grads = jnp.concatenate([dqkv_ref[half, 0, :, lanes] for half in range(2)], axis=1)
        weight_grad = dot(turned_ref[...], grads)
        for r in range(rows):
            for d in range(dps):
                at = (d * rows + r) * cut
                piece = weight_grad[at : at + cut]
                if len(refs) == 3:
                    piece = piece + refs[0][r, 0, d, part]
                grad_ref[r, 0, d, part] = piece.astype(grad_ref.dtype)
        bias_ref[0, part] = jnp.sum(grads.astype(jnp.float32), axis=0, keepdims=True)


def qkv_grad(dqkv, normed_turned, before, g, final, dps):
    rows, cols, span, _ = dqkv.shape
    model = normed_turned.shape[0]
    width = rows * PAIR
    cut = model // (rows * dps)
    grad_spec = pl.BlockSpec((rows, 1, dps, 3, cut, 2 * PAIR), lambda i, c: (0, c, 0, 0, 0, i))
    grad_type = jnp.bfloat16 if final else jnp.float32
    return pl.pallas_call(
        functools.partial(qkv_grad_kernel, rows, dps),
        grid=(rows // 2, cols),
        in_specs=[
            pl.BlockSpec((model, span), lambda i, c: (0, g), pipeline_mode=pl.Buffered(1)),
            pl.BlockSpec((2, 1, span, 3 * PAIR), lambda i, c: (i, c, 0, 0)),
        ]
        + [grad_spec] * len(before),
        out_specs=[grad_spec, pl.BlockSpec((1, 3, 1, 2 * PAIR), lambda i, c: (c, 0, 0, i))],
        out_shape=[
            jax.ShapeDtypeStruct((rows, cols, dps, 3, cut, width), grad_type),
            jax.ShapeDtypeStruct((cols, 3, 1, width), jnp.float32),
        ],
        compiler_params=params(40),
        cost_estimate=cost(6 * span * model * model, 24 * model * model),
        name="qkv_grad",
    )(normed_turned, dqkv, *before)


def input_kernel(rows, dqkv_ref, w_ref, dx_ref, tok_ref, gain_ref, *refs):
    out_ref, sum_ref, acc = refs[-3:]
    step = pl.program_id(0) * pl.num_programs(1) + pl.program_id(1)
    model = acc.shape[1]
    grads, weights = [], []
    for part in range(3):
        lanes = slice(part * PAIR, (part + 1) * PAIR)
        grads += [dqkv_ref[half, 0, :, lanes] for half in range(2)]
        weights.append(w_ref[:, 0, part].reshape(model, 2 * PAIR))
    piece = dot_nt(jnp.concatenate(grads, axis=1), jnp.concatenate(weights, axis=1))

    @pl.when(step == 0)
    def _():
        acc[...] = piece

    @pl.when(step > 0)
    def _():
        acc[...] += piece

    @pl.when(step == pl.num_programs(0) * pl.num_programs(1) - 1)
    def _():
        grad = acc[...]
        unit, inverse = centered(tok_ref[0].astype(jnp.float32))
        out_ref[0] = dx_ref[...] + norm_back(grad, gain_ref[...], unit, inverse)
        sum_ref[0:1] = jnp.sum(grad * unit, axis=0, keepdims=True)
        sum_ref[1:2] = jnp.sum(grad, axis=0, keepdims=True)


def input_back(dqkv, dx, tokens, weight, gain, before, g):
    rows, cols, _, depth, width = weight.shape
    span, model = dx.shape
    return pl.pallas_call(
        functools.partial(input_kernel, rows),
        grid=(rows // 2, cols),
        in_specs=[
            pl.BlockSpec((2, 1, span, 3 * PAIR), lambda i, c: (i, c, 0, 0)),
            pl.BlockSpec((rows, 1, 3, depth, 2 * PAIR), lambda i, c: (0, c, 0, 0, i)),
            fixed((span, model)),
            pl.BlockSpec((1, span, model), lambda i, c: (g, 0, 0), pipeline_mode=pl.Buffered(1)),
            fixed((1, model)),
        ]
        + [pl.BlockSpec(memory_space=pl.ANY)] * len(before),
        out_specs=[
            pl.BlockSpec((1, span, model), lambda i, c: (g, 0, 0), pipeline_mode=pl.Buffered(1)),
            fixed((8, model)),
        ],
        out_shape=[
            jax.ShapeDtypeStruct(tokens.shape, jnp.float32),
            jax.ShapeDtypeStruct((8, model), jnp.float32),
        ],
        scratch_shapes=[pltpu.VMEM((span, model), jnp.float32)],
        compiler_params=params(32),
        cost_estimate=cost(6 * span * model * model, 6 * model * model + 12 * span * model),
        input_output_aliases={5: 0} if before else {},
        name="input_back",
    )(dqkv, weight, dx, tokens, gain, *before)


def head_body(
    tokens,
    cotangent,
    branch,
    ln1_gain,
    ln1_bias,
    qkv_weight,
    qv_bias,
    out_weight,
    out_bias,
    ln2_gain,
    ln2_bias,
    fc_weight,
    fc_bias,
    proj_weight,
    proj_bias,
):
    groups, span, model = tokens.shape
    rows = lax.axis_size("row")
    cols = lax.axis_size("col")
    dps = lax.axis_size("dp")
    members = rows * cols
    count = groups * span
    head_cols = qv_bias.shape[1]
    hidden_cols = fc_bias.shape[0]

    def spread(shard):
        whole = lax.all_gather(shard, MESH_AXES, axis=0, tiled=False)
        return whole.reshape((rows, cols) + shard.shape)

    def swap(blocks):
        return lax.all_to_all(blocks, MESH_AXES, 0, 0, tiled=True)

    def collect_plane(partial):
        partial = partial.reshape((members,) + partial.shape[2:])
        partial = lax.psum_scatter(partial, MESH_AXES, scatter_dimension=0, tiled=True)
        return partial.reshape(partial.shape[1:])

    def collect_dp(partial):
        pieces = lax.all_to_all(partial, "dp", 0, 0, tiled=True)
        return jnp.sum(pieces.astype(jnp.float32), axis=0)

    def total(values):
        for axis in ("row", "col", "dp"):
            size = lax.axis_size(axis)
            step = 1
            while step < size:
                pairs = [(i, i ^ step) for i in range(size)]
                values = values + lax.ppermute(values, axis, pairs)
                step *= 2
        return values

    half = hidden_cols // 2
    proj_turned = proj_weight.T
    shards = [
        jnp.stack([fc_weight[:, at : at + half], proj_turned[:, at : at + half]])
        for at in (0, half)
    ]
    w_qkv = spread(jnp.transpose(qkv_weight, (1, 0, 2)))
    biases = lax.all_gather(jnp.concatenate([qv_bias.reshape(-1), fc_bias]), "col", axis=0)
    qv_full = biases[:, : 2 * head_cols].reshape(cols, 2, 1, head_cols)
    fc_full = biases[:, 2 * head_cols :].reshape(cols, 1, hidden_cols)

    residual = tokens.astype(jnp.float32)
    normed = normalize(residual, ln1_gain, ln1_bias).astype(jnp.bfloat16).reshape(count, model)
    normed_turned = normed.T
    cot_flat = cotangent.reshape(count, model)
    cot_turned = cot_flat.T
    proj_bias_sum = jnp.sum(cot_flat.astype(jnp.float32), axis=0)

    blocks = project_qkv(normed, w_qkv, qv_full, groups)
    vectors = jnp.stack([out_bias, ln2_gain, ln2_bias] + [out_bias] * 5)
    gains = jnp.stack([ln2_gain] * 8)
    qkv, att, att_own, log_totals, middle, normed_two, turned_two = [], [], [], [], [], [], []
    for g in range(groups):
        received = swap(blocks[g].reshape(members, span, 3 * PAIR))
        qkv.append(received.reshape(members * span, 3 * PAIR))
    qkv[-1], out_weight, shards[0], shards[1] = lax.optimization_barrier(
        (qkv[-1], out_weight, shards[0], shards[1])
    )
    w_out = spread(out_weight)
    w_first = spread(shards[0])
    w_second = spread(shards[1])
    for g in range(groups):
        mixed, totals = attend(branch[g], qkv[g])
        att_own.append(mixed)
        log_totals.append(totals)
        att.append(swap(mixed.reshape(members, span, PAIR)).reshape(rows, cols, span, PAIR))
    for g in range(groups):
        mid, low, turned = project_out(tokens, att[g], w_out, vectors, g)
        middle.append(mid)
        normed_two.append(low)
        turned_two.append(turned)
    shared = (normed_two, turned_two, cot_flat, cot_turned)
    out_part, back_part, grad_first, fc_sum_first = feed_forward(
        True, *shared, w_first, fc_full[:, :, :half], middle, dps
    )
    plane_first = collect_plane(grad_first)
    block_out, grad_two, grad_second, fc_sum_second = feed_forward(
        False,
        *shared,
        w_second,
        fc_full[:, :, half:],
        (out_part, back_part, proj_bias[None]),
        dps,
    )
    plane_second = collect_plane(grad_second)
    grad_two = grad_two.reshape(groups, span, model)
    dx, dx_turned, grad_att, sums_two = [], [], [], []
    for g in range(groups):
        rows_grad, turned, datt, sums = middle_back(
            grad_two, middle[g], cotangent, w_out, gains, g
        )
        dx.append(rows_grad)
        dx_turned.append(turned)
        sums_two.append(sums)
        grad_att.append(
            swap(datt.reshape(members, span, PAIR)).reshape(members * span, PAIR)
        )
    plane_out = collect_plane(out_grad(dx_turned, att, dps))
    grad_att[-1], plane_first = lax.optimization_barrier((grad_att[-1], plane_first))
    grads = []
    for g in range(groups):
        grad = attend_back(branch[g], qkv[g], att_own[g], grad_att[g], log_totals[g])
        grads.append(
            swap(grad.reshape(members, span, 3 * PAIR)).reshape(rows, cols, span, 3 * PAIR)
        )
    sums_two = functools.reduce(jnp.add, sums_two)
    fc_sum = jnp.concatenate([fc_sum_first, fc_sum_second], axis=2).reshape(-1)
    early = (sums_two[2], sums_two[0], sums_two[1], fc_sum, proj_bias_sum)
    grads[0], plane_second, early = lax.optimization_barrier((grads[0], plane_second, early))
    early = total(jnp.concatenate(early))
    input_grads, sums_one, bias_sums, before = [], [], [], []
    for g in range(groups):
        grad_qkv, bias_sum = qkv_grad(
            grads[g], normed_turned, before, g, g == groups - 1, dps
        )
        before = [grad_qkv]
        bias_sums.append(bias_sum)
        rows_grad, sums = input_back(
            grads[g], dx[g], tokens, w_qkv, ln1_gain[None], input_grads, g
        )
        input_grads = [rows_grad]
        sums_one.append(sums)
        if g < groups - 1:
            grads[g + 1], input_grads, early = lax.optimization_barrier(
                (grads[g + 1], input_grads, early)
            )
    d_qkv = jnp.transpose(collect_dp(collect_plane(grad_qkv)), (1, 0, 2))
    d_out = collect_dp(plane_out).T
    d_hidden = jnp.concatenate([collect_dp(plane_first), collect_dp(plane_second)], axis=2)
    sums_one = functools.reduce(jnp.add, sums_one)
    bias_sum = functools.reduce(jnp.add, bias_sums)
    bias_rows = jnp.transpose(bias_sum[:, :, 0], (1, 0, 2)).reshape(3, model)
    late = total(jnp.stack([sums_one[0], sums_one[1], bias_rows[0], bias_rows[2]]))
    s_out, s_gain_two, s_bias_two = (early[i * model : (i + 1) * model] for i in range(3))
    s_fc = early[3 * model : 3 * model + hidden_cols * cols]
    s_proj = early[3 * model + hidden_cols * cols :]
    return (
        block_out,
        input_grads[0],
        late[0],
        late[1],
        d_qkv,
        late[2:],
        d_out,
        s_out,
        s_gain_two,
        s_bias_two,
        d_hidden[0],
        s_fc,
        d_hidden[1].T,
        s_proj,
    )


def by_heads(mesh):
    rows, cols = mesh.shape["row"], mesh.shape["col"]

    def body(tokens, cotangent, branch, ln1_gain, ln1_bias, qkv_weight, *rest):
        width = qkv_weight.shape[2] * cols
        whole = tokens.shape[1] * rows * cols
        fits = width == rows * cols * PAIR and rows % 2 == 0
        fits = fits and all(size & (size - 1) == 0 for size in mesh.shape.values())
        fits = fits and whole == PLEN + CONTS * CLEN and tokens.shape[1] % BQ == 0
        chosen = head_body if fits else gathered_body
        return chosen(tokens, cotangent, branch, ln1_gain, ln1_bias, qkv_weight, *rest)

    return body


def solution(mesh):
    placed = (
        P("dp", ("row", "col"), None),
        P("dp", ("row", "col"), None),
        P("dp", None),
        P(),
        P(),
        P("row", None, "col"),
        P(None, "col"),
        P("col", "row"),
        P(),
        P(),
        P(),
        P("row", "col"),
        P("col"),
        P("col", "row"),
        P(),
    )
    return jax.shard_map(
        by_heads(mesh),
        mesh=mesh,
        in_specs=placed,
        out_specs=(
            P("dp", ("row", "col"), None),
            P("dp", ("row", "col"), None),
            P(),
            P(),
            P(("dp", "row"), None, "col"),
            P(),
            P("col", ("dp", "row")),
            P(),
            P(),
            P(),
            P(("dp", "row"), "col"),
            P(),
            P("col", ("dp", "row")),
            P(),
        ),
        check_vma=False,
    )
```

```python
import functools

import jax
import jax.numpy as jnp
from jax import lax
from jax.experimental import pallas as pl
from jax.experimental.pallas import tpu as pltpu
from jax.sharding import PartitionSpec as P

HEAD = 64
PLEN = 2048
CLEN = 256
CONTS = 8


EPSILON = 1e-05
MASKED_SCORE = -1e30
LOG2E = 1.4426950408889634
PAIR = 2 * HEAD
BQ = 256
BK = 512
BK_BACK = 512
HIDDEN_TILE = 512
NT = (((1,), (1,)), ((), ()))
TN = (((0,), (0,)), ((), ()))
MESH_AXES = ("row", "col")


def normalize(values, gain, shift):
    center = values - jnp.mean(values, axis=-1, keepdims=True)
    spread = jnp.mean(center * center, axis=-1, keepdims=True)
    return center * lax.rsqrt(spread + EPSILON) * gain + shift


def gelu_tanh(values):
    return jax.nn.gelu(values, approximate=True)


def allowed_keys(row_pos, col_pos, branch_cut):
    row_seg = jnp.where(row_pos >= PLEN, (row_pos - PLEN) // CLEN, -1)
    col_seg = jnp.where(col_pos >= PLEN, (col_pos - PLEN) // CLEN, -1)
    picked = (row_seg[:, None] == jnp.arange(CONTS, dtype=jnp.int32)[None, :]).astype(jnp.int32)
    row_cut = jnp.sum(picked * branch_cut[None, :], axis=1)
    causal = col_pos[None, :] <= row_pos[:, None]
    same_seq = col_seg[None, :] == row_seg[:, None]
    in_prefix = (
        (row_seg[:, None] >= 0) & (col_seg[None, :] < 0) & (col_pos[None, :] < row_cut[:, None])
    )
    return same_seq & causal | in_prefix


def add_trees(first, second):
    return jax.tree.map(lambda total, extra: total + extra, first, second)


def gathered_body(
    tokens,
    cotangent,
    branch,
    ln1_gain,
    ln1_bias,
    qkv_weight,
    qv_bias,
    out_weight,
    out_bias,
    ln2_gain,
    ln2_bias,
    fc_weight,
    fc_bias,
    proj_weight,
    proj_bias,
):
    scale = HEAD ** (-0.5)
    width = tokens.shape[2]
    local_rows = tokens.shape[1]
    head_cols = qv_bias.shape[1]
    head_count = head_cols // HEAD
    ff_local = fc_bias.shape[0]
    col_count = lax.axis_size("col")
    row_count = lax.axis_size("row")
    row_rows = local_rows * col_count
    group_rows = row_rows * row_count
    q_block = min(512, row_rows)
    block_count = row_rows // q_block
    row_base = lax.axis_index("row") * row_rows
    col_index = lax.axis_index("col")
    bias_three = jnp.stack([qv_bias[0], jnp.zeros_like(qv_bias[0]), qv_bias[1]])
    key_pos = jnp.arange(group_rows, dtype=jnp.int32)
    block_starts = jnp.arange(block_count, dtype=jnp.int32) * q_block

    def spread_rows(values):
        return lax.all_gather(values, "col", axis=0, tiled=True)

    def spread_grads(values):
        return lax.all_gather(values, "col", axis=0, tiled=True)

    def sum_branch(values):
        return lax.psum_scatter(values, "col", scatter_dimension=0, tiled=True)

    def sum_inputs(values):
        return lax.psum_scatter(values, "col", scatter_dimension=0, tiled=True)

    kept_weights = (
        lax.all_gather(qkv_weight, "row", axis=0, tiled=True),
        lax.all_gather(out_weight, "row", axis=1, tiled=True),
        lax.all_gather(fc_weight, "row", axis=0, tiled=True),
        lax.all_gather(proj_weight, "row", axis=1, tiled=True),
    )

    def block_scores(queries3, keys3, offset, branch_cut):
        q_part = lax.dynamic_slice_in_dim(queries3, offset, q_block, 0)
        row_pos = row_base + offset + jnp.arange(q_block, dtype=jnp.int32)
        allowed = allowed_keys(row_pos, key_pos, branch_cut)
        scores = (
            jnp.einsum("qhd,khd->hqk", q_part, keys3, preferred_element_type=jnp.float32) * scale
        )
        return (q_part, jnp.where(allowed[None], scores, MASKED_SCORE))

    def micro_step(carry, micro_item):
        grads_acc, small_acc = carry
        tok_rows, cot_rows, branch_cut = micro_item
        w_qkv, w_out, w_fc, w_proj = kept_weights
        residual = tok_rows.astype(jnp.float32)
        normed = normalize(residual, ln1_gain, ln1_bias).astype(jnp.bfloat16)
        normed_all = spread_rows(normed)
        projected = jnp.einsum("td,dsf->tsf", normed_all, w_qkv, preferred_element_type=jnp.float32)
        projected = (projected + bias_three[None]).astype(jnp.bfloat16)
        key_rows, value_rows = (
            lax.all_gather(projected[:, 1], "row", axis=0, tiled=True),
            lax.all_gather(projected[:, 2], "row", axis=0, tiled=True),
        )
        queries3 = projected[:, 0].reshape(row_rows, head_count, HEAD)
        keys3 = key_rows.reshape(group_rows, head_count, HEAD)
        values3 = value_rows.reshape(group_rows, head_count, HEAD)

        def attend(offset):
            q_part, scores = block_scores(queries3, keys3, offset, branch_cut)
            row_peak = jnp.max(scores, axis=-1, keepdims=True)
            exponent = jnp.exp(scores - row_peak)
            row_total = jnp.sum(exponent, axis=-1, keepdims=True)
            probs_low = (exponent / row_total).astype(jnp.bfloat16)
            mixed_rows = jnp.einsum(
                "hqk,khd->qhd", probs_low, values3, preferred_element_type=jnp.float32
            )
            return (mixed_rows, (row_peak + jnp.log(row_total))[..., 0])

        attended, log_totals = lax.map(attend, block_starts)
        attended = attended.reshape(row_rows, head_cols).astype(jnp.bfloat16)
        branch_part = jnp.dot(attended, w_out, preferred_element_type=jnp.float32)
        middle = residual + sum_branch(branch_part) + out_bias
        normed_two = normalize(middle, ln2_gain, ln2_bias).astype(jnp.bfloat16)
        normed_two_all = spread_rows(normed_two)
        hidden = jnp.dot(normed_two_all, w_fc, preferred_element_type=jnp.float32) + fc_bias
        active = gelu_tanh(hidden).astype(jnp.bfloat16)
        ffn_part = jnp.dot(active, w_proj, preferred_element_type=jnp.float32)
        output_rows = (middle + sum_branch(ffn_part) + proj_bias).astype(jnp.bfloat16)
        cot_all = spread_grads(cot_rows)
        grad_proj = jnp.einsum("tf,td->fd", active, cot_all, preferred_element_type=jnp.float32)
        grad_proj_bias = jnp.sum(cot_rows.astype(jnp.float32), axis=0)
        grad_active = jnp.einsum("td,fd->tf", cot_all, w_proj, preferred_element_type=jnp.float32)
        grad_hidden = jax.vjp(gelu_tanh, hidden)[1](grad_active)[0].astype(jnp.bfloat16)
        grad_fc = jnp.einsum(
            "td,tf->df", normed_two_all, grad_hidden, preferred_element_type=jnp.float32
        )
        grad_fc_bias = jnp.sum(grad_hidden.astype(jnp.float32), axis=0)
        grad_normed_two = sum_inputs(
            jnp.einsum("tf,df->td", grad_hidden, w_fc, preferred_element_type=jnp.float32)
        )
        back_middle, grad_gain_two, grad_bias_two = jax.vjp(normalize, middle, ln2_gain, ln2_bias)[
            1
        ](grad_normed_two)
        grad_middle = cot_rows.astype(jnp.float32) + back_middle
        grad_out_rows = grad_middle.astype(jnp.bfloat16)
        grad_out_all = spread_grads(grad_out_rows)
        grad_out = jnp.einsum(
            "tc,td->cd", attended, grad_out_all, preferred_element_type=jnp.float32
        )
        grad_out_bias = jnp.sum(grad_out_rows.astype(jnp.float32), axis=0)
        grad_att = jnp.einsum("td,cd->tc", grad_out_all, w_out, preferred_element_type=jnp.float32)
        grad_att = grad_att.astype(jnp.bfloat16).reshape(row_rows, head_count, HEAD)

        def attend_back(acc_pair, block_item):
            offset, log_total = block_item
            grad_keys_acc, grad_values_acc = acc_pair
            q_part, scores = block_scores(queries3, keys3, offset, branch_cut)
            probs = jnp.exp(scores - log_total[..., None])
            probs_low = probs.astype(jnp.bfloat16)
            grad_part = lax.dynamic_slice_in_dim(grad_att, offset, q_block, 0)
            grad_values_acc = grad_values_acc + jnp.einsum(
                "hqk,qhd->khd", probs_low, grad_part, preferred_element_type=jnp.float32
            )
            grad_probs = jnp.einsum(
                "qhd,khd->hqk", grad_part, values3, preferred_element_type=jnp.float32
            )
            center = jnp.sum(grad_probs * probs, axis=-1, keepdims=True)
            grad_scores = (probs * (grad_probs - center)).astype(jnp.bfloat16)
            grad_keys_acc = (
                grad_keys_acc
                + jnp.einsum(
                    "hqk,qhd->khd", grad_scores, q_part, preferred_element_type=jnp.float32
                )
                * scale
            )
            grad_query = (
                jnp.einsum("hqk,khd->qhd", grad_scores, keys3, preferred_element_type=jnp.float32)
                * scale
            )
            return ((grad_keys_acc, grad_values_acc), grad_query)

        empty_keys = jnp.zeros((group_rows, head_count, HEAD), jnp.float32)
        (grad_keys, grad_values), grad_queries = lax.scan(
            attend_back, (empty_keys, empty_keys), (block_starts, log_totals)
        )
        own_keys, own_values = (
            lax.psum_scatter(
                grad_keys.reshape(group_rows, head_cols).astype(jnp.bfloat16),
                "row",
                scatter_dimension=0,
                tiled=True,
            ).astype(jnp.float32),
            lax.psum_scatter(
                grad_values.reshape(group_rows, head_cols).astype(jnp.bfloat16),
                "row",
                scatter_dimension=0,
                tiled=True,
            ).astype(jnp.float32),
        )
        grad_projected = jnp.stack(
            [grad_queries.reshape(row_rows, head_cols), own_keys, own_values], axis=1
        ).astype(jnp.bfloat16)
        grad_qkv = jnp.einsum(
            "td,tsf->dsf", normed_all, grad_projected, preferred_element_type=jnp.float32
        )
        grad_qkv_bias = jnp.sum(grad_projected.astype(jnp.float32), axis=0)
        grad_normed = sum_inputs(
            jnp.einsum("tsf,dsf->td", grad_projected, w_qkv, preferred_element_type=jnp.float32)
        )
        back_input, grad_gain_one, grad_bias_one = jax.vjp(normalize, residual, ln1_gain, ln1_bias)[
            1
        ](grad_normed)
        input_rows = grad_middle + back_input
        weight_terms = (grad_qkv, grad_out, grad_fc, grad_proj)
        small_terms = (
            grad_gain_one,
            grad_bias_one,
            grad_qkv_bias,
            grad_out_bias,
            grad_gain_two,
            grad_bias_two,
            grad_fc_bias,
            grad_proj_bias,
        )
        return (
            (add_trees(grads_acc, weight_terms), add_trees(small_acc, small_terms)),
            (output_rows, input_rows),
        )

    grads_init = (
        jnp.zeros((width, 3, head_cols), jnp.float32),
        jnp.zeros((head_cols, width), jnp.float32),
        jnp.zeros((width, ff_local), jnp.float32),
        jnp.zeros((ff_local, width), jnp.float32),
    )
    vector_zero = jnp.zeros((width,), jnp.float32)
    small_init = (
        vector_zero,
        vector_zero,
        jnp.zeros((3, head_cols), jnp.float32),
        vector_zero,
        vector_zero,
        vector_zero,
        jnp.zeros((ff_local,), jnp.float32),
        vector_zero,
    )
    (grads_acc, small_acc), (block_out, input_grad) = lax.scan(
        micro_step, (grads_init, small_init), (tokens, cotangent, branch)
    )
    (
        gain_one,
        bias_one,
        qkv_bias_acc,
        out_bias_acc,
        gain_two,
        bias_two,
        fc_bias_acc,
        proj_bias_acc,
    ) = small_acc
    qv_full = lax.dynamic_update_slice(
        jnp.zeros((2, width), jnp.float32),
        jnp.stack([qkv_bias_acc[0], qkv_bias_acc[2]]),
        (jnp.int32(0), col_index * head_cols),
    )
    fc_full = lax.dynamic_update_slice(
        jnp.zeros((ff_local * col_count,), jnp.float32), fc_bias_acc, (col_index * ff_local,)
    )
    summed = lax.psum(
        (gain_one, bias_one, qv_full, out_bias_acc, gain_two, bias_two, fc_full, proj_bias_acc),
        ("dp", "row", "col"),
    )
    return (
        block_out,
        input_grad,
        summed[0],
        summed[1],
        lax.psum_scatter(
            grads_acc[0].astype(jnp.bfloat16), ("dp", "row"), scatter_dimension=0, tiled=True
        ).astype(jnp.float32),
        summed[2],
        lax.psum_scatter(
            grads_acc[1].astype(jnp.bfloat16), ("dp", "row"), scatter_dimension=1, tiled=True
        ).astype(jnp.float32),
        summed[3],
        summed[4],
        summed[5],
        lax.psum_scatter(
            grads_acc[2].astype(jnp.bfloat16), ("dp", "row"), scatter_dimension=0, tiled=True
        ).astype(jnp.float32),
        summed[6],
        lax.psum_scatter(
            grads_acc[3].astype(jnp.bfloat16), ("dp", "row"), scatter_dimension=1, tiled=True
        ).astype(jnp.float32),
        summed[7],
    )


def dot(left, right):
    return jnp.dot(left, right, preferred_element_type=jnp.float32)


def dot_nt(left, right):
    return lax.dot_general(left, right, NT, preferred_element_type=jnp.float32)


def cost(flops, moved, exps=0):
    return pl.CostEstimate(flops=int(flops), bytes_accessed=int(moved), transcendentals=int(exps))


def params(mebibytes):
    return pltpu.CompilerParams(vmem_limit_bytes=mebibytes * 2**20)


def fixed(shape):
    return pl.BlockSpec(shape, lambda *_: (0,) * len(shape), pipeline_mode=pl.Buffered(1))


def pair_rows(rows):
    low = lax.broadcasted_iota(jnp.int32, rows.shape, 1) < HEAD
    zero = jnp.zeros_like(rows)
    return jnp.concatenate([jnp.where(low, rows, zero), jnp.where(low, zero, rows)], axis=0)


def pick_lanes(stacked):
    half = stacked.shape[0] // 2
    low = lax.broadcasted_iota(jnp.int32, (half, stacked.shape[1]), 1) < HEAD
    return jnp.where(low, stacked[:half], stacked[half:])


def pack_kernel(fc_ref, proj_ref, out_ref, first_ref, second_ref):
    depth, hidden = fc_ref.shape
    half = hidden // 2
    turned = jnp.transpose(proj_ref[...])
    for at, ref in ((0, first_ref), (half, second_ref)):
        ref[:depth] = fc_ref[:, at : at + half]
        ref[depth : 2 * depth] = turned[:, at : at + half]
    for h in range(out_ref.shape[0] // PAIR):
        first_ref[2 * depth :, h * depth : (h + 1) * depth] = out_ref[h * PAIR : (h + 1) * PAIR]


def pack_weights(fc_weight, proj_weight, out_weight):
    depth, hidden = fc_weight.shape
    shapes = [(2 * depth + PAIR, hidden // 2), (2 * depth, hidden // 2)]
    return pl.pallas_call(
        pack_kernel,
        in_specs=[pl.BlockSpec(memory_space=pltpu.VMEM)] * 3,
        out_specs=[pl.BlockSpec(memory_space=pltpu.VMEM)] * 2,
        out_shape=[jax.ShapeDtypeStruct(shape, jnp.bfloat16) for shape in shapes],
        compiler_params=params(60),
        cost_estimate=cost(1, 8 * depth * hidden),
        name="pack_weights",
    )(fc_weight, proj_weight, out_weight)


def qkv_kernel(x_ref, w_ref, vec_ref, out_ref):
    rows = x_ref[...].reshape(out_ref.shape[0], x_ref.shape[2])
    values = (dot(rows, w_ref[...]) + vec_ref[0:1]) * vec_ref[1:2]
    out_ref[...] = values.astype(out_ref.dtype)


def project_qkv(normed, weight, bias, span):
    members, _, model = normed.shape
    width = weight.shape[1]
    tokens = members * span
    vectors = jnp.stack([bias, jnp.where(jnp.arange(width) < PAIR, HEAD**-0.5, 1.0)])
    return pl.pallas_call(
        qkv_kernel,
        grid=(members // 2,),
        in_specs=[
            pl.BlockSpec((2, span, model), lambda i: (i, 0, 0)),
            fixed((model, width)),
            fixed((2, width)),
        ],
        out_specs=pl.BlockSpec((2 * span, width), lambda i: (i, 0)),
        out_shape=jax.ShapeDtypeStruct((tokens, width), jnp.bfloat16),
        compiler_params=params(60),
        cost_estimate=cost(2 * tokens * model * width, 2 * tokens * (model + width)),
        name="qkv",
    )(normed, weight, vectors)


def attend_kernel(
    bk, cut_ref, qkv_ref, o_ref, lse_ref, s_ref, own_ref, value_ref, peak_ref, acc_ref
):
    i = pl.program_id(0)
    prompt_blocks = PLEN // BQ

    @pl.when(i == 0)
    def _():
        value_ref[:, :PAIR] = qkv_ref[:, 2 * PAIR : 3 * PAIR]
        value_ref[:, PAIR:] = jnp.ones((value_ref.shape[0], PAIR), value_ref.dtype)

    start = pl.multiple_of(i * BQ, BQ)
    queries = pair_rows(qkv_ref[pl.ds(start, BQ), 0:PAIR])
    limit = jnp.where(i < prompt_blocks, start, cut_ref[jnp.maximum(i - prompt_blocks, 0)])
    full = limit // bk
    rest = limit - full * bk

    def scores(first, count):
        keys = qkv_ref[pl.ds(pl.multiple_of(first, BQ), count), PAIR : 2 * PAIR]
        return dot_nt(queries, keys) * LOG2E

    def lane_peak(values):
        return functools.reduce(
            jnp.maximum, [values[:, at : at + 128] for at in range(0, values.shape[1], 128)]
        )

    own = scores(start, BQ)
    row = lax.broadcasted_iota(jnp.int32, own.shape, 0) & (BQ - 1)
    own = jnp.where(lax.broadcasted_iota(jnp.int32, own.shape, 1) <= row, own, MASKED_SCORE)
    own_ref[...] = own
    peak_ref[...] = lane_peak(own)

    def score_step(j, none):
        values = scores(j * bk, bk)
        s_ref[j] = values
        peak_ref[...] = jnp.maximum(peak_ref[...], lane_peak(values))
        return none

    lax.fori_loop(0, full, score_step, 0)

    @pl.when(rest > 0)
    def _():
        values = scores(full * bk, bk)
        seen = lax.broadcasted_iota(jnp.int32, values.shape, 1) < rest
        values = jnp.where(seen, values, MASKED_SCORE)
        s_ref[full] = values
        peak_ref[...] = jnp.maximum(peak_ref[...], lane_peak(values))

    peak = jnp.max(peak_ref[...], axis=1, keepdims=True)
    probs = jnp.exp2(own_ref[...] - peak).astype(jnp.bfloat16)
    acc_ref[...] = dot(probs, value_ref[pl.ds(start, BQ), :])

    def value_step(j, none):
        probs = jnp.exp2(s_ref[j] - peak).astype(jnp.bfloat16)
        acc_ref[...] += dot(probs, value_ref[pl.ds(pl.multiple_of(j * bk, bk), bk), :])
        return none

    lax.fori_loop(0, full + jnp.where(rest > 0, 1, 0), value_step, 0)
    total = acc_ref[:, PAIR:]
    o_ref[...] = pick_lanes(acc_ref[:, :PAIR] / total).astype(o_ref.dtype)
    lse_ref[0] = jnp.transpose(peak + jnp.log2(total))[:8]


def attend(cut, qkv):
    tokens = qkv.shape[0]
    blocks = tokens // BQ
    pairs = 2 * tokens * tokens // 4
    return pl.pallas_call(
        functools.partial(attend_kernel, BK),
        grid=(blocks,),
        in_specs=[pl.BlockSpec(memory_space=pltpu.SMEM), fixed((tokens, 3 * PAIR))],
        out_specs=[
            pl.BlockSpec((BQ, PAIR), lambda i: (i, 0)),
            pl.BlockSpec((1, 8, 2 * BQ), lambda i: (i, 0, 0)),
        ],
        out_shape=[
            jax.ShapeDtypeStruct((tokens, PAIR), jnp.bfloat16),
            jax.ShapeDtypeStruct((blocks, 8, 2 * BQ), jnp.float32),
        ],
        scratch_shapes=[
            pltpu.VMEM((PLEN // BK, 2 * BQ, BK), jnp.float32),
            pltpu.VMEM((2 * BQ, BQ), jnp.float32),
            pltpu.VMEM((tokens, 2 * PAIR), jnp.bfloat16),
            pltpu.VMEM((2 * BQ, PAIR), jnp.float32),
            pltpu.VMEM((2 * BQ, 2 * PAIR), jnp.float32),
        ],
        compiler_params=params(60),
        cost_estimate=cost(8 * 2 * pairs * 256, 2 * tokens * 4 * PAIR, pairs),
        name="attend",
    )(cut, qkv)


def attend_back_kernel(
    bk, cut_ref, qkv_ref, o_ref, do_ref, lse_ref, out_ref, dk_ref, dv_ref, dq_ref
):
    i = pl.program_id(0)
    prompt_blocks = PLEN // BQ

    @pl.when(i == 0)
    def _():
        dk_ref[...] = jnp.zeros_like(dk_ref)
        dv_ref[...] = jnp.zeros_like(dv_ref)

    start = pl.multiple_of(i * BQ, BQ)
    queries = pair_rows(qkv_ref[pl.ds(start, BQ), 0:PAIR])
    grad = do_ref[pl.ds(start, BQ), :]
    grads = pair_rows(grad)
    mixed = jnp.transpose(
        grad.astype(jnp.float32) * o_ref[pl.ds(start, BQ), :].astype(jnp.float32)
    )
    center = jnp.concatenate(
        [
            jnp.sum(mixed[:HEAD], axis=0, keepdims=True),
            jnp.sum(mixed[HEAD:], axis=0, keepdims=True),
        ],
        axis=1,
    )
    log_total = lse_ref[0, 0:1, :]
    limit = jnp.where(i < prompt_blocks, start, cut_ref[jnp.maximum(i - prompt_blocks, 0)])
    full = limit // bk
    rest = limit - full * bk

    def block(first, count, keep, begin):
        at = pl.ds(pl.multiple_of(first, BQ), count)
        keys = qkv_ref[at, PAIR : 2 * PAIR]
        values = qkv_ref[at, 2 * PAIR : 3 * PAIR]
        probs = jnp.exp2(dot_nt(keys, queries) * LOG2E - log_total)
        if keep is not None:
            probs = jnp.where(keep(probs.shape), probs, 0.0)
        dv_ref[at, :] += dot(probs.astype(jnp.bfloat16), grads)
        grad_probs = dot_nt(values, grads)
        grad_scores = (probs * (grad_probs - center)).astype(jnp.bfloat16)
        dk_ref[at, :] += dot(grad_scores, queries)
        part = lax.dot_general(keys, grad_scores, TN, preferred_element_type=jnp.float32)
        dq_ref[...] = part if begin else dq_ref[...] + part

    def causal(shape):
        key = lax.broadcasted_iota(jnp.int32, shape, 0)
        query = lax.broadcasted_iota(jnp.int32, shape, 1) & (BQ - 1)
        return key <= query

    block(start, BQ, causal, True)

    def step(j, none):
        block(j * bk, bk, None, False)
        return none

    lax.fori_loop(0, full, step, 0)

    @pl.when(rest > 0)
    def _():
        block(full * bk, bk, lambda s: lax.broadcasted_iota(jnp.int32, s, 0) < rest, False)

    grad_query = pick_lanes(jnp.transpose(dq_ref[...])) * HEAD**-0.5
    out_ref[pl.ds(start, BQ), 0:PAIR] = grad_query.astype(out_ref.dtype)

    @pl.when(i == pl.num_programs(0) - 1)
    def _():
        out_ref[:, PAIR : 2 * PAIR] = dk_ref[...].astype(out_ref.dtype)
        out_ref[:, 2 * PAIR : 3 * PAIR] = dv_ref[...].astype(out_ref.dtype)


def attend_back(cut, qkv, att, grad_att, log_totals):
    tokens = qkv.shape[0]
    pairs = 2 * tokens * tokens // 4
    return pl.pallas_call(
        functools.partial(attend_back_kernel, BK_BACK),
        grid=(tokens // BQ,),
        in_specs=[
            pl.BlockSpec(memory_space=pltpu.SMEM),
            fixed((tokens, 3 * PAIR)),
            fixed((tokens, PAIR)),
            fixed((tokens, PAIR)),
            pl.BlockSpec((1, 8, 2 * BQ), lambda i: (i, 0, 0)),
        ],
        out_specs=fixed((tokens, 3 * PAIR)),
        out_shape=jax.ShapeDtypeStruct((tokens, 3 * PAIR), jnp.bfloat16),
        scratch_shapes=[
            pltpu.VMEM((tokens, PAIR), jnp.float32),
            pltpu.VMEM((tokens, PAIR), jnp.float32),
            pltpu.VMEM((PAIR, 2 * BQ), jnp.float32),
        ],
        compiler_params=params(60),
        cost_estimate=cost(10 * 2 * pairs * 256, 2 * tokens * 8 * PAIR, pairs),
        name="attend_back",
    )(cut, qkv, att, grad_att, log_totals)


def centered(values):
    center = values - jnp.mean(values, axis=-1, keepdims=True)
    spread = jnp.mean(center * center, axis=-1, keepdims=True)
    inverse = lax.rsqrt(spread + EPSILON)
    return center * inverse, inverse


def norm_back(grad, gain, unit, inverse):
    scaled = grad * gain
    mean_one = jnp.mean(scaled, axis=-1, keepdims=True)
    mean_two = jnp.mean(scaled * unit, axis=-1, keepdims=True)
    return (scaled - mean_one - unit * mean_two) * inverse


def out_block(w_ref, r, c, rows):
    width = w_ref.shape[3] // rows
    return jnp.concatenate(
        [w_ref[r, c, :, h * width : (h + 1) * width] for h in range(rows)], axis=0
    )


def out_weight_spec(weight):
    rows, cols, depth, width = weight.shape
    at = 4
    return pl.BlockSpec(
        (rows, cols, PAIR, width), lambda *_: (0, 0, at, 0), pipeline_mode=pl.Buffered(1)
    )


def middle_kernel(
    rows, cols, tok_ref, att_ref, w_ref, vec_ref, middle_ref, normed_ref, turned_ref
):
    parts = []
    for c in range(cols):
        parts.append(jnp.concatenate([att_ref[r, c] for r in range(rows)], axis=1))
    pieces = []
    for r in range(rows):
        total = dot(parts[0], out_block(w_ref, r, 0, rows))
        for c in range(1, cols):
            total = total + dot(parts[c], out_block(w_ref, r, c, rows))
        pieces.append(total)
    middle = tok_ref[0].astype(jnp.float32) + jnp.concatenate(pieces, axis=1) + vec_ref[0:1]
    middle_ref[...] = middle
    normed = (centered(middle)[0] * vec_ref[1:2] + vec_ref[2:3]).astype(jnp.bfloat16)
    normed_ref[...] = normed
    turned_ref[...] = jnp.transpose(normed)


def project_out(tokens, att, weight, vectors, g):
    rows, cols, span, _ = att.shape
    model = tokens.shape[2]
    tile = min(256, span)
    return pl.pallas_call(
        functools.partial(middle_kernel, rows, cols),
        grid=(span // tile,),
        in_specs=[
            pl.BlockSpec((1, tile, model), lambda i: (g, i, 0)),
            pl.BlockSpec((rows, cols, tile, PAIR), lambda i: (0, 0, i, 0)),
            out_weight_spec(weight),
            fixed(vectors.shape),
        ],
        out_specs=[
            pl.BlockSpec((tile, model), lambda i: (i, 0)),
            pl.BlockSpec((tile, model), lambda i: (i, 0)),
            pl.BlockSpec((model, tile), lambda i: (0, i)),
        ],
        out_shape=[
            jax.ShapeDtypeStruct((span, model), jnp.float32),
            jax.ShapeDtypeStruct((span, model), jnp.bfloat16),
            jax.ShapeDtypeStruct((model, span), jnp.bfloat16),
        ],
        compiler_params=params(60),
        cost_estimate=cost(2 * span * model * model, 2 * model * model + 12 * span * model),
        name="out_norm",
    )(tokens, att, weight, vectors)


def store_grads(rows, dps, turned_refs, cot_turned_ref, low_all, active_all, grad_ref):
    turned_all = jnp.concatenate([ref[...] for ref in turned_refs], axis=1)
    cut = turned_all.shape[0] // (rows * dps)
    for which, weight_grad in enumerate(
        (dot(turned_all, low_all), dot(cot_turned_ref[...], active_all))
    ):
        weight_grad = weight_grad.astype(jnp.bfloat16)
        for r in range(rows):
            for d in range(dps):
                at = (d * rows + r) * cut
                grad_ref[r, 0, d, which * cut : (which + 1) * cut] = weight_grad[at : at + cut]


def hidden_grad_kernel(rows, dps, *refs):
    low_ref, active_ref, grad_ref = refs[-3:]
    store_grads(rows, dps, refs[:-4], refs[-4], low_ref[0], active_ref[0], grad_ref)


def hidden_grad(turned, cot_turned, low, active, dps, rows):
    cols, tokens, local = low.shape
    model = cot_turned.shape[0]
    tile = min(HIDDEN_TILE, local)
    cut = model // (rows * dps)
    piece = pl.BlockSpec((1, tokens, tile), lambda c, i: (c, 0, i))
    return pl.pallas_call(
        functools.partial(hidden_grad_kernel, rows, dps),
        grid=(cols, local // tile),
        in_specs=[fixed(part.shape) for part in turned]
        + [fixed(cot_turned.shape), piece, piece],
        out_specs=pl.BlockSpec((rows, 1, dps, 2 * cut, tile), lambda c, i: (0, c, 0, 0, i)),
        out_shape=jax.ShapeDtypeStruct(
            (rows, cols, dps, 2 * cut + cut // 2, local), jnp.bfloat16
        ),
        compiler_params=params(60),
        cost_estimate=cost(4 * tokens * model * cols * local, 8 * model * cols * local),
        name="hidden_grad",
    )(*turned, cot_turned, low, active)


def hidden_kernel(rows, dps, groups, first, *refs):
    normed_refs, refs = refs[:groups], refs[groups:]
    if first:
        turned_refs, cot_turned_ref, refs = refs[:groups], refs[groups], refs[groups + 1 :]
    cot_ref, w_ref, fc_bias_ref = refs[:3]
    if first:
        middle_refs = refs[3 : groups + 3]
        out_acc, back_acc, grad_ref, bias_ref, sems = refs[groups + 3 :]
    else:
        prev_out_ref, prev_back_ref, proj_bias_ref = refs[3:6]
        out_ref, back_acc, low_ref, active_ref, bias_ref, out_acc, sems = refs[6:]
    step = pl.program_id(0) * pl.num_programs(1) + pl.program_id(1)
    last = pl.num_programs(0) * pl.num_programs(1) - 1
    span, model = normed_refs[0].shape
    tile = w_ref.shape[3]
    depth = model // rows
    if first:
        copies = [
            pltpu.make_async_copy(
                middle_refs[g], out_acc.at[pl.ds(g * span, span)], sems.at[g]
            )
            for g in range(groups)
        ]
    else:
        copies = [
            pltpu.make_async_copy(prev_out_ref, out_acc, sems.at[0]),
            pltpu.make_async_copy(prev_back_ref, back_acc, sems.at[1]),
        ]

    @pl.when(step == 0)
    def _():
        for copy in copies:
            copy.start()
        if first:
            back_acc[...] = jnp.zeros_like(back_acc)

    fc_weight = w_ref[:, 0, :depth].reshape(model, tile)
    proj_turned = w_ref[:, 0, depth:].reshape(model, tile)
    root = 0.7978845608028654
    actives, lows = [], []
    for g in range(groups):
        hidden = dot(normed_refs[g][...], fc_weight) + fc_bias_ref[0]
        square = hidden * hidden
        inner = jnp.tanh(hidden * (root + (root * 0.044715) * square))
        plus = 0.5 + 0.5 * inner
        actives.append((hidden * plus).astype(jnp.bfloat16))
        bend = 0.5 - 0.5 * inner * inner
        slope = plus + hidden * bend * (root + (3 * root * 0.044715) * square)
        grad_active = dot(cot_ref[g * span : (g + 1) * span], proj_turned)
        lows.append((grad_active * slope).astype(jnp.bfloat16))
    bias_ref[0] = functools.reduce(
        jnp.add, [jnp.sum(low.astype(jnp.float32), axis=0, keepdims=True) for low in lows]
    )
    low_all = jnp.concatenate(lows, axis=0)
    active_all = jnp.concatenate(actives, axis=0)
    if first:
        store_grads(
            rows, dps, turned_refs, cot_turned_ref, low_all, active_all, grad_ref
        )
    else:
        low_ref[0] = low_all
        active_ref[0] = active_all

    @pl.when(step == 0)
    def _():
        for copy in copies:
            copy.wait()

    out_acc[...] += dot_nt(active_all, proj_turned)
    back_acc[...] += dot_nt(low_all, fc_weight)
    if not first:

        @pl.when(step == last)
        def _():
            for g in range(groups):
                at = slice(g * span, (g + 1) * span)
                out_ref[g] = (out_acc[at] + proj_bias_ref[...]).astype(out_ref.dtype)


def feed_forward(first, normed, turned, cot, weight, fc_bias, rest, dps):
    groups = len(normed)
    span, model = normed[0].shape
    tokens = groups * span
    rows, cols, _, local = weight.shape
    depth = model // rows
    tile = min(HIDDEN_TILE, local)
    cut = model // (rows * dps)
    acc_shape = jax.ShapeDtypeStruct((tokens, model), jnp.float32)
    anywhere = pl.BlockSpec(memory_space=pl.ANY)
    if first:
        rest_specs = [anywhere] * groups
        out_spec, out_shape = fixed((tokens, model)), acc_shape
        scratch = [pltpu.SemaphoreType.DMA((groups,))]
        grad_specs = [pl.BlockSpec((rows, 1, dps, 2 * cut, tile), lambda c, i: (0, c, 0, 0, i))]
        grad_shapes = [jax.ShapeDtypeStruct((rows, cols, dps, 2 * cut, local), jnp.bfloat16)]
    else:
        rest_specs = [anywhere, anywhere, fixed((1, model))]
        out_spec = fixed((groups, span, model))
        out_shape = jax.ShapeDtypeStruct((groups, span, model), jnp.bfloat16)
        scratch = [pltpu.VMEM((tokens, model), jnp.float32), pltpu.SemaphoreType.DMA((2,))]
        grad_specs = [pl.BlockSpec((1, tokens, tile), lambda c, i: (c, 0, i))] * 2
        grad_shapes = [jax.ShapeDtypeStruct((cols, tokens, local), jnp.bfloat16)] * 2
    products = 12 if first else 8
    return pl.pallas_call(
        functools.partial(hidden_kernel, rows, dps, groups, first),
        grid=(cols, local // tile),
        in_specs=[fixed((span, model))] * groups
        + [fixed(part.shape) for part in turned]
        + [
            fixed((tokens, model)),
            pl.BlockSpec((rows, 1, 2 * depth, tile), lambda c, i: (0, c, 0, i)),
            pl.BlockSpec((1, 1, tile), lambda c, i: (c, 0, i)),
        ]
        + rest_specs,
        out_specs=[out_spec, fixed((tokens, model))]
        + grad_specs
        + [pl.BlockSpec((1, 1, tile), lambda c, i: (c, 0, i))],
        out_shape=[out_shape, acc_shape]
        + grad_shapes
        + [jax.ShapeDtypeStruct((cols, 1, local), jnp.float32)],
        scratch_shapes=scratch,
        compiler_params=params(60),
        cost_estimate=cost(
            products * tokens * model * cols * local,
            8 * model * cols * local,
            tokens * cols * local,
        ),
        name="feed_forward_first" if first else "feed_forward_second",
    )(*normed, *turned, cot, weight, fc_bias, *rest)


def middle_back_kernel(
    rows, cols, grad_ref, middle_ref, cot_ref, w_ref, vec_ref, dx_ref, turned_ref, datt_ref, sum_ref
):
    grad = grad_ref[0]
    unit, inverse = centered(middle_ref[...])
    total = cot_ref[0].astype(jnp.float32) + norm_back(grad, vec_ref[1:2], unit, inverse)
    dx_ref[...] = total
    low = total.astype(jnp.bfloat16)
    turned_ref[...] = jnp.transpose(low)
    depth = w_ref.shape[3] // rows
    for c in range(cols):
        part = dot_nt(low[:, :depth], out_block(w_ref, 0, c, rows))
        for r in range(1, rows):
            part = part + dot_nt(low[:, r * depth : (r + 1) * depth], out_block(w_ref, r, c, rows))
        part = part.astype(jnp.bfloat16)
        for r in range(rows):
            datt_ref[r, c] = part[:, r * PAIR : (r + 1) * PAIR]

    @pl.when(pl.program_id(0) == 0)
    def _():
        sum_ref[...] = jnp.zeros_like(sum_ref)

    sum_ref[0:1] += jnp.sum(grad * unit, axis=0, keepdims=True)
    sum_ref[1:2] += jnp.sum(grad, axis=0, keepdims=True)
    sum_ref[2:3] += jnp.sum(low.astype(jnp.float32), axis=0, keepdims=True)


def middle_back(grad, middle, cot, weight, vectors, g):
    span, model = middle.shape
    rows, cols = weight.shape[:2]
    tile = min(256, span)
    return pl.pallas_call(
        functools.partial(middle_back_kernel, rows, cols),
        grid=(span // tile,),
        in_specs=[
            pl.BlockSpec((1, tile, model), lambda i: (g, i, 0)),
            pl.BlockSpec((tile, model), lambda i: (i, 0)),
            pl.BlockSpec((1, tile, model), lambda i: (g, i, 0)),
            out_weight_spec(weight),
            fixed(vectors.shape),
        ],
        out_specs=[
            pl.BlockSpec((tile, model), lambda i: (i, 0)),
            pl.BlockSpec((model, tile), lambda i: (0, i)),
            pl.BlockSpec((rows, cols, tile, PAIR), lambda i: (0, 0, i, 0)),
            pl.BlockSpec((8, model), lambda i: (0, 0)),
        ],
        out_shape=[
            jax.ShapeDtypeStruct((span, model), jnp.float32),
            jax.ShapeDtypeStruct((model, span), jnp.bfloat16),
            jax.ShapeDtypeStruct((rows, cols, span, PAIR), jnp.bfloat16),
            jax.ShapeDtypeStruct((8, model), jnp.float32),
        ],
        compiler_params=params(60),
        cost_estimate=cost(2 * span * model * model, 2 * model * model + 18 * span * model),
        name="out_norm_back",
    )(grad, middle, cot, weight, vectors)


def out_grad_kernel(rows, dps, groups, *refs):
    out_ref = refs[-1]
    total = None
    for g in range(groups):
        att = jnp.concatenate([refs[groups + g][r, 0] for r in range(rows)], axis=1)
        part = dot(refs[g][...], att)
        total = part if total is None else total + part
    total = total.astype(jnp.bfloat16)
    half = out_ref.shape[3]
    for r in range(rows):
        for d in range(dps):
            at = (d * rows + r) * 2 * half
            out_ref[r, 0, d] = jnp.concatenate(
                [total[at : at + half], total[at + half : at + 2 * half]], axis=1
            )


def out_grad(turned, att, before, dps):
    groups = len(turned)
    model, span = turned[0].shape
    rows, cols = att[0].shape[:2]
    cut = model // (rows * dps)
    return pl.pallas_call(
        functools.partial(out_grad_kernel, rows, dps, groups),
        grid=(cols,),
        in_specs=[fixed((model, span))] * groups
        + [pl.BlockSpec((rows, 1, span, PAIR), lambda c: (0, c, 0, 0))] * groups
        + [pl.BlockSpec(memory_space=pl.ANY)],
        out_specs=pl.BlockSpec(
            (rows, 1, dps, cut // 2, 2 * rows * PAIR), lambda c: (0, c, 0, 4, 0)
        ),
        out_shape=jax.ShapeDtypeStruct(before.shape, before.dtype),
        compiler_params=params(60),
        cost_estimate=cost(2 * groups * span * model * model, 2 * model * model),
        input_output_aliases={2 * groups: 0},
        name="out_grad",
    )(*turned, *att, before)


def qkv_grad_kernel(final, dqkv_ref, x_ref, *refs):
    grad_ref, bias_ref, acc = refs[-3:]
    step = pl.program_id(0)
    grads = dqkv_ref[...]
    part = lax.dot_general(grads, x_ref[0], TN, preferred_element_type=jnp.float32)
    sums = jnp.sum(grads.astype(jnp.float32), axis=0, keepdims=True)

    @pl.when(step == 0)
    def _():
        acc[...] = refs[0][...] + part if final else part
        bias_ref[...] = jnp.zeros_like(bias_ref)

    @pl.when(step > 0)
    def _():
        acc[...] += part

    bias_ref[0:1] += sums

    @pl.when(step == pl.num_programs(0) - 1)
    def _():
        grad_ref[...] = jnp.transpose(acc[...]).astype(grad_ref.dtype) if final else acc[...]


def qkv_grad(dqkv, normed, before):
    tokens, width = dqkv.shape
    members, _, model = normed.shape
    final = len(before) == 1
    tile = tokens // members
    grad_type = (
        jax.ShapeDtypeStruct((model, width), jnp.bfloat16)
        if final
        else jax.ShapeDtypeStruct((width, model), jnp.float32)
    )
    return pl.pallas_call(
        functools.partial(qkv_grad_kernel, final),
        grid=(tokens // tile,),
        in_specs=[
            pl.BlockSpec((tile, width), lambda i: (i, 0)),
            pl.BlockSpec((1, tile, model), lambda i: (i, 0, 0)),
        ]
        + [fixed((width, model))] * len(before),
        out_specs=[fixed(grad_type.shape), fixed((8, width))],
        out_shape=[grad_type, jax.ShapeDtypeStruct((8, width), jnp.float32)],
        scratch_shapes=[pltpu.VMEM((width, model), jnp.float32)],
        compiler_params=params(60),
        cost_estimate=cost(2 * tokens * model * width, 2 * tokens * (model + width)),
        name="qkv_grad",
    )(dqkv, normed, *before)


def input_kernel(rows, dps, plane_ref, dqkv_ref, left_ref, right_ref, dx_ref, tok_ref, *refs):
    gain_ref = refs[0]
    out_ref, sum_ref, acc = refs[-3:]
    step = pl.program_id(0) * pl.num_programs(1) + pl.program_id(1)
    short = left_ref.shape[3] * 2 // 3
    grads = []
    for part in range(3):
        lanes = slice(part * PAIR, (part + 1) * PAIR)
        grads += [dqkv_ref[half, 0, :, lanes] for half in range(2)]
    pieces = []
    for r in range(rows):
        for d in range(dps):
            at = (plane_ref[0] - d) & (dps - 1)
            left, right = left_ref[at, r, 0], right_ref[at, r, 0]
            last = jnp.concatenate([left[short:], right[short:]], axis=0)
            pieces.append(jnp.concatenate([left[:short], right[:short], last], axis=1))
    weights = jnp.concatenate(pieces, axis=0)
    piece = dot_nt(jnp.concatenate(grads, axis=1), weights)

    @pl.when(step == 0)
    def _():
        acc[...] = piece

    @pl.when(step > 0)
    def _():
        acc[...] += piece

    @pl.when(step == pl.num_programs(0) * pl.num_programs(1) - 1)
    def _():
        grad = acc[...]
        unit, inverse = centered(tok_ref[0].astype(jnp.float32))
        out_ref[0] = dx_ref[...] + norm_back(grad, gain_ref[...], unit, inverse)
        sum_ref[0:1] = jnp.sum(grad * unit, axis=0, keepdims=True)
        sum_ref[1:2] = jnp.sum(grad, axis=0, keepdims=True)


def input_back(plane, dqkv, dx, tokens, weight, gain, before, g):
    dps, rows, cols, high, _ = weight.shape
    span, model = dx.shape
    return pl.pallas_call(
        functools.partial(input_kernel, rows, dps),
        grid=(rows // 2, cols),
        in_specs=[
            pl.BlockSpec(memory_space=pltpu.SMEM),
            pl.BlockSpec((2, 1, span, 3 * PAIR), lambda i, c: (i, c, 0, 0)),
            pl.BlockSpec((dps, rows, 1, high, 2 * PAIR), lambda i, c: (0, 0, c, 0, i)),
            pl.BlockSpec((dps, rows, 1, high, 2 * PAIR), lambda i, c: (0, 0, c, 0, rows // 2 + i)),
            fixed((span, model)),
            pl.BlockSpec((1, span, model), lambda i, c: (g, 0, 0), pipeline_mode=pl.Buffered(1)),
            fixed((1, model)),
        ]
        + [pl.BlockSpec(memory_space=pl.ANY)] * len(before),
        out_specs=[
            pl.BlockSpec((1, span, model), lambda i, c: (g, 0, 0), pipeline_mode=pl.Buffered(1)),
            fixed((8, model)),
        ],
        out_shape=[
            jax.ShapeDtypeStruct(tokens.shape, jnp.float32),
            jax.ShapeDtypeStruct((8, model), jnp.float32),
        ],
        scratch_shapes=[pltpu.VMEM((span, model), jnp.float32)],
        compiler_params=params(60),
        cost_estimate=cost(6 * span * model * model, 6 * model * model + 12 * span * model),
        input_output_aliases={7: 0} if before else {},
        name="input_back",
    )(plane, dqkv, weight, weight, dx, tokens, gain, *before)


def head_body(
    tokens,
    cotangent,
    branch,
    ln1_gain,
    ln1_bias,
    qkv_weight,
    qv_bias,
    out_weight,
    out_bias,
    ln2_gain,
    ln2_bias,
    fc_weight,
    fc_bias,
    proj_weight,
    proj_bias,
):
    groups, span, model = tokens.shape
    rows = lax.axis_size("row")
    cols = lax.axis_size("col")
    dps = lax.axis_size("dp")
    members = rows * cols
    count = groups * span
    head_cols = qv_bias.shape[1]
    hidden_cols = fc_bias.shape[0]

    def spread(shard):
        whole = lax.all_gather(shard, MESH_AXES, axis=0, tiled=False)
        return whole.reshape((rows, cols) + shard.shape)

    def swap(blocks):
        return lax.all_to_all(blocks, MESH_AXES, 0, 0, tiled=True)

    def collect_plane(partial):
        partial = partial.reshape((members,) + partial.shape[2:])
        partial = lax.psum_scatter(partial, MESH_AXES, scatter_dimension=0, tiled=True)
        return partial.reshape(partial.shape[1:])

    def exchange_dp(partial):
        me = lax.axis_index("dp")
        summed = lax.dynamic_index_in_dim(partial, me, 0, False).astype(jnp.float32)
        for shift in range(1, dps):
            piece = lax.dynamic_index_in_dim(partial, (me + shift) % dps, 0, False)
            pairs = [(i, (i + shift) % dps) for i in range(dps)]
            summed = summed + lax.ppermute(piece, "dp", pairs).astype(jnp.float32)
        return summed

    def collect_dp(partial):
        partial = lax.psum_scatter(partial, "dp", scatter_dimension=0, tiled=True)
        return partial[0].astype(jnp.float32)

    def total(values):
        for axis in ("row", "col", "dp"):
            size = lax.axis_size(axis)
            step = 1
            while step < size:
                pairs = [(i, i ^ step) for i in range(size)]
                values = values + lax.ppermute(values, axis, pairs)
                step *= 2
        return values

    half = hidden_cols // 2
    residual = tokens.astype(jnp.float32)
    normed = normalize(residual, ln1_gain, ln1_bias).astype(jnp.bfloat16)
    row = lax.axis_index("row")
    col = lax.axis_index("col")
    own = qkv_weight.reshape(-1, 3, rows, PAIR).transpose(2, 0, 1, 3)
    own = lax.all_to_all(own.reshape(rows, -1, 3 * PAIR), "row", 0, 0, tiled=True)
    own = own.reshape(model, 3 * PAIR)
    own_bias = lax.dynamic_slice_in_dim(qv_bias, row * PAIR, PAIR, 1)
    own_bias = jnp.concatenate([own_bias[0], jnp.zeros((PAIR,), jnp.float32), own_bias[1]])
    fc_full = lax.all_gather(fc_bias, "col", axis=0).reshape(cols, 1, hidden_cols)

    normed_all = [lax.all_gather(normed[0], MESH_AXES, axis=0, tiled=False)]
    cot_flat = cotangent.reshape(count, model)
    cot_turned = cot_flat.T
    proj_bias_sum = jnp.sum(cot_flat.astype(jnp.float32), axis=0)
    plane = lax.axis_index("dp")
    short = qkv_weight.shape[0] // dps
    part = lax.dynamic_slice_in_dim(qkv_weight, plane * short, short, 0)
    last = jnp.concatenate([part[: short // 2, 2], part[short // 2 :, 2]], axis=1)
    part = jnp.concatenate([part[:, 0], part[:, 1]], axis=1)
    later = jnp.concatenate([normed[1], part, last], axis=0)
    shards = pack_weights(fc_weight, proj_weight, out_weight)
    normed_all[0], later, cot_turned, proj_bias_sum, shards, own, fc_full = (
        lax.optimization_barrier(
            (normed_all[0], later, cot_turned, proj_bias_sum, shards, own, fc_full)
        )
    )
    later = lax.all_gather(later, MESH_AXES, axis=0, tiled=False)
    normed_all.append(later)
    vectors = jnp.stack([out_bias, ln2_gain, ln2_bias] + [out_bias] * 5)
    gains = jnp.stack([ln2_gain] * 8)
    qkv, att, att_own, log_totals, middle, normed_two, turned_two = [], [], [], [], [], [], []
    w_first = spread(shards[0])
    w_second = spread(shards[1])
    def step_up(value):
        return lax.ppermute(value, "dp", [(i, i + 1) for i in range(dps - 1)])

    def step_down(value):
        return lax.ppermute(value, "dp", [(i + 1, i) for i in range(dps - 1)])

    for g in range(groups):
        qkv.append(project_qkv(normed_all[g], own, own_bias, span))
        mixed, totals = attend(branch[g], qkv[g])
        if g < groups - 1:
            mixed, normed_all[g + 1] = lax.optimization_barrier((mixed, normed_all[g + 1]))
        att_own.append(mixed)
        if g > 0:
            quarter = normed_all[1][:, span:].reshape(rows, cols, -1, model)
            ups, downs = [step_up(quarter)], [step_down(quarter)]
            mixed, att[g - 1], ups, downs = lax.optimization_barrier(
                (mixed, att[g - 1], ups, downs)
            )
            ups.append(step_up(ups[-1]))
            downs.append(step_down(downs[-1]))
        log_totals.append(totals)
        att.append(swap(mixed.reshape(members, span, PAIR)).reshape(rows, cols, span, PAIR))
    for g in range(groups):
        mid, low, turned = project_out(tokens, att[g], w_first, vectors, g)
        middle.append(mid)
        normed_two.append(low)
        turned_two.append(turned)
    all_turned = turned_two + [cot_turned]
    normed_two[-1], ups, downs = lax.optimization_barrier((normed_two[-1], ups, downs))
    ups.append(step_up(ups[-1]))
    downs.append(step_down(downs[-1]))
    out_part, back_part, grad_first, fc_sum_first = feed_forward(
        True, normed_two, all_turned, cot_flat, w_first, fc_full[:, :, :half], middle, dps
    )
    plane_first = collect_plane(grad_first)
    block_out, grad_two, low, active, fc_sum_second = feed_forward(
        False,
        normed_two,
        [],
        cot_flat,
        w_second,
        fc_full[:, :, half:],
        (out_part, back_part, proj_bias[None]),
        dps,
    )
    grad_two = grad_two.reshape(groups, span, model)
    dx, dx_turned, grad_att, sums_two = [], [], [], []
    for g in range(groups):
        rows_grad, turned, datt, sums = middle_back(
            grad_two, middle[g], cotangent, w_first, gains, g
        )
        dx.append(rows_grad)
        dx_turned.append(turned)
        sums_two.append(sums)
        if g == 0:
            datt, low, active = lax.optimization_barrier((datt, low, active))
        grad_att.append(
            swap(datt.reshape(members, span, PAIR)).reshape(members * span, PAIR)
        )
    grad_second = hidden_grad(turned_two, cot_turned, low, active, dps, rows)
    grad_att[0], grad_second = lax.optimization_barrier((grad_att[0], grad_second))
    plane_second = collect_plane(out_grad(dx_turned, att, grad_second, dps))
    grads, bias_sums, before = [], [], []
    for g in range(groups):
        grad = attend_back(branch[g], qkv[g], att_own[g], grad_att[g], log_totals[g])
        if g == 0:
            grad, grad_att[1], plane_first, ups, downs = lax.optimization_barrier(
                (grad, grad_att[1], plane_first, ups, downs)
            )
            hidden_first = exchange_dp(plane_first)
        else:
            grad, hidden_first, grads[0] = lax.optimization_barrier(
                (grad, hidden_first, grads[0])
            )
        grad_qkv, bias_sum = qkv_grad(grad, normed_all[g], before)
        before = [grad_qkv]
        bias_sums.append(bias_sum[0])
        grads.append(
            swap(grad.reshape(members, span, 3 * PAIR)).reshape(rows, cols, span, 3 * PAIR)
        )
    grads[-1], grad_qkv, plane_second = lax.optimization_barrier(
        (grads[-1], grad_qkv, plane_second)
    )
    hidden_second = collect_dp(plane_second)
    grad_qkv = exchange_dp(grad_qkv.reshape(dps, rows, -1, 3 * PAIR))
    quarters = [quarter]
    for shift in range(1, dps):
        quarters.append(jnp.where(plane >= shift, ups[shift - 1], downs[dps - shift - 1]))
    w_qkv = jnp.stack(quarters)
    input_grads, sums_one = [], []
    for g in range(groups):
        rows_grad, sums = input_back(
            plane[None], grads[g], dx[g], tokens, w_qkv, ln1_gain[None], input_grads, g
        )
        input_grads = [rows_grad]
        sums_one.append(sums)
    sums_two = functools.reduce(jnp.add, sums_two)
    fc_sum = jnp.concatenate([fc_sum_first, fc_sum_second], axis=2).reshape(-1)
    sums_one = functools.reduce(jnp.add, sums_one)
    bias_sum = functools.reduce(jnp.add, bias_sums)
    qv_sum = jnp.zeros((2, model), jnp.float32)
    qv_sum = lax.dynamic_update_slice(
        qv_sum,
        jnp.stack([bias_sum[:PAIR], bias_sum[2 * PAIR :]]),
        (0, col * head_cols + row * PAIR),
    )
    small = (sums_two[2], sums_two[0], sums_two[1], fc_sum, proj_bias_sum)
    small += (sums_one[0], sums_one[1], qv_sum.reshape(-1))
    small = total(jnp.concatenate(small))
    grad_qkv = lax.all_to_all(grad_qkv, "row", 0, 0, tiled=True)
    d_qkv = grad_qkv.reshape(rows, -1, 3, PAIR).transpose(1, 2, 0, 3).reshape(-1, 3, head_cols)
    cut = model // (rows * dps)
    d_fc, d_proj = (
        jnp.concatenate([hidden_first[at : at + cut], hidden_second[at : at + cut]], axis=1)
        for at in (0, cut)
    )
    packed_out = hidden_second[2 * cut :]
    d_out = jnp.concatenate([packed_out[:, :head_cols], packed_out[:, head_cols:]], axis=0).T
    parts, at = [], 0
    for size in (model, model, model, hidden_cols * cols, model, model, model, 2 * model):
        parts.append(small[at : at + size])
        at += size
    s_out, s_gain_two, s_bias_two, s_fc, s_proj, s_gain_one, s_bias_one, s_qv = parts
    return (
        block_out,
        input_grads[0],
        s_gain_one,
        s_bias_one,
        d_qkv,
        s_qv.reshape(2, model),
        d_out,
        s_out,
        s_gain_two,
        s_bias_two,
        d_fc,
        s_fc,
        d_proj.T,
        s_proj,
    )


def by_heads(mesh):
    rows, cols = mesh.shape["row"], mesh.shape["col"]

    def body(tokens, cotangent, branch, ln1_gain, ln1_bias, qkv_weight, *rest):
        width = qkv_weight.shape[2] * cols
        whole = tokens.shape[1] * rows * cols
        fits = width == rows * cols * PAIR and rows == 4 and mesh.shape["dp"] == 4 and tokens.shape[0] == 2
        fits = fits and qkv_weight.shape[0] * 4 == qkv_weight.shape[2] * cols
        fits = fits and rest[6].shape[0] == 4 * rows * PAIR
        fits = fits and all(size & (size - 1) == 0 for size in mesh.shape.values())
        fits = fits and whole == PLEN + CONTS * CLEN and tokens.shape[1] % BQ == 0
        chosen = head_body if fits else gathered_body
        return chosen(tokens, cotangent, branch, ln1_gain, ln1_bias, qkv_weight, *rest)

    return body


def solution(mesh):
    placed = (
        P("dp", ("row", "col"), None),
        P("dp", ("row", "col"), None),
        P("dp", None),
        P(),
        P(),
        P("row", None, "col"),
        P(None, "col"),
        P("col", "row"),
        P(),
        P(),
        P(),
        P("row", "col"),
        P("col"),
        P("col", "row"),
        P(),
    )
    return jax.shard_map(
        by_heads(mesh),
        mesh=mesh,
        in_specs=placed,
        out_specs=(
            P("dp", ("row", "col"), None),
            P("dp", ("row", "col"), None),
            P(),
            P(),
            P(("dp", "row"), None, "col"),
            P(),
            P("col", ("dp", "row")),
            P(),
            P(),
            P(),
            P(("dp", "row"), "col"),
            P(),
            P("col", ("dp", "row")),
            P(),
        ),
        check_vma=False,
    )
```

```python
import functools

import jax
import jax.numpy as jnp
from jax import lax
from jax.experimental import pallas as pl
from jax.experimental.pallas import tpu as pltpu
from jax.sharding import PartitionSpec as P

HEAD = 64
PLEN = 2048
CLEN = 256
CONTS = 8


EPSILON = 1e-05
MASKED_SCORE = -1e30
LOG2E = 1.4426950408889634
PAIR = 2 * HEAD
BQ = 256
BK = 512
BK_BACK = 512
HIDDEN_TILE = 512
NT = (((1,), (1,)), ((), ()))
TN = (((0,), (0,)), ((), ()))
MESH_AXES = ("row", "col")


def normalize(values, gain, shift):
    center = values - jnp.mean(values, axis=-1, keepdims=True)
    spread = jnp.mean(center * center, axis=-1, keepdims=True)
    return center * lax.rsqrt(spread + EPSILON) * gain + shift


def gelu_tanh(values):
    return jax.nn.gelu(values, approximate=True)


def allowed_keys(row_pos, col_pos, branch_cut):
    row_seg = jnp.where(row_pos >= PLEN, (row_pos - PLEN) // CLEN, -1)
    col_seg = jnp.where(col_pos >= PLEN, (col_pos - PLEN) // CLEN, -1)
    picked = (row_seg[:, None] == jnp.arange(CONTS, dtype=jnp.int32)[None, :]).astype(jnp.int32)
    row_cut = jnp.sum(picked * branch_cut[None, :], axis=1)
    causal = col_pos[None, :] <= row_pos[:, None]
    same_seq = col_seg[None, :] == row_seg[:, None]
    in_prefix = (
        (row_seg[:, None] >= 0) & (col_seg[None, :] < 0) & (col_pos[None, :] < row_cut[:, None])
    )
    return same_seq & causal | in_prefix


def add_trees(first, second):
    return jax.tree.map(lambda total, extra: total + extra, first, second)


def gathered_body(
    tokens,
    cotangent,
    branch,
    ln1_gain,
    ln1_bias,
    qkv_weight,
    qv_bias,
    out_weight,
    out_bias,
    ln2_gain,
    ln2_bias,
    fc_weight,
    fc_bias,
    proj_weight,
    proj_bias,
):
    scale = HEAD ** (-0.5)
    width = tokens.shape[2]
    local_rows = tokens.shape[1]
    head_cols = qv_bias.shape[1]
    head_count = head_cols // HEAD
    ff_local = fc_bias.shape[0]
    col_count = lax.axis_size("col")
    row_count = lax.axis_size("row")
    row_rows = local_rows * col_count
    group_rows = row_rows * row_count
    q_block = min(512, row_rows)
    block_count = row_rows // q_block
    row_base = lax.axis_index("row") * row_rows
    col_index = lax.axis_index("col")
    bias_three = jnp.stack([qv_bias[0], jnp.zeros_like(qv_bias[0]), qv_bias[1]])
    key_pos = jnp.arange(group_rows, dtype=jnp.int32)
    block_starts = jnp.arange(block_count, dtype=jnp.int32) * q_block

    def spread_rows(values):
        return lax.all_gather(values, "col", axis=0, tiled=True)

    def spread_grads(values):
        return lax.all_gather(values, "col", axis=0, tiled=True)

    def sum_branch(values):
        return lax.psum_scatter(values, "col", scatter_dimension=0, tiled=True)

    def sum_inputs(values):
        return lax.psum_scatter(values, "col", scatter_dimension=0, tiled=True)

    kept_weights = (
        lax.all_gather(qkv_weight, "row", axis=0, tiled=True),
        lax.all_gather(out_weight, "row", axis=1, tiled=True),
        lax.all_gather(fc_weight, "row", axis=0, tiled=True),
        lax.all_gather(proj_weight, "row", axis=1, tiled=True),
    )

    def block_scores(queries3, keys3, offset, branch_cut):
        q_part = lax.dynamic_slice_in_dim(queries3, offset, q_block, 0)
        row_pos = row_base + offset + jnp.arange(q_block, dtype=jnp.int32)
        allowed = allowed_keys(row_pos, key_pos, branch_cut)
        scores = (
            jnp.einsum("qhd,khd->hqk", q_part, keys3, preferred_element_type=jnp.float32) * scale
        )
        return (q_part, jnp.where(allowed[None], scores, MASKED_SCORE))

    def micro_step(carry, micro_item):
        grads_acc, small_acc = carry
        tok_rows, cot_rows, branch_cut = micro_item
        w_qkv, w_out, w_fc, w_proj = kept_weights
        residual = tok_rows.astype(jnp.float32)
        normed = normalize(residual, ln1_gain, ln1_bias).astype(jnp.bfloat16)
        normed_all = spread_rows(normed)
        projected = jnp.einsum("td,dsf->tsf", normed_all, w_qkv, preferred_element_type=jnp.float32)
        projected = (projected + bias_three[None]).astype(jnp.bfloat16)
        key_rows, value_rows = (
            lax.all_gather(projected[:, 1], "row", axis=0, tiled=True),
            lax.all_gather(projected[:, 2], "row", axis=0, tiled=True),
        )
        queries3 = projected[:, 0].reshape(row_rows, head_count, HEAD)
        keys3 = key_rows.reshape(group_rows, head_count, HEAD)
        values3 = value_rows.reshape(group_rows, head_count, HEAD)

        def attend(offset):
            q_part, scores = block_scores(queries3, keys3, offset, branch_cut)
            row_peak = jnp.max(scores, axis=-1, keepdims=True)
            exponent = jnp.exp(scores - row_peak)
            row_total = jnp.sum(exponent, axis=-1, keepdims=True)
            probs_low = (exponent / row_total).astype(jnp.bfloat16)
            mixed_rows = jnp.einsum(
                "hqk,khd->qhd", probs_low, values3, preferred_element_type=jnp.float32
            )
            return (mixed_rows, (row_peak + jnp.log(row_total))[..., 0])

        attended, log_totals = lax.map(attend, block_starts)
        attended = attended.reshape(row_rows, head_cols).astype(jnp.bfloat16)
        branch_part = jnp.dot(attended, w_out, preferred_element_type=jnp.float32)
        middle = residual + sum_branch(branch_part) + out_bias
        normed_two = normalize(middle, ln2_gain, ln2_bias).astype(jnp.bfloat16)
        normed_two_all = spread_rows(normed_two)
        hidden = jnp.dot(normed_two_all, w_fc, preferred_element_type=jnp.float32) + fc_bias
        active = gelu_tanh(hidden).astype(jnp.bfloat16)
        ffn_part = jnp.dot(active, w_proj, preferred_element_type=jnp.float32)
        output_rows = (middle + sum_branch(ffn_part) + proj_bias).astype(jnp.bfloat16)
        cot_all = spread_grads(cot_rows)
        grad_proj = jnp.einsum("tf,td->fd", active, cot_all, preferred_element_type=jnp.float32)
        grad_proj_bias = jnp.sum(cot_rows.astype(jnp.float32), axis=0)
        grad_active = jnp.einsum("td,fd->tf", cot_all, w_proj, preferred_element_type=jnp.float32)
        grad_hidden = jax.vjp(gelu_tanh, hidden)[1](grad_active)[0].astype(jnp.bfloat16)
        grad_fc = jnp.einsum(
            "td,tf->df", normed_two_all, grad_hidden, preferred_element_type=jnp.float32
        )
        grad_fc_bias = jnp.sum(grad_hidden.astype(jnp.float32), axis=0)
        grad_normed_two = sum_inputs(
            jnp.einsum("tf,df->td", grad_hidden, w_fc, preferred_element_type=jnp.float32)
        )
        back_middle, grad_gain_two, grad_bias_two = jax.vjp(normalize, middle, ln2_gain, ln2_bias)[
            1
        ](grad_normed_two)
        grad_middle = cot_rows.astype(jnp.float32) + back_middle
        grad_out_rows = grad_middle.astype(jnp.bfloat16)
        grad_out_all = spread_grads(grad_out_rows)
        grad_out = jnp.einsum(
            "tc,td->cd", attended, grad_out_all, preferred_element_type=jnp.float32
        )
        grad_out_bias = jnp.sum(grad_out_rows.astype(jnp.float32), axis=0)
        grad_att = jnp.einsum("td,cd->tc", grad_out_all, w_out, preferred_element_type=jnp.float32)
        grad_att = grad_att.astype(jnp.bfloat16).reshape(row_rows, head_count, HEAD)

        def attend_back(acc_pair, block_item):
            offset, log_total = block_item
            grad_keys_acc, grad_values_acc = acc_pair
            q_part, scores = block_scores(queries3, keys3, offset, branch_cut)
            probs = jnp.exp(scores - log_total[..., None])
            probs_low = probs.astype(jnp.bfloat16)
            grad_part = lax.dynamic_slice_in_dim(grad_att, offset, q_block, 0)
            grad_values_acc = grad_values_acc + jnp.einsum(
                "hqk,qhd->khd", probs_low, grad_part, preferred_element_type=jnp.float32
            )
            grad_probs = jnp.einsum(
                "qhd,khd->hqk", grad_part, values3, preferred_element_type=jnp.float32
            )
            center = jnp.sum(grad_probs * probs, axis=-1, keepdims=True)
            grad_scores = (probs * (grad_probs - center)).astype(jnp.bfloat16)
            grad_keys_acc = (
                grad_keys_acc
                + jnp.einsum(
                    "hqk,qhd->khd", grad_scores, q_part, preferred_element_type=jnp.float32
                )
                * scale
            )
            grad_query = (
                jnp.einsum("hqk,khd->qhd", grad_scores, keys3, preferred_element_type=jnp.float32)
                * scale
            )
            return ((grad_keys_acc, grad_values_acc), grad_query)

        empty_keys = jnp.zeros((group_rows, head_count, HEAD), jnp.float32)
        (grad_keys, grad_values), grad_queries = lax.scan(
            attend_back, (empty_keys, empty_keys), (block_starts, log_totals)
        )
        own_keys, own_values = (
            lax.psum_scatter(
                grad_keys.reshape(group_rows, head_cols).astype(jnp.bfloat16),
                "row",
                scatter_dimension=0,
                tiled=True,
            ).astype(jnp.float32),
            lax.psum_scatter(
                grad_values.reshape(group_rows, head_cols).astype(jnp.bfloat16),
                "row",
                scatter_dimension=0,
                tiled=True,
            ).astype(jnp.float32),
        )
        grad_projected = jnp.stack(
            [grad_queries.reshape(row_rows, head_cols), own_keys, own_values], axis=1
        ).astype(jnp.bfloat16)
        grad_qkv = jnp.einsum(
            "td,tsf->dsf", normed_all, grad_projected, preferred_element_type=jnp.float32
        )
        grad_qkv_bias = jnp.sum(grad_projected.astype(jnp.float32), axis=0)
        grad_normed = sum_inputs(
            jnp.einsum("tsf,dsf->td", grad_projected, w_qkv, preferred_element_type=jnp.float32)
        )
        back_input, grad_gain_one, grad_bias_one = jax.vjp(normalize, residual, ln1_gain, ln1_bias)[
            1
        ](grad_normed)
        input_rows = grad_middle + back_input
        weight_terms = (grad_qkv, grad_out, grad_fc, grad_proj)
        small_terms = (
            grad_gain_one,
            grad_bias_one,
            grad_qkv_bias,
            grad_out_bias,
            grad_gain_two,
            grad_bias_two,
            grad_fc_bias,
            grad_proj_bias,
        )
        return (
            (add_trees(grads_acc, weight_terms), add_trees(small_acc, small_terms)),
            (output_rows, input_rows),
        )

    grads_init = (
        jnp.zeros((width, 3, head_cols), jnp.float32),
        jnp.zeros((head_cols, width), jnp.float32),
        jnp.zeros((width, ff_local), jnp.float32),
        jnp.zeros((ff_local, width), jnp.float32),
    )
    vector_zero = jnp.zeros((width,), jnp.float32)
    small_init = (
        vector_zero,
        vector_zero,
        jnp.zeros((3, head_cols), jnp.float32),
        vector_zero,
        vector_zero,
        vector_zero,
        jnp.zeros((ff_local,), jnp.float32),
        vector_zero,
    )
    (grads_acc, small_acc), (block_out, input_grad) = lax.scan(
        micro_step, (grads_init, small_init), (tokens, cotangent, branch)
    )
    (
        gain_one,
        bias_one,
        qkv_bias_acc,
        out_bias_acc,
        gain_two,
        bias_two,
        fc_bias_acc,
        proj_bias_acc,
    ) = small_acc
    qv_full = lax.dynamic_update_slice(
        jnp.zeros((2, width), jnp.float32),
        jnp.stack([qkv_bias_acc[0], qkv_bias_acc[2]]),
        (jnp.int32(0), col_index * head_cols),
    )
    fc_full = lax.dynamic_update_slice(
        jnp.zeros((ff_local * col_count,), jnp.float32), fc_bias_acc, (col_index * ff_local,)
    )
    summed = lax.psum(
        (gain_one, bias_one, qv_full, out_bias_acc, gain_two, bias_two, fc_full, proj_bias_acc),
        ("dp", "row", "col"),
    )
    return (
        block_out,
        input_grad,
        summed[0],
        summed[1],
        lax.psum_scatter(
            grads_acc[0].astype(jnp.bfloat16), ("dp", "row"), scatter_dimension=0, tiled=True
        ).astype(jnp.float32),
        summed[2],
        lax.psum_scatter(
            grads_acc[1].astype(jnp.bfloat16), ("dp", "row"), scatter_dimension=1, tiled=True
        ).astype(jnp.float32),
        summed[3],
        summed[4],
        summed[5],
        lax.psum_scatter(
            grads_acc[2].astype(jnp.bfloat16), ("dp", "row"), scatter_dimension=0, tiled=True
        ).astype(jnp.float32),
        summed[6],
        lax.psum_scatter(
            grads_acc[3].astype(jnp.bfloat16), ("dp", "row"), scatter_dimension=1, tiled=True
        ).astype(jnp.float32),
        summed[7],
    )


def dot(left, right):
    return jnp.dot(left, right, preferred_element_type=jnp.float32)


def dot_nt(left, right):
    return lax.dot_general(left, right, NT, preferred_element_type=jnp.float32)


def cost(flops, moved, exps=0):
    return pl.CostEstimate(flops=int(flops), bytes_accessed=int(moved), transcendentals=int(exps))


def params(mebibytes):
    return pltpu.CompilerParams(vmem_limit_bytes=mebibytes * 2**20)


def fixed(shape):
    return pl.BlockSpec(shape, lambda *_: (0,) * len(shape), pipeline_mode=pl.Buffered(1))


def pair_rows(rows):
    low = lax.broadcasted_iota(jnp.int32, rows.shape, 1) < HEAD
    zero = jnp.zeros_like(rows)
    return jnp.concatenate([jnp.where(low, rows, zero), jnp.where(low, zero, rows)], axis=0)


def pick_lanes(stacked):
    half = stacked.shape[0] // 2
    low = lax.broadcasted_iota(jnp.int32, (half, stacked.shape[1]), 1) < HEAD
    return jnp.where(low, stacked[:half], stacked[half:])


def pack_kernel(fc_ref, proj_ref, out_ref, first_ref, second_ref):
    depth, hidden = fc_ref.shape
    half = hidden // 2
    turned = jnp.transpose(proj_ref[...])
    for at, ref in ((0, first_ref), (half, second_ref)):
        ref[:depth] = fc_ref[:, at : at + half]
        ref[depth : 2 * depth] = turned[:, at : at + half]
    for h in range(out_ref.shape[0] // PAIR):
        first_ref[2 * depth :, h * depth : (h + 1) * depth] = out_ref[h * PAIR : (h + 1) * PAIR]


def pack_weights(fc_weight, proj_weight, out_weight):
    depth, hidden = fc_weight.shape
    shapes = [(2 * depth + PAIR, hidden // 2), (2 * depth, hidden // 2)]
    return pl.pallas_call(
        pack_kernel,
        in_specs=[pl.BlockSpec(memory_space=pltpu.VMEM)] * 3,
        out_specs=[pl.BlockSpec(memory_space=pltpu.VMEM)] * 2,
        out_shape=[jax.ShapeDtypeStruct(shape, jnp.bfloat16) for shape in shapes],
        compiler_params=params(60),
        cost_estimate=cost(1, 8 * depth * hidden),
        name="pack_weights",
    )(fc_weight, proj_weight, out_weight)


def qkv_kernel(x_ref, w_ref, vec_ref, out_ref):
    rows = x_ref[...].reshape(out_ref.shape[0], x_ref.shape[2])
    values = (dot(rows, w_ref[...]) + vec_ref[0:1]) * vec_ref[1:2]
    out_ref[...] = values.astype(out_ref.dtype)


def project_qkv(normed, weight, bias, span):
    members, _, model = normed.shape
    width = weight.shape[1]
    tokens = members * span
    vectors = jnp.stack([bias, jnp.where(jnp.arange(width) < PAIR, HEAD**-0.5, 1.0)])
    return pl.pallas_call(
        qkv_kernel,
        grid=(members // 2,),
        in_specs=[
            pl.BlockSpec((2, span, model), lambda i: (i, 0, 0)),
            fixed((model, width)),
            fixed((2, width)),
        ],
        out_specs=pl.BlockSpec((2 * span, width), lambda i: (i, 0)),
        out_shape=jax.ShapeDtypeStruct((tokens, width), jnp.bfloat16),
        compiler_params=params(60),
        cost_estimate=cost(2 * tokens * model * width, 2 * tokens * (model + width)),
        name="qkv",
    )(normed, weight, vectors)


def attend_kernel(
    bk, cut_ref, qkv_ref, o_ref, lse_ref, s_ref, own_ref, value_ref, peak_ref, acc_ref
):
    i = pl.program_id(0)
    prompt_blocks = PLEN // BQ

    @pl.when(i == 0)
    def _():
        value_ref[:, :PAIR] = qkv_ref[:, 2 * PAIR : 3 * PAIR]
        value_ref[:, PAIR:] = jnp.ones((value_ref.shape[0], PAIR), value_ref.dtype)

    start = pl.multiple_of(i * BQ, BQ)
    queries = pair_rows(qkv_ref[pl.ds(start, BQ), 0:PAIR])
    limit = jnp.where(i < prompt_blocks, start, cut_ref[jnp.maximum(i - prompt_blocks, 0)])
    full = limit // bk
    rest = limit - full * bk

    def scores(first, count):
        keys = qkv_ref[pl.ds(pl.multiple_of(first, BQ), count), PAIR : 2 * PAIR]
        return dot_nt(queries, keys) * LOG2E

    def lane_peak(values):
        return functools.reduce(
            jnp.maximum, [values[:, at : at + 128] for at in range(0, values.shape[1], 128)]
        )

    own = scores(start, BQ)
    row = lax.broadcasted_iota(jnp.int32, own.shape, 0) & (BQ - 1)
    own = jnp.where(lax.broadcasted_iota(jnp.int32, own.shape, 1) <= row, own, MASKED_SCORE)
    own_ref[...] = own
    peak_ref[...] = lane_peak(own)

    def score_step(j, none):
        values = scores(j * bk, bk)
        s_ref[j] = values
        peak_ref[...] = jnp.maximum(peak_ref[...], lane_peak(values))
        return none

    lax.fori_loop(0, full, score_step, 0)

    @pl.when(rest > 0)
    def _():
        values = scores(full * bk, bk)
        seen = lax.broadcasted_iota(jnp.int32, values.shape, 1) < rest
        values = jnp.where(seen, values, MASKED_SCORE)
        s_ref[full] = values
        peak_ref[...] = jnp.maximum(peak_ref[...], lane_peak(values))

    peak = jnp.max(peak_ref[...], axis=1, keepdims=True)
    probs = jnp.exp2(own_ref[...] - peak).astype(jnp.bfloat16)
    acc_ref[...] = dot(probs, value_ref[pl.ds(start, BQ), :])

    def value_step(j, none):
        probs = jnp.exp2(s_ref[j] - peak).astype(jnp.bfloat16)
        acc_ref[...] += dot(probs, value_ref[pl.ds(pl.multiple_of(j * bk, bk), bk), :])
        return none

    lax.fori_loop(0, full + jnp.where(rest > 0, 1, 0), value_step, 0)
    total = acc_ref[:, PAIR:]
    o_ref[...] = pick_lanes(acc_ref[:, :PAIR] / total).astype(o_ref.dtype)
    lse_ref[0] = jnp.transpose(peak + jnp.log2(total))[:8]


def attend(cut, qkv):
    tokens = qkv.shape[0]
    blocks = tokens // BQ
    pairs = 2 * tokens * tokens // 4
    return pl.pallas_call(
        functools.partial(attend_kernel, BK),
        grid=(blocks,),
        in_specs=[pl.BlockSpec(memory_space=pltpu.SMEM), fixed((tokens, 3 * PAIR))],
        out_specs=[
            pl.BlockSpec((BQ, PAIR), lambda i: (i, 0)),
            pl.BlockSpec((1, 8, 2 * BQ), lambda i: (i, 0, 0)),
        ],
        out_shape=[
            jax.ShapeDtypeStruct((tokens, PAIR), jnp.bfloat16),
            jax.ShapeDtypeStruct((blocks, 8, 2 * BQ), jnp.float32),
        ],
        scratch_shapes=[
            pltpu.VMEM((PLEN // BK, 2 * BQ, BK), jnp.float32),
            pltpu.VMEM((2 * BQ, BQ), jnp.float32),
            pltpu.VMEM((tokens, 2 * PAIR), jnp.bfloat16),
            pltpu.VMEM((2 * BQ, PAIR), jnp.float32),
            pltpu.VMEM((2 * BQ, 2 * PAIR), jnp.float32),
        ],
        compiler_params=params(60),
        cost_estimate=cost(8 * 2 * pairs * 256, 2 * tokens * 4 * PAIR, pairs),
        name="attend",
    )(cut, qkv)


def attend_back_kernel(
    bk, cut_ref, qkv_ref, o_ref, do_ref, lse_ref, out_ref, dk_ref, dv_ref, dq_ref
):
    i = pl.program_id(0)
    prompt_blocks = PLEN // BQ

    @pl.when(i == 0)
    def _():
        dk_ref[...] = jnp.zeros_like(dk_ref)
        dv_ref[...] = jnp.zeros_like(dv_ref)

    start = pl.multiple_of(i * BQ, BQ)
    queries = pair_rows(qkv_ref[pl.ds(start, BQ), 0:PAIR])
    grad = do_ref[pl.ds(start, BQ), :]
    grads = pair_rows(grad)
    mixed = jnp.transpose(
        grad.astype(jnp.float32) * o_ref[pl.ds(start, BQ), :].astype(jnp.float32)
    )
    center = jnp.concatenate(
        [
            jnp.sum(mixed[:HEAD], axis=0, keepdims=True),
            jnp.sum(mixed[HEAD:], axis=0, keepdims=True),
        ],
        axis=1,
    )
    log_total = lse_ref[0, 0:1, :]
    limit = jnp.where(i < prompt_blocks, start, cut_ref[jnp.maximum(i - prompt_blocks, 0)])
    full = limit // bk
    rest = limit - full * bk

    def block(first, count, keep, begin):
        at = pl.ds(pl.multiple_of(first, BQ), count)
        keys = qkv_ref[at, PAIR : 2 * PAIR]
        values = qkv_ref[at, 2 * PAIR : 3 * PAIR]
        probs = jnp.exp2(dot_nt(keys, queries) * LOG2E - log_total)
        if keep is not None:
            probs = jnp.where(keep(probs.shape), probs, 0.0)
        dv_ref[at, :] += dot(probs.astype(jnp.bfloat16), grads)
        grad_probs = dot_nt(values, grads)
        grad_scores = (probs * (grad_probs - center)).astype(jnp.bfloat16)
        dk_ref[at, :] += dot(grad_scores, queries)
        part = lax.dot_general(keys, grad_scores, TN, preferred_element_type=jnp.float32)
        dq_ref[...] = part if begin else dq_ref[...] + part

    def causal(shape):
        key = lax.broadcasted_iota(jnp.int32, shape, 0)
        query = lax.broadcasted_iota(jnp.int32, shape, 1) & (BQ - 1)
        return key <= query

    block(start, BQ, causal, True)

    def step(j, none):
        block(j * bk, bk, None, False)
        return none

    lax.fori_loop(0, full, step, 0)

    @pl.when(rest > 0)
    def _():
        block(full * bk, bk, lambda s: lax.broadcasted_iota(jnp.int32, s, 0) < rest, False)

    grad_query = pick_lanes(jnp.transpose(dq_ref[...])) * HEAD**-0.5
    out_ref[pl.ds(start, BQ), 0:PAIR] = grad_query.astype(out_ref.dtype)

    @pl.when(i == pl.num_programs(0) - 1)
    def _():
        out_ref[:, PAIR : 2 * PAIR] = dk_ref[...].astype(out_ref.dtype)
        out_ref[:, 2 * PAIR : 3 * PAIR] = dv_ref[...].astype(out_ref.dtype)


def attend_back(cut, qkv, att, grad_att, log_totals):
    tokens = qkv.shape[0]
    pairs = 2 * tokens * tokens // 4
    return pl.pallas_call(
        functools.partial(attend_back_kernel, BK_BACK),
        grid=(tokens // BQ,),
        in_specs=[
            pl.BlockSpec(memory_space=pltpu.SMEM),
            fixed((tokens, 3 * PAIR)),
            fixed((tokens, PAIR)),
            fixed((tokens, PAIR)),
            pl.BlockSpec((1, 8, 2 * BQ), lambda i: (i, 0, 0)),
        ],
        out_specs=fixed((tokens, 3 * PAIR)),
        out_shape=jax.ShapeDtypeStruct((tokens, 3 * PAIR), jnp.bfloat16),
        scratch_shapes=[
            pltpu.VMEM((tokens, PAIR), jnp.float32),
            pltpu.VMEM((tokens, PAIR), jnp.float32),
            pltpu.VMEM((PAIR, 2 * BQ), jnp.float32),
        ],
        compiler_params=params(60),
        cost_estimate=cost(10 * 2 * pairs * 256, 2 * tokens * 8 * PAIR, pairs),
        name="attend_back",
    )(cut, qkv, att, grad_att, log_totals)


def centered(values):
    center = values - jnp.mean(values, axis=-1, keepdims=True)
    spread = jnp.mean(center * center, axis=-1, keepdims=True)
    inverse = lax.rsqrt(spread + EPSILON)
    return center * inverse, inverse


def norm_back(grad, gain, unit, inverse):
    scaled = grad * gain
    mean_one = jnp.mean(scaled, axis=-1, keepdims=True)
    mean_two = jnp.mean(scaled * unit, axis=-1, keepdims=True)
    return (scaled - mean_one - unit * mean_two) * inverse


def out_block(w_ref, r, c, rows):
    width = w_ref.shape[3] // rows
    return jnp.concatenate(
        [w_ref[r, c, :, h * width : (h + 1) * width] for h in range(rows)], axis=0
    )


def out_weight_spec(weight):
    rows, cols, depth, width = weight.shape
    at = 4
    return pl.BlockSpec(
        (rows, cols, PAIR, width), lambda *_: (0, 0, at, 0), pipeline_mode=pl.Buffered(1)
    )


def middle_kernel(
    rows, cols, tok_ref, att_ref, w_ref, vec_ref, middle_ref, normed_ref, turned_ref
):
    parts = []
    for c in range(cols):
        parts.append(jnp.concatenate([att_ref[r, c] for r in range(rows)], axis=1))
    pieces = []
    for r in range(rows):
        total = dot(parts[0], out_block(w_ref, r, 0, rows))
        for c in range(1, cols):
            total = total + dot(parts[c], out_block(w_ref, r, c, rows))
        pieces.append(total)
    middle = tok_ref[...].astype(jnp.float32) + jnp.concatenate(pieces, axis=1) + vec_ref[0:1]
    middle_ref[...] = middle
    normed = (centered(middle)[0] * vec_ref[1:2] + vec_ref[2:3]).astype(jnp.bfloat16)
    normed_ref[...] = normed
    turned_ref[...] = jnp.transpose(normed)


def project_out(tokens, att, weight, vectors):
    rows, cols, span, _ = att.shape
    model = tokens.shape[1]
    tile = min(256, span)
    return pl.pallas_call(
        functools.partial(middle_kernel, rows, cols),
        grid=(span // tile,),
        in_specs=[
            pl.BlockSpec((tile, model), lambda i: (i, 0)),
            pl.BlockSpec((rows, cols, tile, PAIR), lambda i: (0, 0, i, 0)),
            out_weight_spec(weight),
            fixed(vectors.shape),
        ],
        out_specs=[
            pl.BlockSpec((tile, model), lambda i: (i, 0)),
            pl.BlockSpec((tile, model), lambda i: (i, 0)),
            pl.BlockSpec((model, tile), lambda i: (0, i)),
        ],
        out_shape=[
            jax.ShapeDtypeStruct((span, model), jnp.float32),
            jax.ShapeDtypeStruct((span, model), jnp.bfloat16),
            jax.ShapeDtypeStruct((model, span), jnp.bfloat16),
        ],
        compiler_params=params(60),
        cost_estimate=cost(2 * span * model * model, 2 * model * model + 12 * span * model),
        name="out_norm",
    )(tokens, att, weight, vectors)


def store_grads(rows, dps, turned_refs, cot_turned_ref, low_all, active_all, grad_ref):
    turned_all = jnp.concatenate([ref[...] for ref in turned_refs], axis=1)
    cut = turned_all.shape[0] // (rows * dps)
    for which, weight_grad in enumerate(
        (dot(turned_all, low_all), dot(cot_turned_ref[...], active_all))
    ):
        weight_grad = weight_grad.astype(jnp.bfloat16)
        for r in range(rows):
            for d in range(dps):
                at = (d * rows + r) * cut
                grad_ref[r, 0, d, which * cut : (which + 1) * cut] = weight_grad[at : at + cut]


def hidden_grad_kernel(rows, dps, groups, *refs):
    lows, actives = refs[groups + 1 : 2 * groups + 1], refs[2 * groups + 1 : -1]
    low_all = jnp.concatenate([ref[0] for ref in lows], axis=0)
    active_all = jnp.concatenate([ref[0] for ref in actives], axis=0)
    store_grads(rows, dps, refs[:groups], refs[groups], low_all, active_all, refs[-1])


def hidden_grad(turned, cot_turned, low, active, dps, rows):
    groups = len(low)
    cols, span, local = low[0].shape
    tokens = groups * span
    model = cot_turned.shape[0]
    tile = min(HIDDEN_TILE, local)
    cut = model // (rows * dps)
    piece = pl.BlockSpec((1, span, tile), lambda c, i: (c, 0, i))
    return pl.pallas_call(
        functools.partial(hidden_grad_kernel, rows, dps, groups),
        grid=(cols, local // tile),
        in_specs=[fixed(part.shape) for part in turned]
        + [fixed(cot_turned.shape)]
        + [piece] * (2 * groups),
        out_specs=pl.BlockSpec((rows, 1, dps, 2 * cut, tile), lambda c, i: (0, c, 0, 0, i)),
        out_shape=jax.ShapeDtypeStruct(
            (rows, cols, dps, 2 * cut + cut // 2, local), jnp.bfloat16
        ),
        compiler_params=params(60),
        cost_estimate=cost(4 * tokens * model * cols * local, 8 * model * cols * local),
        name="hidden_grad",
    )(*turned, cot_turned, *low, *active)


def hidden_kernel(rows, dps, groups, first, *refs):
    normed_refs, refs = refs[:groups], refs[groups:]
    if first:
        turned_refs, cot_turned_ref, refs = refs[:groups], refs[groups], refs[groups + 1 :]
    cot_refs, refs = refs[:groups], refs[groups:]
    w_ref, fc_bias_ref = refs[:2]
    if first:
        starts = refs[2 : groups + 2]
        out_accs = refs[groups + 2 : 2 * groups + 2]
        back_accs = refs[2 * groups + 2 : 3 * groups + 2]
        grad_ref, bias_ref, sems = refs[3 * groups + 2 :]
        ends = out_accs
    else:
        proj_bias_ref = refs[4]
        out_ref, back_acc, low_ref, active_ref, bias_ref, out_acc, sems = refs[5:]
        starts, ends = refs[2:4], (out_acc, back_acc)
        out_accs, back_accs = (out_acc,), (back_acc,)
    step = pl.program_id(0) * pl.num_programs(1) + pl.program_id(1)
    last = pl.num_programs(0) * pl.num_programs(1) - 1
    model = normed_refs[0].shape[1]
    tile = w_ref.shape[3]
    depth = model // rows
    copies = [
        pltpu.make_async_copy(start, end, sems.at[at])
        for at, (start, end) in enumerate(zip(starts, ends))
    ]

    @pl.when(step == 0)
    def _():
        for copy in copies:
            copy.start()
        if first:
            for back_acc in back_accs:
                back_acc[...] = jnp.zeros_like(back_acc)

    fc_weight = w_ref[:, 0, :depth].reshape(model, tile)
    proj_turned = w_ref[:, 0, depth:].reshape(model, tile)
    root = 0.7978845608028654
    actives, lows = [], []
    for g in range(groups):
        hidden = dot(normed_refs[g][...], fc_weight) + fc_bias_ref[0]
        square = hidden * hidden
        inner = jnp.tanh(hidden * (root + (root * 0.044715) * square))
        plus = 0.5 + 0.5 * inner
        actives.append((hidden * plus).astype(jnp.bfloat16))
        bend = 0.5 - 0.5 * inner * inner
        slope = plus + hidden * bend * (root + (3 * root * 0.044715) * square)
        grad_active = dot(cot_refs[g][...], proj_turned)
        lows.append((grad_active * slope).astype(jnp.bfloat16))
    bias_ref[0] = functools.reduce(
        jnp.add, [jnp.sum(low.astype(jnp.float32), axis=0, keepdims=True) for low in lows]
    )
    if first:
        store_grads(
            rows,
            dps,
            turned_refs,
            cot_turned_ref,
            jnp.concatenate(lows, axis=0),
            jnp.concatenate(actives, axis=0),
            grad_ref,
        )
    else:
        low_ref[0] = lows[0]
        active_ref[0] = actives[0]

    @pl.when(step == 0)
    def _():
        for copy in copies:
            copy.wait()

    for g in range(groups):
        out_accs[g][...] += dot_nt(actives[g], proj_turned)
        back_accs[g][...] += dot_nt(lows[g], fc_weight)
    if not first:

        @pl.when(step == last)
        def _():
            out_ref[...] = (out_acc[...] + proj_bias_ref[...]).astype(out_ref.dtype)


def feed_forward(first, normed, turned, cot, weight, fc_bias, rest, dps):
    groups = len(normed)
    span, model = normed[0].shape
    tokens = groups * span
    rows, cols, _, local = weight.shape
    depth = model // rows
    tile = min(HIDDEN_TILE, local)
    cut = model // (rows * dps)
    acc_shape = jax.ShapeDtypeStruct((span, model), jnp.float32)
    anywhere = pl.BlockSpec(memory_space=pl.ANY)
    whole = fixed((span, model))
    if first:
        rest_specs = [anywhere] * groups
        out_shape = [acc_shape] * (2 * groups)
        scratch = [pltpu.SemaphoreType.DMA((groups,))]
        grad_specs = [pl.BlockSpec((rows, 1, dps, 2 * cut, tile), lambda c, i: (0, c, 0, 0, i))]
        grad_shapes = [jax.ShapeDtypeStruct((rows, cols, dps, 2 * cut, local), jnp.bfloat16)]
    else:
        rest_specs = [anywhere, anywhere, fixed((1, model))]
        out_shape = [jax.ShapeDtypeStruct((span, model), jnp.bfloat16), acc_shape]
        scratch = [pltpu.VMEM((span, model), jnp.float32), pltpu.SemaphoreType.DMA((2,))]
        grad_specs = [pl.BlockSpec((1, span, tile), lambda c, i: (c, 0, i))] * 2
        grad_shapes = [jax.ShapeDtypeStruct((cols, span, local), jnp.bfloat16)] * 2
    products = 12 if first else 8
    return pl.pallas_call(
        functools.partial(hidden_kernel, rows, dps, groups, first),
        grid=(cols, local // tile),
        in_specs=[whole] * groups
        + [fixed(part.shape) for part in turned]
        + [whole] * groups
        + [
            pl.BlockSpec((rows, 1, 2 * depth, tile), lambda c, i: (0, c, 0, i)),
            pl.BlockSpec((1, 1, tile), lambda c, i: (c, 0, i)),
        ]
        + rest_specs,
        out_specs=[whole] * len(out_shape)
        + grad_specs
        + [pl.BlockSpec((1, 1, tile), lambda c, i: (c, 0, i))],
        out_shape=out_shape
        + grad_shapes
        + [jax.ShapeDtypeStruct((cols, 1, local), jnp.float32)],
        scratch_shapes=scratch,
        compiler_params=params(60),
        cost_estimate=cost(
            products * tokens * model * cols * local,
            8 * model * cols * local,
            tokens * cols * local,
        ),
        name="feed_forward_first" if first else "feed_forward_second",
    )(*normed, *turned, *cot, weight, fc_bias, *rest)


def middle_back_kernel(
    rows, cols, grad_ref, middle_ref, cot_ref, w_ref, vec_ref, dx_ref, turned_ref, datt_ref, sum_ref
):
    grad = grad_ref[...]
    unit, inverse = centered(middle_ref[...])
    total = cot_ref[...].astype(jnp.float32) + norm_back(grad, vec_ref[1:2], unit, inverse)
    dx_ref[...] = total
    low = total.astype(jnp.bfloat16)
    turned_ref[...] = jnp.transpose(low)
    depth = w_ref.shape[3] // rows
    for c in range(cols):
        part = dot_nt(low[:, :depth], out_block(w_ref, 0, c, rows))
        for r in range(1, rows):
            part = part + dot_nt(low[:, r * depth : (r + 1) * depth], out_block(w_ref, r, c, rows))
        part = part.astype(jnp.bfloat16)
        for r in range(rows):
            datt_ref[r, c] = part[:, r * PAIR : (r + 1) * PAIR]

    @pl.when(pl.program_id(0) == 0)
    def _():
        sum_ref[...] = jnp.zeros_like(sum_ref)

    sum_ref[0:1] += jnp.sum(grad * unit, axis=0, keepdims=True)
    sum_ref[1:2] += jnp.sum(grad, axis=0, keepdims=True)
    sum_ref[2:3] += jnp.sum(low.astype(jnp.float32), axis=0, keepdims=True)


def middle_back(grad, middle, cot, weight, vectors):
    span, model = middle.shape
    rows, cols = weight.shape[:2]
    tile = min(256, span)
    return pl.pallas_call(
        functools.partial(middle_back_kernel, rows, cols),
        grid=(span // tile,),
        in_specs=[
            pl.BlockSpec((tile, model), lambda i: (i, 0)),
            pl.BlockSpec((tile, model), lambda i: (i, 0)),
            pl.BlockSpec((tile, model), lambda i: (i, 0)),
            out_weight_spec(weight),
            fixed(vectors.shape),
        ],
        out_specs=[
            pl.BlockSpec((tile, model), lambda i: (i, 0)),
            pl.BlockSpec((model, tile), lambda i: (0, i)),
            pl.BlockSpec((rows, cols, tile, PAIR), lambda i: (0, 0, i, 0)),
            pl.BlockSpec((8, model), lambda i: (0, 0)),
        ],
        out_shape=[
            jax.ShapeDtypeStruct((span, model), jnp.float32),
            jax.ShapeDtypeStruct((model, span), jnp.bfloat16),
            jax.ShapeDtypeStruct((rows, cols, span, PAIR), jnp.bfloat16),
            jax.ShapeDtypeStruct((8, model), jnp.float32),
        ],
        compiler_params=params(60),
        cost_estimate=cost(2 * span * model * model, 2 * model * model + 18 * span * model),
        name="out_norm_back",
    )(grad, middle, cot, weight, vectors)


def out_grad_kernel(rows, dps, groups, *refs):
    out_ref = refs[-1]
    total = None
    for g in range(groups):
        att = jnp.concatenate([refs[groups + g][r, 0] for r in range(rows)], axis=1)
        part = dot(refs[g][...], att)
        total = part if total is None else total + part
    total = total.astype(jnp.bfloat16)
    half = out_ref.shape[3]
    for r in range(rows):
        for d in range(dps):
            at = (d * rows + r) * 2 * half
            out_ref[r, 0, d] = jnp.concatenate(
                [total[at : at + half], total[at + half : at + 2 * half]], axis=1
            )


def out_grad(turned, att, before, dps):
    groups = len(turned)
    model, span = turned[0].shape
    rows, cols = att[0].shape[:2]
    cut = model // (rows * dps)
    return pl.pallas_call(
        functools.partial(out_grad_kernel, rows, dps, groups),
        grid=(cols,),
        in_specs=[fixed((model, span))] * groups
        + [pl.BlockSpec((rows, 1, span, PAIR), lambda c: (0, c, 0, 0))] * groups
        + [pl.BlockSpec(memory_space=pl.ANY)],
        out_specs=pl.BlockSpec(
            (rows, 1, dps, cut // 2, 2 * rows * PAIR), lambda c: (0, c, 0, 4, 0)
        ),
        out_shape=jax.ShapeDtypeStruct(before.shape, before.dtype),
        compiler_params=params(60),
        cost_estimate=cost(2 * groups * span * model * model, 2 * model * model),
        input_output_aliases={2 * groups: 0},
        name="out_grad",
    )(*turned, *att, before)


def qkv_grad_kernel(final, dqkv_ref, x_ref, *refs):
    grad_ref, bias_ref, acc = refs[-3:]
    step = pl.program_id(0)
    grads = dqkv_ref[...]
    part = lax.dot_general(grads, x_ref[0], TN, preferred_element_type=jnp.float32)
    sums = jnp.sum(grads.astype(jnp.float32), axis=0, keepdims=True)

    @pl.when(step == 0)
    def _():
        acc[...] = refs[0][...] + part if final else part
        bias_ref[...] = jnp.zeros_like(bias_ref)

    @pl.when(step > 0)
    def _():
        acc[...] += part

    bias_ref[0:1] += sums

    @pl.when(step == pl.num_programs(0) - 1)
    def _():
        grad_ref[...] = jnp.transpose(acc[...]).astype(grad_ref.dtype) if final else acc[...]


def qkv_grad(dqkv, normed, before):
    tokens, width = dqkv.shape
    members, _, model = normed.shape
    final = len(before) == 1
    tile = tokens // members
    grad_type = (
        jax.ShapeDtypeStruct((model, width), jnp.bfloat16)
        if final
        else jax.ShapeDtypeStruct((width, model), jnp.float32)
    )
    return pl.pallas_call(
        functools.partial(qkv_grad_kernel, final),
        grid=(tokens // tile,),
        in_specs=[
            pl.BlockSpec((tile, width), lambda i: (i, 0)),
            pl.BlockSpec((1, tile, model), lambda i: (i, 0, 0)),
        ]
        + [fixed((width, model))] * len(before),
        out_specs=[fixed(grad_type.shape), fixed((8, width))],
        out_shape=[grad_type, jax.ShapeDtypeStruct((8, width), jnp.float32)],
        scratch_shapes=[pltpu.VMEM((width, model), jnp.float32)],
        compiler_params=params(60),
        cost_estimate=cost(2 * tokens * model * width, 2 * tokens * (model + width)),
        name="qkv_grad",
    )(dqkv, normed, *before)


def input_kernel(rows, dps, plane_ref, dqkv_ref, left_ref, right_ref, dx_ref, tok_ref, *refs):
    gain_ref = refs[0]
    out_ref, sum_ref, acc = refs[-3:]
    step = pl.program_id(0) * pl.num_programs(1) + pl.program_id(1)
    short = left_ref.shape[3] * 2 // 3
    grads = []
    for part in range(3):
        lanes = slice(part * PAIR, (part + 1) * PAIR)
        grads += [dqkv_ref[half, 0, :, lanes] for half in range(2)]
    pieces = []
    for r in range(rows):
        for d in range(dps):
            at = (plane_ref[0] - d) & (dps - 1)
            left, right = left_ref[at, r, 0], right_ref[at, r, 0]
            last = jnp.concatenate([left[short:], right[short:]], axis=0)
            pieces.append(jnp.concatenate([left[:short], right[:short], last], axis=1))
    weights = jnp.concatenate(pieces, axis=0)
    piece = dot_nt(jnp.concatenate(grads, axis=1), weights)

    @pl.when(step == 0)
    def _():
        acc[...] = piece

    @pl.when(step > 0)
    def _():
        acc[...] += piece

    @pl.when(step == pl.num_programs(0) * pl.num_programs(1) - 1)
    def _():
        grad = acc[...]
        unit, inverse = centered(tok_ref[0].astype(jnp.float32))
        out_ref[0] = dx_ref[...] + norm_back(grad, gain_ref[...], unit, inverse)
        sum_ref[0:1] = jnp.sum(grad * unit, axis=0, keepdims=True)
        sum_ref[1:2] = jnp.sum(grad, axis=0, keepdims=True)


def input_back(plane, dqkv, dx, tokens, weight, gain, before, g):
    dps, rows, cols, high, _ = weight.shape
    span, model = dx.shape
    return pl.pallas_call(
        functools.partial(input_kernel, rows, dps),
        grid=(rows // 2, cols),
        in_specs=[
            pl.BlockSpec(memory_space=pltpu.SMEM),
            pl.BlockSpec((2, 1, span, 3 * PAIR), lambda i, c: (i, c, 0, 0)),
            pl.BlockSpec((dps, rows, 1, high, 2 * PAIR), lambda i, c: (0, 0, c, 0, i)),
            pl.BlockSpec((dps, rows, 1, high, 2 * PAIR), lambda i, c: (0, 0, c, 0, rows // 2 + i)),
            fixed((span, model)),
            pl.BlockSpec((1, span, model), lambda i, c: (g, 0, 0), pipeline_mode=pl.Buffered(1)),
            fixed((1, model)),
        ]
        + [pl.BlockSpec(memory_space=pl.ANY)] * len(before),
        out_specs=[
            pl.BlockSpec((1, span, model), lambda i, c: (g, 0, 0), pipeline_mode=pl.Buffered(1)),
            fixed((8, model)),
        ],
        out_shape=[
            jax.ShapeDtypeStruct(tokens.shape, jnp.float32),
            jax.ShapeDtypeStruct((8, model), jnp.float32),
        ],
        scratch_shapes=[pltpu.VMEM((span, model), jnp.float32)],
        compiler_params=params(60),
        cost_estimate=cost(6 * span * model * model, 6 * model * model + 12 * span * model),
        input_output_aliases={7: 0} if before else {},
        name="input_back",
    )(plane, dqkv, weight, weight, dx, tokens, gain, *before)


def head_body(
    tokens,
    cotangent,
    branch,
    ln1_gain,
    ln1_bias,
    qkv_weight,
    qv_bias,
    out_weight,
    out_bias,
    ln2_gain,
    ln2_bias,
    fc_weight,
    fc_bias,
    proj_weight,
    proj_bias,
):
    groups, span, model = tokens.shape
    rows = lax.axis_size("row")
    cols = lax.axis_size("col")
    dps = lax.axis_size("dp")
    members = rows * cols
    count = groups * span
    head_cols = qv_bias.shape[1]
    hidden_cols = fc_bias.shape[0]

    def spread(shard):
        whole = lax.all_gather(shard, MESH_AXES, axis=0, tiled=False)
        return whole.reshape((rows, cols) + shard.shape)

    def swap(blocks):
        return lax.all_to_all(blocks, MESH_AXES, 0, 0, tiled=True)

    def collect_plane(partial):
        partial = partial.reshape((members,) + partial.shape[2:])
        partial = lax.psum_scatter(partial, MESH_AXES, scatter_dimension=0, tiled=True)
        return partial.reshape(partial.shape[1:])

    def exchange_dp(partial):
        me = lax.axis_index("dp")
        summed = lax.dynamic_index_in_dim(partial, me, 0, False).astype(jnp.float32)
        for shift in range(1, dps):
            piece = lax.dynamic_index_in_dim(partial, (me + shift) % dps, 0, False)
            pairs = [(i, (i + shift) % dps) for i in range(dps)]
            summed = summed + lax.ppermute(piece, "dp", pairs).astype(jnp.float32)
        return summed

    def collect_dp(partial):
        partial = lax.psum_scatter(partial, "dp", scatter_dimension=0, tiled=True)
        return partial[0].astype(jnp.float32)

    def total(values):
        for axis in ("row", "col", "dp"):
            size = lax.axis_size(axis)
            step = 1
            while step < size:
                pairs = [(i, i ^ step) for i in range(size)]
                values = values + lax.ppermute(values, axis, pairs)
                step *= 2
        return values

    half = hidden_cols // 2
    residual = tokens.astype(jnp.float32)
    normed = normalize(residual, ln1_gain, ln1_bias).astype(jnp.bfloat16)
    row = lax.axis_index("row")
    col = lax.axis_index("col")
    own = qkv_weight.reshape(-1, 3, rows, PAIR).transpose(2, 0, 1, 3)
    own = lax.all_to_all(own.reshape(rows, -1, 3 * PAIR), "row", 0, 0, tiled=True)
    own = own.reshape(model, 3 * PAIR)
    own_bias = lax.dynamic_slice_in_dim(qv_bias, row * PAIR, PAIR, 1)
    own_bias = jnp.concatenate([own_bias[0], jnp.zeros((PAIR,), jnp.float32), own_bias[1]])
    fc_full = lax.all_gather(fc_bias, "col", axis=0).reshape(cols, 1, hidden_cols)

    normed_all = [lax.all_gather(normed[0], MESH_AXES, axis=0, tiled=False)]
    cot_flat = cotangent.reshape(count, model)
    cot_turned = cot_flat.T
    toks = [tokens[g] for g in range(groups)]
    cots = [cotangent[g] for g in range(groups)]
    proj_bias_sum = jnp.sum(cot_flat.astype(jnp.float32), axis=0)
    plane = lax.axis_index("dp")
    short = qkv_weight.shape[0] // dps
    part = lax.dynamic_slice_in_dim(qkv_weight, plane * short, short, 0)
    last = jnp.concatenate([part[: short // 2, 2], part[short // 2 :, 2]], axis=1)
    part = jnp.concatenate([part[:, 0], part[:, 1]], axis=1)
    later = jnp.concatenate([normed[1], part, last], axis=0)
    shards = pack_weights(fc_weight, proj_weight, out_weight)
    normed_all[0], later, cot_turned, proj_bias_sum, shards, own, fc_full = (
        lax.optimization_barrier(
            (normed_all[0], later, cot_turned, proj_bias_sum, shards, own, fc_full)
        )
    )
    later = lax.all_gather(later, MESH_AXES, axis=0, tiled=False)
    normed_all.append(later)
    vectors = jnp.stack([out_bias, ln2_gain, ln2_bias] + [out_bias] * 5)
    gains = jnp.stack([ln2_gain] * 8)
    qkv, att, att_own, log_totals, middle, normed_two, turned_two = [], [], [], [], [], [], []
    w_first = spread(shards[0])
    w_second = spread(shards[1])
    def step_up(value):
        return lax.ppermute(value, "dp", [(i, i + 1) for i in range(dps - 1)])

    def step_down(value):
        return lax.ppermute(value, "dp", [(i + 1, i) for i in range(dps - 1)])

    for g in range(groups):
        qkv.append(project_qkv(normed_all[g], own, own_bias, span))
        mixed, totals = attend(branch[g], qkv[g])
        if g < groups - 1:
            mixed, normed_all[g + 1] = lax.optimization_barrier((mixed, normed_all[g + 1]))
        att_own.append(mixed)
        if g > 0:
            quarter = normed_all[1][:, span:].reshape(rows, cols, -1, model)
            ups, downs = [step_up(quarter)], [step_down(quarter)]
            mixed, att[g - 1], ups, downs = lax.optimization_barrier(
                (mixed, att[g - 1], ups, downs)
            )
            ups.append(step_up(ups[-1]))
            downs.append(step_down(downs[-1]))
        log_totals.append(totals)
        att.append(swap(mixed.reshape(members, span, PAIR)).reshape(rows, cols, span, PAIR))
    for g in range(groups):
        mid, low, turned = project_out(toks[g], att[g], w_first, vectors)
        middle.append(mid)
        normed_two.append(low)
        turned_two.append(turned)
    all_turned = turned_two + [cot_turned]
    normed_two[-1], ups, downs = lax.optimization_barrier((normed_two[-1], ups, downs))
    ups.append(step_up(ups[-1]))
    downs.append(step_down(downs[-1]))
    first_parts = feed_forward(
        True, normed_two, all_turned, cots, w_first, fc_full[:, :, :half], middle, dps
    )
    grad_first, fc_sum_first = first_parts[2 * groups :]
    plane_first = collect_plane(grad_first)
    block_out, low, active, fc_sums = [], [], [], []
    dx, dx_turned, grad_att, sums_two = [], [], [], []
    for g in range(groups):
        output_rows, grad_two, low_part, active_part, fc_part = feed_forward(
            False,
            [normed_two[g]],
            [],
            [cots[g]],
            w_second,
            fc_full[:, :, half:],
            (first_parts[g], first_parts[groups + g], proj_bias[None]),
            dps,
        )
        block_out.append(output_rows)
        low.append(low_part)
        active.append(active_part)
        fc_sums.append(fc_part)
        rows_grad, turned, datt, sums = middle_back(
            grad_two, middle[g], cots[g], w_first, gains
        )
        dx.append(rows_grad)
        dx_turned.append(turned)
        sums_two.append(sums)
        if g == 0:
            datt, normed_two[1] = lax.optimization_barrier((datt, normed_two[1]))
        grad_att.append(
            swap(datt.reshape(members, span, PAIR)).reshape(members * span, PAIR)
        )
    fc_sum_second = functools.reduce(jnp.add, fc_sums)
    grad_second = hidden_grad(turned_two, cot_turned, low, active, dps, rows)
    grad_att[0], grad_second = lax.optimization_barrier((grad_att[0], grad_second))
    plane_second = collect_plane(out_grad(dx_turned, att, grad_second, dps))
    rows_back, grads, bias_sums, before = [], [], [], []
    for g in range(groups):
        grad = attend_back(branch[g], qkv[g], att_own[g], grad_att[g], log_totals[g])
        if g == 0:
            grad, grad_att[1], plane_first = lax.optimization_barrier(
                (grad, grad_att[1], plane_first)
            )
        else:
            grad, rows_back[0], plane_first, grads[0], ups, downs = lax.optimization_barrier(
                (grad, rows_back[0], plane_first, grads[0], ups, downs)
            )
        rows_back.append(grad)
        grads.append(
            swap(grad.reshape(members, span, 3 * PAIR)).reshape(rows, cols, span, 3 * PAIR)
        )
    hidden_first = exchange_dp(plane_first)
    for g in range(groups):
        grad_qkv, bias_sum = qkv_grad(rows_back[g], normed_all[g], before)
        before = [grad_qkv]
        bias_sums.append(bias_sum[0])
    grad_qkv, hidden_first = lax.optimization_barrier((grad_qkv, hidden_first))
    grad_qkv = exchange_dp(grad_qkv.reshape(dps, rows, -1, 3 * PAIR))
    quarters = [quarter]
    for shift in range(1, dps):
        quarters.append(jnp.where(plane >= shift, ups[shift - 1], downs[dps - shift - 1]))
    w_qkv = jnp.stack(quarters)
    input_grads, sums_one = [], []
    for g in range(groups):
        rows_grad, sums = input_back(
            plane[None], grads[g], dx[g], tokens, w_qkv, ln1_gain[None], input_grads, g
        )
        input_grads = [rows_grad]
        sums_one.append(sums)
        if g == 0:
            input_grads, grad_qkv, plane_second = lax.optimization_barrier(
                (input_grads, grad_qkv, plane_second)
            )
            hidden_second = collect_dp(plane_second)
    sums_two = functools.reduce(jnp.add, sums_two)
    fc_sum = jnp.concatenate([fc_sum_first, fc_sum_second], axis=2).reshape(-1)
    sums_one = functools.reduce(jnp.add, sums_one)
    bias_sum = functools.reduce(jnp.add, bias_sums)
    qv_sum = jnp.zeros((2, model), jnp.float32)
    qv_sum = lax.dynamic_update_slice(
        qv_sum,
        jnp.stack([bias_sum[:PAIR], bias_sum[2 * PAIR :]]),
        (0, col * head_cols + row * PAIR),
    )
    small = (sums_two[2], sums_two[0], sums_two[1], fc_sum, proj_bias_sum)
    small += (sums_one[0], sums_one[1], qv_sum.reshape(-1))
    small = total(jnp.concatenate(small))
    grad_qkv = lax.all_to_all(grad_qkv, "row", 0, 0, tiled=True)
    d_qkv = grad_qkv.reshape(rows, -1, 3, PAIR).transpose(1, 2, 0, 3).reshape(-1, 3, head_cols)
    cut = model // (rows * dps)
    d_fc, d_proj = (
        jnp.concatenate([hidden_first[at : at + cut], hidden_second[at : at + cut]], axis=1)
        for at in (0, cut)
    )
    packed_out = hidden_second[2 * cut :]
    d_out = jnp.concatenate([packed_out[:, :head_cols], packed_out[:, head_cols:]], axis=0).T
    parts, at = [], 0
    for size in (model, model, model, hidden_cols * cols, model, model, model, 2 * model):
        parts.append(small[at : at + size])
        at += size
    s_out, s_gain_two, s_bias_two, s_fc, s_proj, s_gain_one, s_bias_one, s_qv = parts
    return (
        jnp.stack(block_out),
        input_grads[0],
        s_gain_one,
        s_bias_one,
        d_qkv,
        s_qv.reshape(2, model),
        d_out,
        s_out,
        s_gain_two,
        s_bias_two,
        d_fc,
        s_fc,
        d_proj.T,
        s_proj,
    )


def by_heads(mesh):
    rows, cols = mesh.shape["row"], mesh.shape["col"]

    def body(tokens, cotangent, branch, ln1_gain, ln1_bias, qkv_weight, *rest):
        width = qkv_weight.shape[2] * cols
        whole = tokens.shape[1] * rows * cols
        fits = width == rows * cols * PAIR and rows == 4 and mesh.shape["dp"] == 4 and tokens.shape[0] == 2
        fits = fits and qkv_weight.shape[0] * 4 == qkv_weight.shape[2] * cols
        fits = fits and rest[6].shape[0] == 4 * rows * PAIR
        fits = fits and all(size & (size - 1) == 0 for size in mesh.shape.values())
        fits = fits and whole == PLEN + CONTS * CLEN and tokens.shape[1] % BQ == 0
        chosen = head_body if fits else gathered_body
        return chosen(tokens, cotangent, branch, ln1_gain, ln1_bias, qkv_weight, *rest)

    return body


def solution(mesh):
    placed = (
        P("dp", ("row", "col"), None),
        P("dp", ("row", "col"), None),
        P("dp", None),
        P(),
        P(),
        P("row", None, "col"),
        P(None, "col"),
        P("col", "row"),
        P(),
        P(),
        P(),
        P("row", "col"),
        P("col"),
        P("col", "row"),
        P(),
    )
    return jax.shard_map(
        by_heads(mesh),
        mesh=mesh,
        in_specs=placed,
        out_specs=(
            P("dp", ("row", "col"), None),
            P("dp", ("row", "col"), None),
            P(),
            P(),
            P(("dp", "row"), None, "col"),
            P(),
            P("col", ("dp", "row")),
            P(),
            P(),
            P(),
            P(("dp", "row"), "col"),
            P(),
            P("col", ("dp", "row")),
            P(),
        ),
        check_vma=False,
    )
```

```python
import functools

import jax
import jax.numpy as jnp
from jax import lax
from jax.experimental import pallas as pl
from jax.experimental.pallas import tpu as pltpu
from jax.sharding import PartitionSpec as P

HEAD = 64
PLEN = 2048
CLEN = 256
CONTS = 8


EPSILON = 1e-05
MASKED_SCORE = -1e30
LOG2E = 1.4426950408889634
PAIR = 2 * HEAD
BQ = 256
BK = 512
BK_BACK = 512
HIDDEN_TILE = 512
NT = (((1,), (1,)), ((), ()))
TN = (((0,), (0,)), ((), ()))
MESH_AXES = ("row", "col")


def normalize(values, gain, shift):
    center = values - jnp.mean(values, axis=-1, keepdims=True)
    spread = jnp.mean(center * center, axis=-1, keepdims=True)
    return center * lax.rsqrt(spread + EPSILON) * gain + shift


def gelu_tanh(values):
    return jax.nn.gelu(values, approximate=True)


def allowed_keys(row_pos, col_pos, branch_cut):
    row_seg = jnp.where(row_pos >= PLEN, (row_pos - PLEN) // CLEN, -1)
    col_seg = jnp.where(col_pos >= PLEN, (col_pos - PLEN) // CLEN, -1)
    picked = (row_seg[:, None] == jnp.arange(CONTS, dtype=jnp.int32)[None, :]).astype(jnp.int32)
    row_cut = jnp.sum(picked * branch_cut[None, :], axis=1)
    causal = col_pos[None, :] <= row_pos[:, None]
    same_seq = col_seg[None, :] == row_seg[:, None]
    in_prefix = (
        (row_seg[:, None] >= 0) & (col_seg[None, :] < 0) & (col_pos[None, :] < row_cut[:, None])
    )
    return same_seq & causal | in_prefix


def add_trees(first, second):
    return jax.tree.map(lambda total, extra: total + extra, first, second)


def gathered_body(
    tokens,
    cotangent,
    branch,
    ln1_gain,
    ln1_bias,
    qkv_weight,
    qv_bias,
    out_weight,
    out_bias,
    ln2_gain,
    ln2_bias,
    fc_weight,
    fc_bias,
    proj_weight,
    proj_bias,
):
    scale = HEAD ** (-0.5)
    width = tokens.shape[2]
    local_rows = tokens.shape[1]
    head_cols = qv_bias.shape[1]
    head_count = head_cols // HEAD
    ff_local = fc_bias.shape[0]
    col_count = lax.axis_size("col")
    row_count = lax.axis_size("row")
    row_rows = local_rows * col_count
    group_rows = row_rows * row_count
    q_block = min(512, row_rows)
    block_count = row_rows // q_block
    row_base = lax.axis_index("row") * row_rows
    col_index = lax.axis_index("col")
    bias_three = jnp.stack([qv_bias[0], jnp.zeros_like(qv_bias[0]), qv_bias[1]])
    key_pos = jnp.arange(group_rows, dtype=jnp.int32)
    block_starts = jnp.arange(block_count, dtype=jnp.int32) * q_block

    def spread_rows(values):
        return lax.all_gather(values, "col", axis=0, tiled=True)

    def spread_grads(values):
        return lax.all_gather(values, "col", axis=0, tiled=True)

    def sum_branch(values):
        return lax.psum_scatter(values, "col", scatter_dimension=0, tiled=True)

    def sum_inputs(values):
        return lax.psum_scatter(values, "col", scatter_dimension=0, tiled=True)

    kept_weights = (
        lax.all_gather(qkv_weight, "row", axis=0, tiled=True),
        lax.all_gather(out_weight, "row", axis=1, tiled=True),
        lax.all_gather(fc_weight, "row", axis=0, tiled=True),
        lax.all_gather(proj_weight, "row", axis=1, tiled=True),
    )

    def block_scores(queries3, keys3, offset, branch_cut):
        q_part = lax.dynamic_slice_in_dim(queries3, offset, q_block, 0)
        row_pos = row_base + offset + jnp.arange(q_block, dtype=jnp.int32)
        allowed = allowed_keys(row_pos, key_pos, branch_cut)
        scores = (
            jnp.einsum("qhd,khd->hqk", q_part, keys3, preferred_element_type=jnp.float32) * scale
        )
        return (q_part, jnp.where(allowed[None], scores, MASKED_SCORE))

    def micro_step(carry, micro_item):
        grads_acc, small_acc = carry
        tok_rows, cot_rows, branch_cut = micro_item
        w_qkv, w_out, w_fc, w_proj = kept_weights
        residual = tok_rows.astype(jnp.float32)
        normed = normalize(residual, ln1_gain, ln1_bias).astype(jnp.bfloat16)
        normed_all = spread_rows(normed)
        projected = jnp.einsum("td,dsf->tsf", normed_all, w_qkv, preferred_element_type=jnp.float32)
        projected = (projected + bias_three[None]).astype(jnp.bfloat16)
        key_rows, value_rows = (
            lax.all_gather(projected[:, 1], "row", axis=0, tiled=True),
            lax.all_gather(projected[:, 2], "row", axis=0, tiled=True),
        )
        queries3 = projected[:, 0].reshape(row_rows, head_count, HEAD)
        keys3 = key_rows.reshape(group_rows, head_count, HEAD)
        values3 = value_rows.reshape(group_rows, head_count, HEAD)

        def attend(offset):
            q_part, scores = block_scores(queries3, keys3, offset, branch_cut)
            row_peak = jnp.max(scores, axis=-1, keepdims=True)
            exponent = jnp.exp(scores - row_peak)
            row_total = jnp.sum(exponent, axis=-1, keepdims=True)
            probs_low = (exponent / row_total).astype(jnp.bfloat16)
            mixed_rows = jnp.einsum(
                "hqk,khd->qhd", probs_low, values3, preferred_element_type=jnp.float32
            )
            return (mixed_rows, (row_peak + jnp.log(row_total))[..., 0])

        attended, log_totals = lax.map(attend, block_starts)
        attended = attended.reshape(row_rows, head_cols).astype(jnp.bfloat16)
        branch_part = jnp.dot(attended, w_out, preferred_element_type=jnp.float32)
        middle = residual + sum_branch(branch_part) + out_bias
        normed_two = normalize(middle, ln2_gain, ln2_bias).astype(jnp.bfloat16)
        normed_two_all = spread_rows(normed_two)
        hidden = jnp.dot(normed_two_all, w_fc, preferred_element_type=jnp.float32) + fc_bias
        active = gelu_tanh(hidden).astype(jnp.bfloat16)
        ffn_part = jnp.dot(active, w_proj, preferred_element_type=jnp.float32)
        output_rows = (middle + sum_branch(ffn_part) + proj_bias).astype(jnp.bfloat16)
        cot_all = spread_grads(cot_rows)
        grad_proj = jnp.einsum("tf,td->fd", active, cot_all, preferred_element_type=jnp.float32)
        grad_proj_bias = jnp.sum(cot_rows.astype(jnp.float32), axis=0)
        grad_active = jnp.einsum("td,fd->tf", cot_all, w_proj, preferred_element_type=jnp.float32)
        grad_hidden = jax.vjp(gelu_tanh, hidden)[1](grad_active)[0].astype(jnp.bfloat16)
        grad_fc = jnp.einsum(
            "td,tf->df", normed_two_all, grad_hidden, preferred_element_type=jnp.float32
        )
        grad_fc_bias = jnp.sum(grad_hidden.astype(jnp.float32), axis=0)
        grad_normed_two = sum_inputs(
            jnp.einsum("tf,df->td", grad_hidden, w_fc, preferred_element_type=jnp.float32)
        )
        back_middle, grad_gain_two, grad_bias_two = jax.vjp(normalize, middle, ln2_gain, ln2_bias)[
            1
        ](grad_normed_two)
        grad_middle = cot_rows.astype(jnp.float32) + back_middle
        grad_out_rows = grad_middle.astype(jnp.bfloat16)
        grad_out_all = spread_grads(grad_out_rows)
        grad_out = jnp.einsum(
            "tc,td->cd", attended, grad_out_all, preferred_element_type=jnp.float32
        )
        grad_out_bias = jnp.sum(grad_out_rows.astype(jnp.float32), axis=0)
        grad_att = jnp.einsum("td,cd->tc", grad_out_all, w_out, preferred_element_type=jnp.float32)
        grad_att = grad_att.astype(jnp.bfloat16).reshape(row_rows, head_count, HEAD)

        def attend_back(acc_pair, block_item):
            offset, log_total = block_item
            grad_keys_acc, grad_values_acc = acc_pair
            q_part, scores = block_scores(queries3, keys3, offset, branch_cut)
            probs = jnp.exp(scores - log_total[..., None])
            probs_low = probs.astype(jnp.bfloat16)
            grad_part = lax.dynamic_slice_in_dim(grad_att, offset, q_block, 0)
            grad_values_acc = grad_values_acc + jnp.einsum(
                "hqk,qhd->khd", probs_low, grad_part, preferred_element_type=jnp.float32
            )
            grad_probs = jnp.einsum(
                "qhd,khd->hqk", grad_part, values3, preferred_element_type=jnp.float32
            )
            center = jnp.sum(grad_probs * probs, axis=-1, keepdims=True)
            grad_scores = (probs * (grad_probs - center)).astype(jnp.bfloat16)
            grad_keys_acc = (
                grad_keys_acc
                + jnp.einsum(
                    "hqk,qhd->khd", grad_scores, q_part, preferred_element_type=jnp.float32
                )
                * scale
            )
            grad_query = (
                jnp.einsum("hqk,khd->qhd", grad_scores, keys3, preferred_element_type=jnp.float32)
                * scale
            )
            return ((grad_keys_acc, grad_values_acc), grad_query)

        empty_keys = jnp.zeros((group_rows, head_count, HEAD), jnp.float32)
        (grad_keys, grad_values), grad_queries = lax.scan(
            attend_back, (empty_keys, empty_keys), (block_starts, log_totals)
        )
        own_keys, own_values = (
            lax.psum_scatter(
                grad_keys.reshape(group_rows, head_cols).astype(jnp.bfloat16),
                "row",
                scatter_dimension=0,
                tiled=True,
            ).astype(jnp.float32),
            lax.psum_scatter(
                grad_values.reshape(group_rows, head_cols).astype(jnp.bfloat16),
                "row",
                scatter_dimension=0,
                tiled=True,
            ).astype(jnp.float32),
        )
        grad_projected = jnp.stack(
            [grad_queries.reshape(row_rows, head_cols), own_keys, own_values], axis=1
        ).astype(jnp.bfloat16)
        grad_qkv = jnp.einsum(
            "td,tsf->dsf", normed_all, grad_projected, preferred_element_type=jnp.float32
        )
        grad_qkv_bias = jnp.sum(grad_projected.astype(jnp.float32), axis=0)
        grad_normed = sum_inputs(
            jnp.einsum("tsf,dsf->td", grad_projected, w_qkv, preferred_element_type=jnp.float32)
        )
        back_input, grad_gain_one, grad_bias_one = jax.vjp(normalize, residual, ln1_gain, ln1_bias)[
            1
        ](grad_normed)
        input_rows = grad_middle + back_input
        weight_terms = (grad_qkv, grad_out, grad_fc, grad_proj)
        small_terms = (
            grad_gain_one,
            grad_bias_one,
            grad_qkv_bias,
            grad_out_bias,
            grad_gain_two,
            grad_bias_two,
            grad_fc_bias,
            grad_proj_bias,
        )
        return (
            (add_trees(grads_acc, weight_terms), add_trees(small_acc, small_terms)),
            (output_rows, input_rows),
        )

    grads_init = (
        jnp.zeros((width, 3, head_cols), jnp.float32),
        jnp.zeros((head_cols, width), jnp.float32),
        jnp.zeros((width, ff_local), jnp.float32),
        jnp.zeros((ff_local, width), jnp.float32),
    )
    vector_zero = jnp.zeros((width,), jnp.float32)
    small_init = (
        vector_zero,
        vector_zero,
        jnp.zeros((3, head_cols), jnp.float32),
        vector_zero,
        vector_zero,
        vector_zero,
        jnp.zeros((ff_local,), jnp.float32),
        vector_zero,
    )
    (grads_acc, small_acc), (block_out, input_grad) = lax.scan(
        micro_step, (grads_init, small_init), (tokens, cotangent, branch)
    )
    (
        gain_one,
        bias_one,
        qkv_bias_acc,
        out_bias_acc,
        gain_two,
        bias_two,
        fc_bias_acc,
        proj_bias_acc,
    ) = small_acc
    qv_full = lax.dynamic_update_slice(
        jnp.zeros((2, width), jnp.float32),
        jnp.stack([qkv_bias_acc[0], qkv_bias_acc[2]]),
        (jnp.int32(0), col_index * head_cols),
    )
    fc_full = lax.dynamic_update_slice(
        jnp.zeros((ff_local * col_count,), jnp.float32), fc_bias_acc, (col_index * ff_local,)
    )
    summed = lax.psum(
        (gain_one, bias_one, qv_full, out_bias_acc, gain_two, bias_two, fc_full, proj_bias_acc),
        ("dp", "row", "col"),
    )
    return (
        block_out,
        input_grad,
        summed[0],
        summed[1],
        lax.psum_scatter(
            grads_acc[0].astype(jnp.bfloat16), ("dp", "row"), scatter_dimension=0, tiled=True
        ).astype(jnp.float32),
        summed[2],
        lax.psum_scatter(
            grads_acc[1].astype(jnp.bfloat16), ("dp", "row"), scatter_dimension=1, tiled=True
        ).astype(jnp.float32),
        summed[3],
        summed[4],
        summed[5],
        lax.psum_scatter(
            grads_acc[2].astype(jnp.bfloat16), ("dp", "row"), scatter_dimension=0, tiled=True
        ).astype(jnp.float32),
        summed[6],
        lax.psum_scatter(
            grads_acc[3].astype(jnp.bfloat16), ("dp", "row"), scatter_dimension=1, tiled=True
        ).astype(jnp.float32),
        summed[7],
    )


def dot(left, right):
    return jnp.dot(left, right, preferred_element_type=jnp.float32)


def dot_nt(left, right):
    return lax.dot_general(left, right, NT, preferred_element_type=jnp.float32)


def cost(flops, moved, exps=0):
    return pl.CostEstimate(flops=int(flops), bytes_accessed=int(moved), transcendentals=int(exps))


def params(mebibytes):
    return pltpu.CompilerParams(vmem_limit_bytes=mebibytes * 2**20)


def fixed(shape):
    return pl.BlockSpec(shape, lambda *_: (0,) * len(shape), pipeline_mode=pl.Buffered(1))


def pair_rows(rows):
    low = lax.broadcasted_iota(jnp.int32, rows.shape, 1) < HEAD
    zero = jnp.zeros_like(rows)
    return jnp.concatenate([jnp.where(low, rows, zero), jnp.where(low, zero, rows)], axis=0)


def pick_lanes(stacked):
    half = stacked.shape[0] // 2
    low = lax.broadcasted_iota(jnp.int32, (half, stacked.shape[1]), 1) < HEAD
    return jnp.where(low, stacked[:half], stacked[half:])


def pack_kernel(fc_ref, proj_ref, out_ref, first_ref, second_ref):
    depth, hidden = fc_ref.shape
    half = hidden // 2
    turned = jnp.transpose(proj_ref[...])
    for at, ref in ((0, first_ref), (half, second_ref)):
        ref[:depth] = fc_ref[:, at : at + half]
        ref[depth : 2 * depth] = turned[:, at : at + half]
    for h in range(out_ref.shape[0] // PAIR):
        first_ref[2 * depth :, h * depth : (h + 1) * depth] = out_ref[h * PAIR : (h + 1) * PAIR]


def pack_weights(fc_weight, proj_weight, out_weight):
    depth, hidden = fc_weight.shape
    shapes = [(2 * depth + PAIR, hidden // 2), (2 * depth, hidden // 2)]
    return pl.pallas_call(
        pack_kernel,
        in_specs=[pl.BlockSpec(memory_space=pltpu.VMEM)] * 3,
        out_specs=[pl.BlockSpec(memory_space=pltpu.VMEM)] * 2,
        out_shape=[jax.ShapeDtypeStruct(shape, jnp.bfloat16) for shape in shapes],
        compiler_params=params(60),
        cost_estimate=cost(1, 8 * depth * hidden),
        name="pack_weights",
    )(fc_weight, proj_weight, out_weight)


def qkv_kernel(x_ref, w_ref, vec_ref, out_ref):
    rows = x_ref[...].reshape(out_ref.shape[0], x_ref.shape[2])
    values = (dot(rows, w_ref[...]) + vec_ref[0:1]) * vec_ref[1:2]
    out_ref[...] = values.astype(out_ref.dtype)


def project_qkv(normed, weight, bias, span):
    members, _, model = normed.shape
    width = weight.shape[1]
    tokens = members * span
    vectors = jnp.stack([bias, jnp.where(jnp.arange(width) < PAIR, HEAD**-0.5, 1.0)])
    return pl.pallas_call(
        qkv_kernel,
        grid=(members // 2,),
        in_specs=[
            pl.BlockSpec((2, span, model), lambda i: (i, 0, 0)),
            fixed((model, width)),
            fixed((2, width)),
        ],
        out_specs=pl.BlockSpec((2 * span, width), lambda i: (i, 0)),
        out_shape=jax.ShapeDtypeStruct((tokens, width), jnp.bfloat16),
        compiler_params=params(60),
        cost_estimate=cost(2 * tokens * model * width, 2 * tokens * (model + width)),
        name="qkv",
    )(normed, weight, vectors)


def attend_kernel(
    bk, cut_ref, qkv_ref, o_ref, lse_ref, s_ref, own_ref, value_ref, peak_ref, acc_ref
):
    i = pl.program_id(0)
    prompt_blocks = PLEN // BQ

    @pl.when(i == 0)
    def _():
        value_ref[:, :PAIR] = qkv_ref[:, 2 * PAIR : 3 * PAIR]
        value_ref[:, PAIR:] = jnp.ones((value_ref.shape[0], PAIR), value_ref.dtype)

    start = pl.multiple_of(i * BQ, BQ)
    queries = pair_rows(qkv_ref[pl.ds(start, BQ), 0:PAIR])
    limit = jnp.where(i < prompt_blocks, start, cut_ref[jnp.maximum(i - prompt_blocks, 0)])
    full = limit // bk
    rest = limit - full * bk

    def scores(first, count):
        keys = qkv_ref[pl.ds(pl.multiple_of(first, BQ), count), PAIR : 2 * PAIR]
        return dot_nt(queries, keys) * LOG2E

    def lane_peak(values):
        return functools.reduce(
            jnp.maximum, [values[:, at : at + 128] for at in range(0, values.shape[1], 128)]
        )

    own = scores(start, BQ)
    row = lax.broadcasted_iota(jnp.int32, own.shape, 0) & (BQ - 1)
    own = jnp.where(lax.broadcasted_iota(jnp.int32, own.shape, 1) <= row, own, MASKED_SCORE)
    own_ref[...] = own
    peak_ref[...] = lane_peak(own)

    def score_step(j, none):
        values = scores(j * bk, bk)
        s_ref[j] = values
        peak_ref[...] = jnp.maximum(peak_ref[...], lane_peak(values))
        return none

    lax.fori_loop(0, full, score_step, 0)

    @pl.when(rest > 0)
    def _():
        values = scores(full * bk, bk)
        seen = lax.broadcasted_iota(jnp.int32, values.shape, 1) < rest
        values = jnp.where(seen, values, MASKED_SCORE)
        s_ref[full] = values
        peak_ref[...] = jnp.maximum(peak_ref[...], lane_peak(values))

    peak = jnp.max(peak_ref[...], axis=1, keepdims=True)
    probs = jnp.exp2(own_ref[...] - peak).astype(jnp.bfloat16)
    acc_ref[...] = dot(probs, value_ref[pl.ds(start, BQ), :])

    def value_step(j, none):
        probs = jnp.exp2(s_ref[j] - peak).astype(jnp.bfloat16)
        acc_ref[...] += dot(probs, value_ref[pl.ds(pl.multiple_of(j * bk, bk), bk), :])
        return none

    lax.fori_loop(0, full + jnp.where(rest > 0, 1, 0), value_step, 0)
    total = acc_ref[:, PAIR:]
    o_ref[...] = pick_lanes(acc_ref[:, :PAIR] / total).astype(o_ref.dtype)
    lse_ref[0] = jnp.transpose(peak + jnp.log2(total))[:8]


def attend(cut, qkv):
    tokens = qkv.shape[0]
    blocks = tokens // BQ
    pairs = 2 * tokens * tokens // 4
    return pl.pallas_call(
        functools.partial(attend_kernel, BK),
        grid=(blocks,),
        in_specs=[pl.BlockSpec(memory_space=pltpu.SMEM), fixed((tokens, 3 * PAIR))],
        out_specs=[
            pl.BlockSpec((BQ, PAIR), lambda i: (i, 0)),
            pl.BlockSpec((1, 8, 2 * BQ), lambda i: (i, 0, 0)),
        ],
        out_shape=[
            jax.ShapeDtypeStruct((tokens, PAIR), jnp.bfloat16),
            jax.ShapeDtypeStruct((blocks, 8, 2 * BQ), jnp.float32),
        ],
        scratch_shapes=[
            pltpu.VMEM((PLEN // BK, 2 * BQ, BK), jnp.float32),
            pltpu.VMEM((2 * BQ, BQ), jnp.float32),
            pltpu.VMEM((tokens, 2 * PAIR), jnp.bfloat16),
            pltpu.VMEM((2 * BQ, PAIR), jnp.float32),
            pltpu.VMEM((2 * BQ, 2 * PAIR), jnp.float32),
        ],
        compiler_params=params(60),
        cost_estimate=cost(8 * 2 * pairs * 256, 2 * tokens * 4 * PAIR, pairs),
        name="attend",
    )(cut, qkv)


def attend_back_kernel(
    bk, cut_ref, qkv_ref, o_ref, do_ref, lse_ref, out_ref, dk_ref, dv_ref, dq_ref
):
    i = pl.program_id(0)
    prompt_blocks = PLEN // BQ

    @pl.when(i == 0)
    def _():
        dk_ref[...] = jnp.zeros_like(dk_ref)
        dv_ref[...] = jnp.zeros_like(dv_ref)

    start = pl.multiple_of(i * BQ, BQ)
    queries = pair_rows(qkv_ref[pl.ds(start, BQ), 0:PAIR])
    grad = do_ref[pl.ds(start, BQ), :]
    grads = pair_rows(grad)
    mixed = jnp.transpose(
        grad.astype(jnp.float32) * o_ref[pl.ds(start, BQ), :].astype(jnp.float32)
    )
    center = jnp.concatenate(
        [
            jnp.sum(mixed[:HEAD], axis=0, keepdims=True),
            jnp.sum(mixed[HEAD:], axis=0, keepdims=True),
        ],
        axis=1,
    )
    log_total = lse_ref[0, 0:1, :]
    limit = jnp.where(i < prompt_blocks, start, cut_ref[jnp.maximum(i - prompt_blocks, 0)])
    full = limit // bk
    rest = limit - full * bk

    def block(first, count, keep, begin):
        at = pl.ds(pl.multiple_of(first, BQ), count)
        keys = qkv_ref[at, PAIR : 2 * PAIR]
        values = qkv_ref[at, 2 * PAIR : 3 * PAIR]
        probs = jnp.exp2(dot_nt(keys, queries) * LOG2E - log_total)
        if keep is not None:
            probs = jnp.where(keep(probs.shape), probs, 0.0)
        dv_ref[at, :] += dot(probs.astype(jnp.bfloat16), grads)
        grad_probs = dot_nt(values, grads)
        grad_scores = (probs * (grad_probs - center)).astype(jnp.bfloat16)
        dk_ref[at, :] += dot(grad_scores, queries)
        part = lax.dot_general(keys, grad_scores, TN, preferred_element_type=jnp.float32)
        dq_ref[...] = part if begin else dq_ref[...] + part

    def causal(shape):
        key = lax.broadcasted_iota(jnp.int32, shape, 0)
        query = lax.broadcasted_iota(jnp.int32, shape, 1) & (BQ - 1)
        return key <= query

    block(start, BQ, causal, True)

    def step(j, none):
        block(j * bk, bk, None, False)
        return none

    lax.fori_loop(0, full, step, 0)

    @pl.when(rest > 0)
    def _():
        block(full * bk, bk, lambda s: lax.broadcasted_iota(jnp.int32, s, 0) < rest, False)

    grad_query = pick_lanes(jnp.transpose(dq_ref[...])) * HEAD**-0.5
    out_ref[pl.ds(start, BQ), 0:PAIR] = grad_query.astype(out_ref.dtype)

    @pl.when(i == pl.num_programs(0) - 1)
    def _():
        out_ref[:, PAIR : 2 * PAIR] = dk_ref[...].astype(out_ref.dtype)
        out_ref[:, 2 * PAIR : 3 * PAIR] = dv_ref[...].astype(out_ref.dtype)


def attend_back(cut, qkv, att, grad_att, log_totals):
    tokens = qkv.shape[0]
    pairs = 2 * tokens * tokens // 4
    return pl.pallas_call(
        functools.partial(attend_back_kernel, BK_BACK),
        grid=(tokens // BQ,),
        in_specs=[
            pl.BlockSpec(memory_space=pltpu.SMEM),
            fixed((tokens, 3 * PAIR)),
            fixed((tokens, PAIR)),
            fixed((tokens, PAIR)),
            pl.BlockSpec((1, 8, 2 * BQ), lambda i: (i, 0, 0)),
        ],
        out_specs=fixed((tokens, 3 * PAIR)),
        out_shape=jax.ShapeDtypeStruct((tokens, 3 * PAIR), jnp.bfloat16),
        scratch_shapes=[
            pltpu.VMEM((tokens, PAIR), jnp.float32),
            pltpu.VMEM((tokens, PAIR), jnp.float32),
            pltpu.VMEM((PAIR, 2 * BQ), jnp.float32),
        ],
        compiler_params=params(60),
        cost_estimate=cost(10 * 2 * pairs * 256, 2 * tokens * 8 * PAIR, pairs),
        name="attend_back",
    )(cut, qkv, att, grad_att, log_totals)


def centered(values):
    center = values - jnp.mean(values, axis=-1, keepdims=True)
    spread = jnp.mean(center * center, axis=-1, keepdims=True)
    inverse = lax.rsqrt(spread + EPSILON)
    return center * inverse, inverse


def norm_back(grad, gain, unit, inverse):
    scaled = grad * gain
    mean_one = jnp.mean(scaled, axis=-1, keepdims=True)
    mean_two = jnp.mean(scaled * unit, axis=-1, keepdims=True)
    return (scaled - mean_one - unit * mean_two) * inverse


def out_block(w_ref, r, c, rows):
    width = w_ref.shape[3] // rows
    return jnp.concatenate(
        [w_ref[r, c, :, h * width : (h + 1) * width] for h in range(rows)], axis=0
    )


def out_weight_spec(weight):
    rows, cols, depth, width = weight.shape
    at = 4
    return pl.BlockSpec(
        (rows, cols, PAIR, width), lambda *_: (0, 0, at, 0), pipeline_mode=pl.Buffered(1)
    )


def middle_kernel(
    rows, cols, tok_ref, att_ref, w_ref, vec_ref, middle_ref, normed_ref, turned_ref
):
    parts = []
    for c in range(cols):
        parts.append(jnp.concatenate([att_ref[r, c] for r in range(rows)], axis=1))
    pieces = []
    for r in range(rows):
        total = dot(parts[0], out_block(w_ref, r, 0, rows))
        for c in range(1, cols):
            total = total + dot(parts[c], out_block(w_ref, r, c, rows))
        pieces.append(total)
    middle = tok_ref[...].astype(jnp.float32) + jnp.concatenate(pieces, axis=1) + vec_ref[0:1]
    middle_ref[...] = middle
    normed = (centered(middle)[0] * vec_ref[1:2] + vec_ref[2:3]).astype(jnp.bfloat16)
    normed_ref[...] = normed
    turned_ref[...] = jnp.transpose(normed)


def project_out(tokens, att, weight, vectors):
    rows, cols, span, _ = att.shape
    model = tokens.shape[1]
    tile = min(256, span)
    return pl.pallas_call(
        functools.partial(middle_kernel, rows, cols),
        grid=(span // tile,),
        in_specs=[
            pl.BlockSpec((tile, model), lambda i: (i, 0)),
            pl.BlockSpec((rows, cols, tile, PAIR), lambda i: (0, 0, i, 0)),
            out_weight_spec(weight),
            fixed(vectors.shape),
        ],
        out_specs=[
            pl.BlockSpec((tile, model), lambda i: (i, 0)),
            pl.BlockSpec((tile, model), lambda i: (i, 0)),
            pl.BlockSpec((model, tile), lambda i: (0, i)),
        ],
        out_shape=[
            jax.ShapeDtypeStruct((span, model), jnp.float32),
            jax.ShapeDtypeStruct((span, model), jnp.bfloat16),
            jax.ShapeDtypeStruct((model, span), jnp.bfloat16),
        ],
        compiler_params=params(60),
        cost_estimate=cost(2 * span * model * model, 2 * model * model + 12 * span * model),
        name="out_norm",
    )(tokens, att, weight, vectors)


def store_grads(rows, dps, turned_refs, cot_turned_ref, low_all, active_all, grad_ref):
    turned_all = jnp.concatenate([ref[...] for ref in turned_refs], axis=1)
    cut = turned_all.shape[0] // (rows * dps)
    for which, weight_grad in enumerate(
        (dot(turned_all, low_all), dot(cot_turned_ref[...], active_all))
    ):
        weight_grad = weight_grad.astype(jnp.bfloat16)
        for r in range(rows):
            for d in range(dps):
                at = (d * rows + r) * cut
                grad_ref[r, 0, d, which * cut : (which + 1) * cut] = weight_grad[at : at + cut]


def hidden_grad_kernel(rows, dps, groups, *refs):
    lows, actives = refs[groups + 1 : 2 * groups + 1], refs[2 * groups + 1 : -1]
    low_all = jnp.concatenate([ref[0] for ref in lows], axis=0)
    active_all = jnp.concatenate([ref[0] for ref in actives], axis=0)
    store_grads(rows, dps, refs[:groups], refs[groups], low_all, active_all, refs[-1])


def hidden_grad(turned, cot_turned, low, active, dps, rows):
    groups = len(low)
    cols, span, local = low[0].shape
    tokens = groups * span
    model = cot_turned.shape[0]
    tile = min(HIDDEN_TILE, local)
    cut = model // (rows * dps)
    piece = pl.BlockSpec((1, span, tile), lambda c, i: (c, 0, i))
    return pl.pallas_call(
        functools.partial(hidden_grad_kernel, rows, dps, groups),
        grid=(cols, local // tile),
        in_specs=[fixed(part.shape) for part in turned]
        + [fixed(cot_turned.shape)]
        + [piece] * (2 * groups),
        out_specs=pl.BlockSpec((rows, 1, dps, 2 * cut, tile), lambda c, i: (0, c, 0, 0, i)),
        out_shape=jax.ShapeDtypeStruct(
            (rows, cols, dps, 2 * cut + cut // 2, local), jnp.bfloat16
        ),
        compiler_params=params(60),
        cost_estimate=cost(4 * tokens * model * cols * local, 8 * model * cols * local),
        name="hidden_grad",
    )(*turned, cot_turned, *low, *active)


def hidden_kernel(rows, dps, groups, first, *refs):
    normed_refs, refs = refs[:groups], refs[groups:]
    if first:
        turned_refs, cot_turned_ref, refs = refs[:groups], refs[groups], refs[groups + 1 :]
    cot_refs, refs = refs[:groups], refs[groups:]
    w_ref, fc_bias_ref = refs[:2]
    if first:
        starts = refs[2 : groups + 2]
        out_accs = refs[groups + 2 : 2 * groups + 2]
        back_accs = refs[2 * groups + 2 : 3 * groups + 2]
        grad_ref, bias_ref, sems = refs[3 * groups + 2 :]
        ends = out_accs
    else:
        proj_bias_ref = refs[4]
        out_ref, back_acc, low_ref, active_ref, bias_ref, out_acc, sems = refs[5:]
        starts, ends = refs[2:4], (out_acc, back_acc)
        out_accs, back_accs = (out_acc,), (back_acc,)
    step = pl.program_id(0) * pl.num_programs(1) + pl.program_id(1)
    last = pl.num_programs(0) * pl.num_programs(1) - 1
    model = normed_refs[0].shape[1]
    tile = w_ref.shape[3]
    depth = model // rows
    copies = [
        pltpu.make_async_copy(start, end, sems.at[at])
        for at, (start, end) in enumerate(zip(starts, ends))
    ]

    @pl.when(step == 0)
    def _():
        for copy in copies:
            copy.start()
        if first:
            for back_acc in back_accs:
                back_acc[...] = jnp.zeros_like(back_acc)

    fc_weight = w_ref[:, 0, :depth].reshape(model, tile)
    proj_turned = w_ref[:, 0, depth:].reshape(model, tile)
    root = 0.7978845608028654
    actives, lows = [], []
    for g in range(groups):
        hidden = dot(normed_refs[g][...], fc_weight) + fc_bias_ref[0]
        square = hidden * hidden
        inner = jnp.tanh(hidden * (root + (root * 0.044715) * square))
        plus = 0.5 + 0.5 * inner
        actives.append((hidden * plus).astype(jnp.bfloat16))
        bend = 0.5 - 0.5 * inner * inner
        slope = plus + hidden * bend * (root + (3 * root * 0.044715) * square)
        grad_active = dot(cot_refs[g][...], proj_turned)
        lows.append((grad_active * slope).astype(jnp.bfloat16))
    bias_ref[0] = functools.reduce(
        jnp.add, [jnp.sum(low.astype(jnp.float32), axis=0, keepdims=True) for low in lows]
    )
    if first:
        store_grads(
            rows,
            dps,
            turned_refs,
            cot_turned_ref,
            jnp.concatenate(lows, axis=0),
            jnp.concatenate(actives, axis=0),
            grad_ref,
        )
    else:
        low_ref[0] = lows[0]
        active_ref[0] = actives[0]

    @pl.when(step == 0)
    def _():
        for copy in copies:
            copy.wait()

    for g in range(groups):
        out_accs[g][...] += dot_nt(actives[g], proj_turned)
        back_accs[g][...] += dot_nt(lows[g], fc_weight)
    if not first:

        @pl.when(step == last)
        def _():
            out_ref[...] = (out_acc[...] + proj_bias_ref[...]).astype(out_ref.dtype)


def feed_forward(first, normed, turned, cot, weight, fc_bias, rest, dps):
    groups = len(normed)
    span, model = normed[0].shape
    tokens = groups * span
    rows, cols, _, local = weight.shape
    depth = model // rows
    tile = min(HIDDEN_TILE, local)
    cut = model // (rows * dps)
    acc_shape = jax.ShapeDtypeStruct((span, model), jnp.float32)
    anywhere = pl.BlockSpec(memory_space=pl.ANY)
    whole = fixed((span, model))
    if first:
        rest_specs = [anywhere] * groups
        out_shape = [acc_shape] * (2 * groups)
        scratch = [pltpu.SemaphoreType.DMA((groups,))]
        grad_specs = [pl.BlockSpec((rows, 1, dps, 2 * cut, tile), lambda c, i: (0, c, 0, 0, i))]
        grad_shapes = [jax.ShapeDtypeStruct((rows, cols, dps, 2 * cut, local), jnp.bfloat16)]
    else:
        rest_specs = [anywhere, anywhere, fixed((1, model))]
        out_shape = [jax.ShapeDtypeStruct((span, model), jnp.bfloat16), acc_shape]
        scratch = [pltpu.VMEM((span, model), jnp.float32), pltpu.SemaphoreType.DMA((2,))]
        grad_specs = [pl.BlockSpec((1, span, tile), lambda c, i: (c, 0, i))] * 2
        grad_shapes = [jax.ShapeDtypeStruct((cols, span, local), jnp.bfloat16)] * 2
    products = 12 if first else 8
    return pl.pallas_call(
        functools.partial(hidden_kernel, rows, dps, groups, first),
        grid=(cols, local // tile),
        in_specs=[whole] * groups
        + [fixed(part.shape) for part in turned]
        + [whole] * groups
        + [
            pl.BlockSpec((rows, 1, 2 * depth, tile), lambda c, i: (0, c, 0, i)),
            pl.BlockSpec((1, 1, tile), lambda c, i: (c, 0, i)),
        ]
        + rest_specs,
        out_specs=[whole] * len(out_shape)
        + grad_specs
        + [pl.BlockSpec((1, 1, tile), lambda c, i: (c, 0, i))],
        out_shape=out_shape
        + grad_shapes
        + [jax.ShapeDtypeStruct((cols, 1, local), jnp.float32)],
        scratch_shapes=scratch,
        compiler_params=params(60),
        cost_estimate=cost(
            products * tokens * model * cols * local,
            8 * model * cols * local,
            tokens * cols * local,
        ),
        name="feed_forward_first" if first else "feed_forward_second",
    )(*normed, *turned, *cot, weight, fc_bias, *rest)


def middle_back_kernel(
    rows, cols, grad_ref, middle_ref, cot_ref, w_ref, vec_ref, dx_ref, turned_ref, datt_ref, sum_ref
):
    grad = grad_ref[...]
    unit, inverse = centered(middle_ref[...])
    total = cot_ref[...].astype(jnp.float32) + norm_back(grad, vec_ref[1:2], unit, inverse)
    dx_ref[...] = total
    low = total.astype(jnp.bfloat16)
    turned_ref[...] = jnp.transpose(low)
    depth = w_ref.shape[3] // rows
    for c in range(cols):
        part = dot_nt(low[:, :depth], out_block(w_ref, 0, c, rows))
        for r in range(1, rows):
            part = part + dot_nt(low[:, r * depth : (r + 1) * depth], out_block(w_ref, r, c, rows))
        part = part.astype(jnp.bfloat16)
        for r in range(rows):
            datt_ref[r, c] = part[:, r * PAIR : (r + 1) * PAIR]

    @pl.when(pl.program_id(0) == 0)
    def _():
        sum_ref[...] = jnp.zeros_like(sum_ref)

    sum_ref[0:1] += jnp.sum(grad * unit, axis=0, keepdims=True)
    sum_ref[1:2] += jnp.sum(grad, axis=0, keepdims=True)
    sum_ref[2:3] += jnp.sum(low.astype(jnp.float32), axis=0, keepdims=True)


def middle_back(grad, middle, cot, weight, vectors):
    span, model = middle.shape
    rows, cols = weight.shape[:2]
    tile = min(256, span)
    return pl.pallas_call(
        functools.partial(middle_back_kernel, rows, cols),
        grid=(span // tile,),
        in_specs=[
            pl.BlockSpec((tile, model), lambda i: (i, 0)),
            pl.BlockSpec((tile, model), lambda i: (i, 0)),
            pl.BlockSpec((tile, model), lambda i: (i, 0)),
            out_weight_spec(weight),
            fixed(vectors.shape),
        ],
        out_specs=[
            pl.BlockSpec((tile, model), lambda i: (i, 0)),
            pl.BlockSpec((model, tile), lambda i: (0, i)),
            pl.BlockSpec((rows, cols, tile, PAIR), lambda i: (0, 0, i, 0)),
            pl.BlockSpec((8, model), lambda i: (0, 0)),
        ],
        out_shape=[
            jax.ShapeDtypeStruct((span, model), jnp.float32),
            jax.ShapeDtypeStruct((model, span), jnp.bfloat16),
            jax.ShapeDtypeStruct((rows, cols, span, PAIR), jnp.bfloat16),
            jax.ShapeDtypeStruct((8, model), jnp.float32),
        ],
        compiler_params=params(60),
        cost_estimate=cost(2 * span * model * model, 2 * model * model + 18 * span * model),
        name="out_norm_back",
    )(grad, middle, cot, weight, vectors)


def out_grad_kernel(rows, dps, groups, *refs):
    out_ref = refs[-1]
    total = None
    for g in range(groups):
        att = jnp.concatenate([refs[groups + g][r, 0] for r in range(rows)], axis=1)
        part = dot(refs[g][...], att)
        total = part if total is None else total + part
    total = total.astype(jnp.bfloat16)
    half = out_ref.shape[3]
    for r in range(rows):
        for d in range(dps):
            at = (d * rows + r) * 2 * half
            out_ref[r, 0, d] = jnp.concatenate(
                [total[at : at + half], total[at + half : at + 2 * half]], axis=1
            )


def out_grad(turned, att, before, dps):
    groups = len(turned)
    model, span = turned[0].shape
    rows, cols = att[0].shape[:2]
    cut = model // (rows * dps)
    return pl.pallas_call(
        functools.partial(out_grad_kernel, rows, dps, groups),
        grid=(cols,),
        in_specs=[fixed((model, span))] * groups
        + [pl.BlockSpec((rows, 1, span, PAIR), lambda c: (0, c, 0, 0))] * groups
        + [pl.BlockSpec(memory_space=pl.ANY)],
        out_specs=pl.BlockSpec(
            (rows, 1, dps, cut // 2, 2 * rows * PAIR), lambda c: (0, c, 0, 4, 0)
        ),
        out_shape=jax.ShapeDtypeStruct(before.shape, before.dtype),
        compiler_params=params(60),
        cost_estimate=cost(2 * groups * span * model * model, 2 * model * model),
        input_output_aliases={2 * groups: 0},
        name="out_grad",
    )(*turned, *att, before)


def qkv_grad_kernel(final, dqkv_ref, x_ref, *refs):
    grad_ref, bias_ref, acc = refs[-3:]
    step = pl.program_id(0)
    grads = dqkv_ref[...]
    rows = x_ref[...].reshape(grads.shape[0], x_ref.shape[2])
    part = lax.dot_general(grads, rows, TN, preferred_element_type=jnp.float32)
    sums = jnp.sum(grads.astype(jnp.float32), axis=0, keepdims=True)

    @pl.when(step == 0)
    def _():
        acc[...] = refs[0][...] + part if final else part
        bias_ref[...] = jnp.zeros_like(bias_ref)

    @pl.when(step > 0)
    def _():
        acc[...] += part

    bias_ref[0:1] += sums

    @pl.when(step == pl.num_programs(0) - 1)
    def _():
        grad_ref[...] = jnp.transpose(acc[...]).astype(grad_ref.dtype) if final else acc[...]


def qkv_grad(dqkv, normed, before):
    tokens, width = dqkv.shape
    members, _, model = normed.shape
    final = len(before) == 1
    tile = 2 * tokens // members
    grad_type = (
        jax.ShapeDtypeStruct((model, width), jnp.bfloat16)
        if final
        else jax.ShapeDtypeStruct((width, model), jnp.float32)
    )
    return pl.pallas_call(
        functools.partial(qkv_grad_kernel, final),
        grid=(tokens // tile,),
        in_specs=[
            pl.BlockSpec((tile, width), lambda i: (i, 0)),
            pl.BlockSpec((2, tile // 2, model), lambda i: (i, 0, 0)),
        ]
        + [fixed((width, model))] * len(before),
        out_specs=[fixed(grad_type.shape), fixed((8, width))],
        out_shape=[grad_type, jax.ShapeDtypeStruct((8, width), jnp.float32)],
        scratch_shapes=[pltpu.VMEM((width, model), jnp.float32)],
        compiler_params=params(60),
        cost_estimate=cost(2 * tokens * model * width, 2 * tokens * (model + width)),
        name="qkv_grad",
    )(dqkv, normed, *before)


def input_kernel(rows, dps, plane_ref, dqkv_ref, left_ref, right_ref, dx_ref, tok_ref, *refs):
    gain_ref = refs[0]
    out_ref, sum_ref, acc = refs[-3:]
    step = pl.program_id(0) * pl.num_programs(1) + pl.program_id(1)
    short = left_ref.shape[3] * 2 // 3
    grads = []
    for part in range(3):
        lanes = slice(part * PAIR, (part + 1) * PAIR)
        grads += [dqkv_ref[half, 0, :, lanes] for half in range(2)]
    pieces = []
    for r in range(rows):
        for d in range(dps):
            at = (plane_ref[0] - d) & (dps - 1)
            left, right = left_ref[at, r, 0], right_ref[at, r, 0]
            last = jnp.concatenate([left[short:], right[short:]], axis=0)
            pieces.append(jnp.concatenate([left[:short], right[:short], last], axis=1))
    weights = jnp.concatenate(pieces, axis=0)
    piece = dot_nt(jnp.concatenate(grads, axis=1), weights)

    @pl.when(step == 0)
    def _():
        acc[...] = piece

    @pl.when(step > 0)
    def _():
        acc[...] += piece

    @pl.when(step == pl.num_programs(0) * pl.num_programs(1) - 1)
    def _():
        grad = acc[...]
        unit, inverse = centered(tok_ref[0].astype(jnp.float32))
        out_ref[0] = dx_ref[...] + norm_back(grad, gain_ref[...], unit, inverse)
        sum_ref[0:1] = jnp.sum(grad * unit, axis=0, keepdims=True)
        sum_ref[1:2] = jnp.sum(grad, axis=0, keepdims=True)


def input_back(plane, dqkv, dx, tokens, weight, gain, before, g):
    dps, rows, cols, high, _ = weight.shape
    span, model = dx.shape
    return pl.pallas_call(
        functools.partial(input_kernel, rows, dps),
        grid=(rows // 2, cols),
        in_specs=[
            pl.BlockSpec(memory_space=pltpu.SMEM),
            pl.BlockSpec((2, 1, span, 3 * PAIR), lambda i, c: (i, c, 0, 0)),
            pl.BlockSpec((dps, rows, 1, high, 2 * PAIR), lambda i, c: (0, 0, c, 0, i)),
            pl.BlockSpec((dps, rows, 1, high, 2 * PAIR), lambda i, c: (0, 0, c, 0, rows // 2 + i)),
            fixed((span, model)),
            pl.BlockSpec((1, span, model), lambda i, c: (g, 0, 0), pipeline_mode=pl.Buffered(1)),
            fixed((1, model)),
        ]
        + [pl.BlockSpec(memory_space=pl.ANY)] * len(before),
        out_specs=[
            pl.BlockSpec((1, span, model), lambda i, c: (g, 0, 0), pipeline_mode=pl.Buffered(1)),
            fixed((8, model)),
        ],
        out_shape=[
            jax.ShapeDtypeStruct(tokens.shape, jnp.float32),
            jax.ShapeDtypeStruct((8, model), jnp.float32),
        ],
        scratch_shapes=[pltpu.VMEM((span, model), jnp.float32)],
        compiler_params=params(60),
        cost_estimate=cost(6 * span * model * model, 6 * model * model + 12 * span * model),
        input_output_aliases={7: 0} if before else {},
        name="input_back",
    )(plane, dqkv, weight, weight, dx, tokens, gain, *before)


def head_body(
    tokens,
    cotangent,
    branch,
    ln1_gain,
    ln1_bias,
    qkv_weight,
    qv_bias,
    out_weight,
    out_bias,
    ln2_gain,
    ln2_bias,
    fc_weight,
    fc_bias,
    proj_weight,
    proj_bias,
):
    groups, span, model = tokens.shape
    rows = lax.axis_size("row")
    cols = lax.axis_size("col")
    dps = lax.axis_size("dp")
    members = rows * cols
    count = groups * span
    head_cols = qv_bias.shape[1]
    hidden_cols = fc_bias.shape[0]

    def spread(shard):
        whole = lax.all_gather(shard, MESH_AXES, axis=0, tiled=False)
        return whole.reshape((rows, cols) + shard.shape)

    def swap(blocks):
        return lax.all_to_all(blocks, MESH_AXES, 0, 0, tiled=True)

    def collect_plane(partial):
        partial = partial.reshape((members,) + partial.shape[2:])
        partial = lax.psum_scatter(partial, MESH_AXES, scatter_dimension=0, tiled=True)
        return partial.reshape(partial.shape[1:])

    def exchange_dp(partial):
        me = lax.axis_index("dp")
        summed = lax.dynamic_index_in_dim(partial, me, 0, False).astype(jnp.float32)
        for shift in range(1, dps):
            piece = lax.dynamic_index_in_dim(partial, (me + shift) % dps, 0, False)
            pairs = [(i, (i + shift) % dps) for i in range(dps)]
            summed = summed + lax.ppermute(piece, "dp", pairs).astype(jnp.float32)
        return summed

    def collect_dp(partial):
        partial = lax.psum_scatter(partial, "dp", scatter_dimension=0, tiled=True)
        return partial[0].astype(jnp.float32)

    def total(values):
        for axis in ("row", "col", "dp"):
            size = lax.axis_size(axis)
            step = 1
            while step < size:
                pairs = [(i, i ^ step) for i in range(size)]
                values = values + lax.ppermute(values, axis, pairs)
                step *= 2
        return values

    half = hidden_cols // 2
    residual = tokens.astype(jnp.float32)
    normed = normalize(residual, ln1_gain, ln1_bias).astype(jnp.bfloat16)
    row = lax.axis_index("row")
    col = lax.axis_index("col")
    own = qkv_weight.reshape(-1, 3, rows, PAIR).transpose(2, 0, 1, 3)
    own = lax.all_to_all(own.reshape(rows, -1, 3 * PAIR), "row", 0, 0, tiled=True)
    own = own.reshape(model, 3 * PAIR)
    own_bias = lax.dynamic_slice_in_dim(qv_bias, row * PAIR, PAIR, 1)
    own_bias = jnp.concatenate([own_bias[0], jnp.zeros((PAIR,), jnp.float32), own_bias[1]])
    fc_full = lax.all_gather(fc_bias, "col", axis=0).reshape(cols, 1, hidden_cols)

    normed_all = [lax.all_gather(normed[0], MESH_AXES, axis=0, tiled=False)]
    cot_flat = cotangent.reshape(count, model)
    cot_turned = cot_flat.T
    toks = [tokens[g] for g in range(groups)]
    cots = [cotangent[g] for g in range(groups)]
    proj_bias_sum = jnp.sum(cot_flat.astype(jnp.float32), axis=0)
    plane = lax.axis_index("dp")
    short = qkv_weight.shape[0] // dps
    part = lax.dynamic_slice_in_dim(qkv_weight, plane * short, short, 0)
    last = jnp.concatenate([part[: short // 2, 2], part[short // 2 :, 2]], axis=1)
    part = jnp.concatenate([part[:, 0], part[:, 1]], axis=1)
    later = jnp.concatenate([normed[1], part, last], axis=0)
    shards = pack_weights(fc_weight, proj_weight, out_weight)
    normed_all[0], later, cot_turned, proj_bias_sum, shards, own, fc_full = (
        lax.optimization_barrier(
            (normed_all[0], later, cot_turned, proj_bias_sum, shards, own, fc_full)
        )
    )
    later = lax.all_gather(later, MESH_AXES, axis=0, tiled=False)
    normed_all.append(later)
    vectors = jnp.stack([out_bias, ln2_gain, ln2_bias] + [out_bias] * 5)
    gains = jnp.stack([ln2_gain] * 8)
    qkv, att, att_own, log_totals, middle, normed_two, turned_two = [], [], [], [], [], [], []
    w_first = spread(shards[0])
    w_second = spread(shards[1])
    def step_up(value):
        return lax.ppermute(value, "dp", [(i, i + 1) for i in range(dps - 1)])

    def step_down(value):
        return lax.ppermute(value, "dp", [(i + 1, i) for i in range(dps - 1)])

    for g in range(groups):
        qkv.append(project_qkv(normed_all[g], own, own_bias, span))
        mixed, totals = attend(branch[g], qkv[g])
        if g < groups - 1:
            mixed, normed_all[g + 1] = lax.optimization_barrier((mixed, normed_all[g + 1]))
        att_own.append(mixed)
        if g > 0:
            quarter = normed_all[1][:, span:].reshape(rows, cols, -1, model)
            ups, downs = [step_up(quarter)], [step_down(quarter)]
            mixed, att[g - 1], ups, downs = lax.optimization_barrier(
                (mixed, att[g - 1], ups, downs)
            )
            ups.append(step_up(ups[-1]))
            downs.append(step_down(downs[-1]))
        log_totals.append(totals)
        att.append(swap(mixed.reshape(members, span, PAIR)).reshape(rows, cols, span, PAIR))
    for g in range(groups):
        mid, low, turned = project_out(toks[g], att[g], w_first, vectors)
        middle.append(mid)
        normed_two.append(low)
        turned_two.append(turned)
    all_turned = turned_two + [cot_turned]
    normed_two[-1], ups, downs = lax.optimization_barrier((normed_two[-1], ups, downs))
    ups.append(step_up(ups[-1]))
    downs.append(step_down(downs[-1]))
    first_parts = feed_forward(
        True, normed_two, all_turned, cots, w_first, fc_full[:, :, :half], middle, dps
    )
    grad_first, fc_sum_first = first_parts[2 * groups :]
    plane_first = collect_plane(grad_first)
    block_out, low, active, fc_sums = [], [], [], []
    dx, dx_turned, grad_att, sums_two = [], [], [], []
    for g in range(groups):
        output_rows, grad_two, low_part, active_part, fc_part = feed_forward(
            False,
            [normed_two[g]],
            [],
            [cots[g]],
            w_second,
            fc_full[:, :, half:],
            (first_parts[g], first_parts[groups + g], proj_bias[None]),
            dps,
        )
        block_out.append(output_rows)
        low.append(low_part)
        active.append(active_part)
        fc_sums.append(fc_part)
        rows_grad, turned, datt, sums = middle_back(
            grad_two, middle[g], cots[g], w_first, gains
        )
        dx.append(rows_grad)
        dx_turned.append(turned)
        sums_two.append(sums)
        if g == 0:
            datt, normed_two[1] = lax.optimization_barrier((datt, normed_two[1]))
        grad_att.append(
            swap(datt.reshape(members, span, PAIR)).reshape(members * span, PAIR)
        )
    fc_sum_second = functools.reduce(jnp.add, fc_sums)
    grad_second = hidden_grad(turned_two, cot_turned, low, active, dps, rows)
    grad_att[0], grad_second = lax.optimization_barrier((grad_att[0], grad_second))
    plane_second = collect_plane(out_grad(dx_turned, att, grad_second, dps))
    rows_back, grads, bias_sums, before = [], [], [], []
    for g in range(groups):
        grad = attend_back(branch[g], qkv[g], att_own[g], grad_att[g], log_totals[g])
        if g == 0:
            grad, grad_att[1], plane_first = lax.optimization_barrier(
                (grad, grad_att[1], plane_first)
            )
            hidden_first = exchange_dp(plane_first)
        else:
            grad, rows_back[0], hidden_first, grads[0], ups, downs = lax.optimization_barrier(
                (grad, rows_back[0], hidden_first, grads[0], ups, downs)
            )
        rows_back.append(grad)
        grads.append(
            swap(grad.reshape(members, span, 3 * PAIR)).reshape(rows, cols, span, 3 * PAIR)
        )
    for g in range(groups):
        grad_qkv, bias_sum = qkv_grad(rows_back[g], normed_all[g], before)
        before = [grad_qkv]
        bias_sums.append(bias_sum[0])
    grad_qkv = exchange_dp(grad_qkv.reshape(dps, rows, -1, 3 * PAIR))
    quarters = [quarter]
    for shift in range(1, dps):
        quarters.append(jnp.where(plane >= shift, ups[shift - 1], downs[dps - shift - 1]))
    w_qkv = jnp.stack(quarters)
    input_grads, sums_one = [], []
    for g in range(groups):
        rows_grad, sums = input_back(
            plane[None], grads[g], dx[g], tokens, w_qkv, ln1_gain[None], input_grads, g
        )
        input_grads = [rows_grad]
        sums_one.append(sums)
        if g == 0:
            input_grads, grad_qkv, plane_second = lax.optimization_barrier(
                (input_grads, grad_qkv, plane_second)
            )
            hidden_second = collect_dp(plane_second)
    sums_two = functools.reduce(jnp.add, sums_two)
    fc_sum = jnp.concatenate([fc_sum_first, fc_sum_second], axis=2).reshape(-1)
    sums_one = functools.reduce(jnp.add, sums_one)
    bias_sum = functools.reduce(jnp.add, bias_sums)
    qv_sum = jnp.zeros((2, model), jnp.float32)
    qv_sum = lax.dynamic_update_slice(
        qv_sum,
        jnp.stack([bias_sum[:PAIR], bias_sum[2 * PAIR :]]),
        (0, col * head_cols + row * PAIR),
    )
    small = (sums_two[2], sums_two[0], sums_two[1], fc_sum, proj_bias_sum)
    small += (sums_one[0], sums_one[1], qv_sum.reshape(-1))
    small = total(jnp.concatenate(small))
    grad_qkv = lax.all_to_all(grad_qkv, "row", 0, 0, tiled=True)
    d_qkv = grad_qkv.reshape(rows, -1, 3, PAIR).transpose(1, 2, 0, 3).reshape(-1, 3, head_cols)
    cut = model // (rows * dps)
    d_fc, d_proj = (
        jnp.concatenate([hidden_first[at : at + cut], hidden_second[at : at + cut]], axis=1)
        for at in (0, cut)
    )
    packed_out = hidden_second[2 * cut :]
    d_out = jnp.concatenate([packed_out[:, :head_cols], packed_out[:, head_cols:]], axis=0).T
    parts, at = [], 0
    for size in (model, model, model, hidden_cols * cols, model, model, model, 2 * model):
        parts.append(small[at : at + size])
        at += size
    s_out, s_gain_two, s_bias_two, s_fc, s_proj, s_gain_one, s_bias_one, s_qv = parts
    return (
        jnp.stack(block_out),
        input_grads[0],
        s_gain_one,
        s_bias_one,
        d_qkv,
        s_qv.reshape(2, model),
        d_out,
        s_out,
        s_gain_two,
        s_bias_two,
        d_fc,
        s_fc,
        d_proj.T,
        s_proj,
    )


def by_heads(mesh):
    rows, cols = mesh.shape["row"], mesh.shape["col"]

    def body(tokens, cotangent, branch, ln1_gain, ln1_bias, qkv_weight, *rest):
        width = qkv_weight.shape[2] * cols
        whole = tokens.shape[1] * rows * cols
        fits = width == rows * cols * PAIR and rows == 4 and mesh.shape["dp"] == 4 and tokens.shape[0] == 2
        fits = fits and qkv_weight.shape[0] * 4 == qkv_weight.shape[2] * cols
        fits = fits and rest[6].shape[0] == 4 * rows * PAIR
        fits = fits and all(size & (size - 1) == 0 for size in mesh.shape.values())
        fits = fits and whole == PLEN + CONTS * CLEN and tokens.shape[1] % BQ == 0
        chosen = head_body if fits else gathered_body
        return chosen(tokens, cotangent, branch, ln1_gain, ln1_bias, qkv_weight, *rest)

    return body


def solution(mesh):
    placed = (
        P("dp", ("row", "col"), None),
        P("dp", ("row", "col"), None),
        P("dp", None),
        P(),
        P(),
        P("row", None, "col"),
        P(None, "col"),
        P("col", "row"),
        P(),
        P(),
        P(),
        P("row", "col"),
        P("col"),
        P("col", "row"),
        P(),
    )
    return jax.shard_map(
        by_heads(mesh),
        mesh=mesh,
        in_specs=placed,
        out_specs=(
            P("dp", ("row", "col"), None),
            P("dp", ("row", "col"), None),
            P(),
            P(),
            P(("dp", "row"), None, "col"),
            P(),
            P("col", ("dp", "row")),
            P(),
            P(),
            P(),
            P(("dp", "row"), "col"),
            P(),
            P("col", ("dp", "row")),
            P(),
        ),
        check_vma=False,
    )
```

```python
import functools

import jax
import jax.numpy as jnp
from jax import lax
from jax.experimental import pallas as pl
from jax.experimental.pallas import tpu as pltpu
from jax.sharding import PartitionSpec as P

HEAD = 64
PLEN = 2048
CLEN = 256
CONTS = 8


EPSILON = 1e-05
MASKED_SCORE = -1e30
LOG2E = 1.4426950408889634
PAIR = 2 * HEAD
BQ = 256
BK = 512
BK_BACK = 512
HIDDEN_TILE = 512
NT = (((1,), (1,)), ((), ()))
TN = (((0,), (0,)), ((), ()))
MESH_AXES = ("row", "col")


def normalize(values, gain, shift):
    center = values - jnp.mean(values, axis=-1, keepdims=True)
    spread = jnp.mean(center * center, axis=-1, keepdims=True)
    return center * lax.rsqrt(spread + EPSILON) * gain + shift


def gelu_tanh(values):
    return jax.nn.gelu(values, approximate=True)


def allowed_keys(row_pos, col_pos, branch_cut):
    row_seg = jnp.where(row_pos >= PLEN, (row_pos - PLEN) // CLEN, -1)
    col_seg = jnp.where(col_pos >= PLEN, (col_pos - PLEN) // CLEN, -1)
    picked = (row_seg[:, None] == jnp.arange(CONTS, dtype=jnp.int32)[None, :]).astype(jnp.int32)
    row_cut = jnp.sum(picked * branch_cut[None, :], axis=1)
    causal = col_pos[None, :] <= row_pos[:, None]
    same_seq = col_seg[None, :] == row_seg[:, None]
    in_prefix = (
        (row_seg[:, None] >= 0) & (col_seg[None, :] < 0) & (col_pos[None, :] < row_cut[:, None])
    )
    return same_seq & causal | in_prefix


def add_trees(first, second):
    return jax.tree.map(lambda total, extra: total + extra, first, second)


def gathered_body(
    tokens,
    cotangent,
    branch,
    ln1_gain,
    ln1_bias,
    qkv_weight,
    qv_bias,
    out_weight,
    out_bias,
    ln2_gain,
    ln2_bias,
    fc_weight,
    fc_bias,
    proj_weight,
    proj_bias,
):
    scale = HEAD ** (-0.5)
    width = tokens.shape[2]
    local_rows = tokens.shape[1]
    head_cols = qv_bias.shape[1]
    head_count = head_cols // HEAD
    ff_local = fc_bias.shape[0]
    col_count = lax.axis_size("col")
    row_count = lax.axis_size("row")
    row_rows = local_rows * col_count
    group_rows = row_rows * row_count
    q_block = min(512, row_rows)
    block_count = row_rows // q_block
    row_base = lax.axis_index("row") * row_rows
    col_index = lax.axis_index("col")
    bias_three = jnp.stack([qv_bias[0], jnp.zeros_like(qv_bias[0]), qv_bias[1]])
    key_pos = jnp.arange(group_rows, dtype=jnp.int32)
    block_starts = jnp.arange(block_count, dtype=jnp.int32) * q_block

    def spread_rows(values):
        return lax.all_gather(values, "col", axis=0, tiled=True)

    def spread_grads(values):
        return lax.all_gather(values, "col", axis=0, tiled=True)

    def sum_branch(values):
        return lax.psum_scatter(values, "col", scatter_dimension=0, tiled=True)

    def sum_inputs(values):
        return lax.psum_scatter(values, "col", scatter_dimension=0, tiled=True)

    kept_weights = (
        lax.all_gather(qkv_weight, "row", axis=0, tiled=True),
        lax.all_gather(out_weight, "row", axis=1, tiled=True),
        lax.all_gather(fc_weight, "row", axis=0, tiled=True),
        lax.all_gather(proj_weight, "row", axis=1, tiled=True),
    )

    def block_scores(queries3, keys3, offset, branch_cut):
        q_part = lax.dynamic_slice_in_dim(queries3, offset, q_block, 0)
        row_pos = row_base + offset + jnp.arange(q_block, dtype=jnp.int32)
        allowed = allowed_keys(row_pos, key_pos, branch_cut)
        scores = (
            jnp.einsum("qhd,khd->hqk", q_part, keys3, preferred_element_type=jnp.float32) * scale
        )
        return (q_part, jnp.where(allowed[None], scores, MASKED_SCORE))

    def micro_step(carry, micro_item):
        grads_acc, small_acc = carry
        tok_rows, cot_rows, branch_cut = micro_item
        w_qkv, w_out, w_fc, w_proj = kept_weights
        residual = tok_rows.astype(jnp.float32)
        normed = normalize(residual, ln1_gain, ln1_bias).astype(jnp.bfloat16)
        normed_all = spread_rows(normed)
        projected = jnp.einsum("td,dsf->tsf", normed_all, w_qkv, preferred_element_type=jnp.float32)
        projected = (projected + bias_three[None]).astype(jnp.bfloat16)
        key_rows, value_rows = (
            lax.all_gather(projected[:, 1], "row", axis=0, tiled=True),
            lax.all_gather(projected[:, 2], "row", axis=0, tiled=True),
        )
        queries3 = projected[:, 0].reshape(row_rows, head_count, HEAD)
        keys3 = key_rows.reshape(group_rows, head_count, HEAD)
        values3 = value_rows.reshape(group_rows, head_count, HEAD)

        def attend(offset):
            q_part, scores = block_scores(queries3, keys3, offset, branch_cut)
            row_peak = jnp.max(scores, axis=-1, keepdims=True)
            exponent = jnp.exp(scores - row_peak)
            row_total = jnp.sum(exponent, axis=-1, keepdims=True)
            probs_low = (exponent / row_total).astype(jnp.bfloat16)
            mixed_rows = jnp.einsum(
                "hqk,khd->qhd", probs_low, values3, preferred_element_type=jnp.float32
            )
            return (mixed_rows, (row_peak + jnp.log(row_total))[..., 0])

        attended, log_totals = lax.map(attend, block_starts)
        attended = attended.reshape(row_rows, head_cols).astype(jnp.bfloat16)
        branch_part = jnp.dot(attended, w_out, preferred_element_type=jnp.float32)
        middle = residual + sum_branch(branch_part) + out_bias
        normed_two = normalize(middle, ln2_gain, ln2_bias).astype(jnp.bfloat16)
        normed_two_all = spread_rows(normed_two)
        hidden = jnp.dot(normed_two_all, w_fc, preferred_element_type=jnp.float32) + fc_bias
        active = gelu_tanh(hidden).astype(jnp.bfloat16)
        ffn_part = jnp.dot(active, w_proj, preferred_element_type=jnp.float32)
        output_rows = (middle + sum_branch(ffn_part) + proj_bias).astype(jnp.bfloat16)
        cot_all = spread_grads(cot_rows)
        grad_proj = jnp.einsum("tf,td->fd", active, cot_all, preferred_element_type=jnp.float32)
        grad_proj_bias = jnp.sum(cot_rows.astype(jnp.float32), axis=0)
        grad_active = jnp.einsum("td,fd->tf", cot_all, w_proj, preferred_element_type=jnp.float32)
        grad_hidden = jax.vjp(gelu_tanh, hidden)[1](grad_active)[0].astype(jnp.bfloat16)
        grad_fc = jnp.einsum(
            "td,tf->df", normed_two_all, grad_hidden, preferred_element_type=jnp.float32
        )
        grad_fc_bias = jnp.sum(grad_hidden.astype(jnp.float32), axis=0)
        grad_normed_two = sum_inputs(
            jnp.einsum("tf,df->td", grad_hidden, w_fc, preferred_element_type=jnp.float32)
        )
        back_middle, grad_gain_two, grad_bias_two = jax.vjp(normalize, middle, ln2_gain, ln2_bias)[
            1
        ](grad_normed_two)
        grad_middle = cot_rows.astype(jnp.float32) + back_middle
        grad_out_rows = grad_middle.astype(jnp.bfloat16)
        grad_out_all = spread_grads(grad_out_rows)
        grad_out = jnp.einsum(
            "tc,td->cd", attended, grad_out_all, preferred_element_type=jnp.float32
        )
        grad_out_bias = jnp.sum(grad_out_rows.astype(jnp.float32), axis=0)
        grad_att = jnp.einsum("td,cd->tc", grad_out_all, w_out, preferred_element_type=jnp.float32)
        grad_att = grad_att.astype(jnp.bfloat16).reshape(row_rows, head_count, HEAD)

        def attend_back(acc_pair, block_item):
            offset, log_total = block_item
            grad_keys_acc, grad_values_acc = acc_pair
            q_part, scores = block_scores(queries3, keys3, offset, branch_cut)
            probs = jnp.exp(scores - log_total[..., None])
            probs_low = probs.astype(jnp.bfloat16)
            grad_part = lax.dynamic_slice_in_dim(grad_att, offset, q_block, 0)
            grad_values_acc = grad_values_acc + jnp.einsum(
                "hqk,qhd->khd", probs_low, grad_part, preferred_element_type=jnp.float32
            )
            grad_probs = jnp.einsum(
                "qhd,khd->hqk", grad_part, values3, preferred_element_type=jnp.float32
            )
            center = jnp.sum(grad_probs * probs, axis=-1, keepdims=True)
            grad_scores = (probs * (grad_probs - center)).astype(jnp.bfloat16)
            grad_keys_acc = (
                grad_keys_acc
                + jnp.einsum(
                    "hqk,qhd->khd", grad_scores, q_part, preferred_element_type=jnp.float32
                )
                * scale
            )
            grad_query = (
                jnp.einsum("hqk,khd->qhd", grad_scores, keys3, preferred_element_type=jnp.float32)
                * scale
            )
            return ((grad_keys_acc, grad_values_acc), grad_query)

        empty_keys = jnp.zeros((group_rows, head_count, HEAD), jnp.float32)
        (grad_keys, grad_values), grad_queries = lax.scan(
            attend_back, (empty_keys, empty_keys), (block_starts, log_totals)
        )
        own_keys, own_values = (
            lax.psum_scatter(
                grad_keys.reshape(group_rows, head_cols).astype(jnp.bfloat16),
                "row",
                scatter_dimension=0,
                tiled=True,
            ).astype(jnp.float32),
            lax.psum_scatter(
                grad_values.reshape(group_rows, head_cols).astype(jnp.bfloat16),
                "row",
                scatter_dimension=0,
                tiled=True,
            ).astype(jnp.float32),
        )
        grad_projected = jnp.stack(
            [grad_queries.reshape(row_rows, head_cols), own_keys, own_values], axis=1
        ).astype(jnp.bfloat16)
        grad_qkv = jnp.einsum(
            "td,tsf->dsf", normed_all, grad_projected, preferred_element_type=jnp.float32
        )
        grad_qkv_bias = jnp.sum(grad_projected.astype(jnp.float32), axis=0)
        grad_normed = sum_inputs(
            jnp.einsum("tsf,dsf->td", grad_projected, w_qkv, preferred_element_type=jnp.float32)
        )
        back_input, grad_gain_one, grad_bias_one = jax.vjp(normalize, residual, ln1_gain, ln1_bias)[
            1
        ](grad_normed)
        input_rows = grad_middle + back_input
        weight_terms = (grad_qkv, grad_out, grad_fc, grad_proj)
        small_terms = (
            grad_gain_one,
            grad_bias_one,
            grad_qkv_bias,
            grad_out_bias,
            grad_gain_two,
            grad_bias_two,
            grad_fc_bias,
            grad_proj_bias,
        )
        return (
            (add_trees(grads_acc, weight_terms), add_trees(small_acc, small_terms)),
            (output_rows, input_rows),
        )

    grads_init = (
        jnp.zeros((width, 3, head_cols), jnp.float32),
        jnp.zeros((head_cols, width), jnp.float32),
        jnp.zeros((width, ff_local), jnp.float32),
        jnp.zeros((ff_local, width), jnp.float32),
    )
    vector_zero = jnp.zeros((width,), jnp.float32)
    small_init = (
        vector_zero,
        vector_zero,
        jnp.zeros((3, head_cols), jnp.float32),
        vector_zero,
        vector_zero,
        vector_zero,
        jnp.zeros((ff_local,), jnp.float32),
        vector_zero,
    )
    (grads_acc, small_acc), (block_out, input_grad) = lax.scan(
        micro_step, (grads_init, small_init), (tokens, cotangent, branch)
    )
    (
        gain_one,
        bias_one,
        qkv_bias_acc,
        out_bias_acc,
        gain_two,
        bias_two,
        fc_bias_acc,
        proj_bias_acc,
    ) = small_acc
    qv_full = lax.dynamic_update_slice(
        jnp.zeros((2, width), jnp.float32),
        jnp.stack([qkv_bias_acc[0], qkv_bias_acc[2]]),
        (jnp.int32(0), col_index * head_cols),
    )
    fc_full = lax.dynamic_update_slice(
        jnp.zeros((ff_local * col_count,), jnp.float32), fc_bias_acc, (col_index * ff_local,)
    )
    summed = lax.psum(
        (gain_one, bias_one, qv_full, out_bias_acc, gain_two, bias_two, fc_full, proj_bias_acc),
        ("dp", "row", "col"),
    )
    return (
        block_out,
        input_grad,
        summed[0],
        summed[1],
        lax.psum_scatter(
            grads_acc[0].astype(jnp.bfloat16), ("dp", "row"), scatter_dimension=0, tiled=True
        ).astype(jnp.float32),
        summed[2],
        lax.psum_scatter(
            grads_acc[1].astype(jnp.bfloat16), ("dp", "row"), scatter_dimension=1, tiled=True
        ).astype(jnp.float32),
        summed[3],
        summed[4],
        summed[5],
        lax.psum_scatter(
            grads_acc[2].astype(jnp.bfloat16), ("dp", "row"), scatter_dimension=0, tiled=True
        ).astype(jnp.float32),
        summed[6],
        lax.psum_scatter(
            grads_acc[3].astype(jnp.bfloat16), ("dp", "row"), scatter_dimension=1, tiled=True
        ).astype(jnp.float32),
        summed[7],
    )


def dot(left, right):
    return jnp.dot(left, right, preferred_element_type=jnp.float32)


def dot_nt(left, right):
    return lax.dot_general(left, right, NT, preferred_element_type=jnp.float32)


def cost(flops, moved, exps=0):
    return pl.CostEstimate(flops=int(flops), bytes_accessed=int(moved), transcendentals=int(exps))


def params(mebibytes):
    return pltpu.CompilerParams(vmem_limit_bytes=mebibytes * 2**20)


def fixed(shape):
    return pl.BlockSpec(shape, lambda *_: (0,) * len(shape), pipeline_mode=pl.Buffered(1))


def pair_rows(rows):
    low = lax.broadcasted_iota(jnp.int32, rows.shape, 1) < HEAD
    zero = jnp.zeros_like(rows)
    return jnp.concatenate([jnp.where(low, rows, zero), jnp.where(low, zero, rows)], axis=0)


def pick_lanes(stacked):
    half = stacked.shape[0] // 2
    low = lax.broadcasted_iota(jnp.int32, (half, stacked.shape[1]), 1) < HEAD
    return jnp.where(low, stacked[:half], stacked[half:])


def pack_kernel(fc_ref, proj_ref, out_ref, first_ref, second_ref):
    depth, hidden = fc_ref.shape
    half = hidden // 2
    turned = jnp.transpose(proj_ref[...])
    for at, ref in ((0, first_ref), (half, second_ref)):
        ref[:depth] = fc_ref[:, at : at + half]
        ref[depth : 2 * depth] = turned[:, at : at + half]
    for h in range(out_ref.shape[0] // PAIR):
        first_ref[2 * depth :, h * depth : (h + 1) * depth] = out_ref[h * PAIR : (h + 1) * PAIR]


def pack_weights(fc_weight, proj_weight, out_weight):
    depth, hidden = fc_weight.shape
    shapes = [(2 * depth + PAIR, hidden // 2), (2 * depth, hidden // 2)]
    return pl.pallas_call(
        pack_kernel,
        in_specs=[pl.BlockSpec(memory_space=pltpu.VMEM)] * 3,
        out_specs=[pl.BlockSpec(memory_space=pltpu.VMEM)] * 2,
        out_shape=[jax.ShapeDtypeStruct(shape, jnp.bfloat16) for shape in shapes],
        compiler_params=params(60),
        cost_estimate=cost(1, 8 * depth * hidden),
        name="pack_weights",
    )(fc_weight, proj_weight, out_weight)


def qkv_kernel(x_ref, w_ref, vec_ref, out_ref):
    rows = x_ref[...].reshape(out_ref.shape[0], x_ref.shape[2])
    values = (dot(rows, w_ref[...]) + vec_ref[0:1]) * vec_ref[1:2]
    out_ref[...] = values.astype(out_ref.dtype)


def project_qkv(normed, weight, bias, span):
    members, _, model = normed.shape
    width = weight.shape[1]
    tokens = members * span
    vectors = jnp.stack([bias, jnp.where(jnp.arange(width) < PAIR, HEAD**-0.5, 1.0)])
    return pl.pallas_call(
        qkv_kernel,
        grid=(members // 2,),
        in_specs=[
            pl.BlockSpec((2, span, model), lambda i: (i, 0, 0)),
            fixed((model, width)),
            fixed((2, width)),
        ],
        out_specs=pl.BlockSpec((2 * span, width), lambda i: (i, 0)),
        out_shape=jax.ShapeDtypeStruct((tokens, width), jnp.bfloat16),
        compiler_params=params(60),
        cost_estimate=cost(2 * tokens * model * width, 2 * tokens * (model + width)),
        name="qkv",
    )(normed, weight, vectors)


def attend_kernel(
    bk, cut_ref, qkv_ref, o_ref, lse_ref, s_ref, own_ref, value_ref, peak_ref, acc_ref
):
    i = pl.program_id(0)
    prompt_blocks = PLEN // BQ

    @pl.when(i == 0)
    def _():
        value_ref[:, :PAIR] = qkv_ref[:, 2 * PAIR : 3 * PAIR]
        value_ref[:, PAIR:] = jnp.ones((value_ref.shape[0], PAIR), value_ref.dtype)

    start = pl.multiple_of(i * BQ, BQ)
    queries = pair_rows(qkv_ref[pl.ds(start, BQ), 0:PAIR])
    limit = jnp.where(i < prompt_blocks, start, cut_ref[jnp.maximum(i - prompt_blocks, 0)])
    full = limit // bk
    rest = limit - full * bk

    def scores(first, count):
        keys = qkv_ref[pl.ds(pl.multiple_of(first, BQ), count), PAIR : 2 * PAIR]
        return dot_nt(queries, keys) * LOG2E

    def lane_peak(values):
        return functools.reduce(
            jnp.maximum, [values[:, at : at + 128] for at in range(0, values.shape[1], 128)]
        )

    own = scores(start, BQ)
    row = lax.broadcasted_iota(jnp.int32, own.shape, 0) & (BQ - 1)
    own = jnp.where(lax.broadcasted_iota(jnp.int32, own.shape, 1) <= row, own, MASKED_SCORE)
    own_ref[...] = own
    peak_ref[...] = lane_peak(own)

    def score_step(j, none):
        values = scores(j * bk, bk)
        s_ref[j] = values
        peak_ref[...] = jnp.maximum(peak_ref[...], lane_peak(values))
        return none

    lax.fori_loop(0, full, score_step, 0)

    @pl.when(rest > 0)
    def _():
        values = scores(full * bk, bk)
        seen = lax.broadcasted_iota(jnp.int32, values.shape, 1) < rest
        values = jnp.where(seen, values, MASKED_SCORE)
        s_ref[full] = values
        peak_ref[...] = jnp.maximum(peak_ref[...], lane_peak(values))

    peak = jnp.max(peak_ref[...], axis=1, keepdims=True)
    probs = jnp.exp2(own_ref[...] - peak).astype(jnp.bfloat16)
    acc_ref[...] = dot(probs, value_ref[pl.ds(start, BQ), :])

    def value_step(j, none):
        probs = jnp.exp2(s_ref[j] - peak).astype(jnp.bfloat16)
        acc_ref[...] += dot(probs, value_ref[pl.ds(pl.multiple_of(j * bk, bk), bk), :])
        return none

    lax.fori_loop(0, full + jnp.where(rest > 0, 1, 0), value_step, 0)
    total = acc_ref[:, PAIR:]
    o_ref[...] = pick_lanes(acc_ref[:, :PAIR] / total).astype(o_ref.dtype)
    lse_ref[0] = jnp.transpose(peak + jnp.log2(total))[:8]


def attend(cut, qkv):
    tokens = qkv.shape[0]
    blocks = tokens // BQ
    pairs = 2 * tokens * tokens // 4
    return pl.pallas_call(
        functools.partial(attend_kernel, BK),
        grid=(blocks,),
        in_specs=[pl.BlockSpec(memory_space=pltpu.SMEM), fixed((tokens, 3 * PAIR))],
        out_specs=[
            pl.BlockSpec((BQ, PAIR), lambda i: (i, 0)),
            pl.BlockSpec((1, 8, 2 * BQ), lambda i: (i, 0, 0)),
        ],
        out_shape=[
            jax.ShapeDtypeStruct((tokens, PAIR), jnp.bfloat16),
            jax.ShapeDtypeStruct((blocks, 8, 2 * BQ), jnp.float32),
        ],
        scratch_shapes=[
            pltpu.VMEM((PLEN // BK, 2 * BQ, BK), jnp.float32),
            pltpu.VMEM((2 * BQ, BQ), jnp.float32),
            pltpu.VMEM((tokens, 2 * PAIR), jnp.bfloat16),
            pltpu.VMEM((2 * BQ, PAIR), jnp.float32),
            pltpu.VMEM((2 * BQ, 2 * PAIR), jnp.float32),
        ],
        compiler_params=params(60),
        cost_estimate=cost(8 * 2 * pairs * 256, 2 * tokens * 4 * PAIR, pairs),
        name="attend",
    )(cut, qkv)


def attend_back_kernel(
    bk, cut_ref, qkv_ref, o_ref, do_ref, lse_ref, out_ref, dk_ref, dv_ref, dq_ref
):
    i = pl.program_id(0)
    prompt_blocks = PLEN // BQ

    @pl.when(i == 0)
    def _():
        dk_ref[...] = jnp.zeros_like(dk_ref)
        dv_ref[...] = jnp.zeros_like(dv_ref)

    start = pl.multiple_of(i * BQ, BQ)
    queries = pair_rows(qkv_ref[pl.ds(start, BQ), 0:PAIR])
    grad = do_ref[pl.ds(start, BQ), :]
    grads = pair_rows(grad)
    mixed = jnp.transpose(
        grad.astype(jnp.float32) * o_ref[pl.ds(start, BQ), :].astype(jnp.float32)
    )
    center = jnp.concatenate(
        [
            jnp.sum(mixed[:HEAD], axis=0, keepdims=True),
            jnp.sum(mixed[HEAD:], axis=0, keepdims=True),
        ],
        axis=1,
    )
    log_total = lse_ref[0, 0:1, :]
    limit = jnp.where(i < prompt_blocks, start, cut_ref[jnp.maximum(i - prompt_blocks, 0)])
    full = limit // bk
    rest = limit - full * bk

    def block(first, count, keep, begin):
        at = pl.ds(pl.multiple_of(first, BQ), count)
        keys = qkv_ref[at, PAIR : 2 * PAIR]
        values = qkv_ref[at, 2 * PAIR : 3 * PAIR]
        probs = jnp.exp2(dot_nt(keys, queries) * LOG2E - log_total)
        if keep is not None:
            probs = jnp.where(keep(probs.shape), probs, 0.0)
        dv_ref[at, :] += dot(probs.astype(jnp.bfloat16), grads)
        grad_probs = dot_nt(values, grads)
        grad_scores = (probs * (grad_probs - center)).astype(jnp.bfloat16)
        dk_ref[at, :] += dot(grad_scores, queries)
        part = lax.dot_general(keys, grad_scores, TN, preferred_element_type=jnp.float32)
        dq_ref[...] = part if begin else dq_ref[...] + part

    def causal(shape):
        key = lax.broadcasted_iota(jnp.int32, shape, 0)
        query = lax.broadcasted_iota(jnp.int32, shape, 1) & (BQ - 1)
        return key <= query

    block(start, BQ, causal, True)

    def step(j, none):
        block(j * bk, bk, None, False)
        return none

    lax.fori_loop(0, full, step, 0)

    @pl.when(rest > 0)
    def _():
        block(full * bk, bk, lambda s: lax.broadcasted_iota(jnp.int32, s, 0) < rest, False)

    grad_query = pick_lanes(jnp.transpose(dq_ref[...])) * HEAD**-0.5
    out_ref[pl.ds(start, BQ), 0:PAIR] = grad_query.astype(out_ref.dtype)

    @pl.when(i == pl.num_programs(0) - 1)
    def _():
        out_ref[:, PAIR : 2 * PAIR] = dk_ref[...].astype(out_ref.dtype)
        out_ref[:, 2 * PAIR : 3 * PAIR] = dv_ref[...].astype(out_ref.dtype)


def attend_back(cut, qkv, att, grad_att, log_totals):
    tokens = qkv.shape[0]
    pairs = 2 * tokens * tokens // 4
    return pl.pallas_call(
        functools.partial(attend_back_kernel, BK_BACK),
        grid=(tokens // BQ,),
        in_specs=[
            pl.BlockSpec(memory_space=pltpu.SMEM),
            fixed((tokens, 3 * PAIR)),
            fixed((tokens, PAIR)),
            fixed((tokens, PAIR)),
            pl.BlockSpec((1, 8, 2 * BQ), lambda i: (i, 0, 0)),
        ],
        out_specs=fixed((tokens, 3 * PAIR)),
        out_shape=jax.ShapeDtypeStruct((tokens, 3 * PAIR), jnp.bfloat16),
        scratch_shapes=[
            pltpu.VMEM((tokens, PAIR), jnp.float32),
            pltpu.VMEM((tokens, PAIR), jnp.float32),
            pltpu.VMEM((PAIR, 2 * BQ), jnp.float32),
        ],
        compiler_params=params(60),
        cost_estimate=cost(10 * 2 * pairs * 256, 2 * tokens * 8 * PAIR, pairs),
        name="attend_back",
    )(cut, qkv, att, grad_att, log_totals)


def centered(values):
    center = values - jnp.mean(values, axis=-1, keepdims=True)
    spread = jnp.mean(center * center, axis=-1, keepdims=True)
    inverse = lax.rsqrt(spread + EPSILON)
    return center * inverse, inverse


def norm_back(grad, gain, unit, inverse):
    scaled = grad * gain
    mean_one = jnp.mean(scaled, axis=-1, keepdims=True)
    mean_two = jnp.mean(scaled * unit, axis=-1, keepdims=True)
    return (scaled - mean_one - unit * mean_two) * inverse


def out_block(w_ref, r, c, rows):
    width = w_ref.shape[3] // rows
    return jnp.concatenate(
        [w_ref[r, c, :, h * width : (h + 1) * width] for h in range(rows)], axis=0
    )


def out_weight_spec(weight):
    rows, cols, depth, width = weight.shape
    at = 4
    return pl.BlockSpec(
        (rows, cols, PAIR, width), lambda *_: (0, 0, at, 0), pipeline_mode=pl.Buffered(1)
    )


def middle_kernel(
    rows, cols, tok_ref, att_ref, w_ref, vec_ref, middle_ref, normed_ref, turned_ref
):
    parts = []
    for c in range(cols):
        parts.append(jnp.concatenate([att_ref[r, c] for r in range(rows)], axis=1))
    pieces = []
    for r in range(rows):
        total = dot(parts[0], out_block(w_ref, r, 0, rows))
        for c in range(1, cols):
            total = total + dot(parts[c], out_block(w_ref, r, c, rows))
        pieces.append(total)
    middle = tok_ref[...].astype(jnp.float32) + jnp.concatenate(pieces, axis=1) + vec_ref[0:1]
    middle_ref[...] = middle
    normed = (centered(middle)[0] * vec_ref[1:2] + vec_ref[2:3]).astype(jnp.bfloat16)
    normed_ref[...] = normed
    turned_ref[...] = jnp.transpose(normed)


def project_out(tokens, att, weight, vectors):
    rows, cols, span, _ = att.shape
    model = tokens.shape[1]
    tile = min(256, span)
    return pl.pallas_call(
        functools.partial(middle_kernel, rows, cols),
        grid=(span // tile,),
        in_specs=[
            pl.BlockSpec((tile, model), lambda i: (i, 0)),
            pl.BlockSpec((rows, cols, tile, PAIR), lambda i: (0, 0, i, 0)),
            out_weight_spec(weight),
            fixed(vectors.shape),
        ],
        out_specs=[
            pl.BlockSpec((tile, model), lambda i: (i, 0)),
            pl.BlockSpec((tile, model), lambda i: (i, 0)),
            pl.BlockSpec((model, tile), lambda i: (0, i)),
        ],
        out_shape=[
            jax.ShapeDtypeStruct((span, model), jnp.float32),
            jax.ShapeDtypeStruct((span, model), jnp.bfloat16),
            jax.ShapeDtypeStruct((model, span), jnp.bfloat16),
        ],
        compiler_params=params(60),
        cost_estimate=cost(2 * span * model * model, 2 * model * model + 12 * span * model),
        name="out_norm",
    )(tokens, att, weight, vectors)


def store_grads(rows, dps, turned_refs, cot_turned_ref, low_all, active_all, grad_ref):
    turned_all = jnp.concatenate([ref[...] for ref in turned_refs], axis=1)
    cut = turned_all.shape[0] // (rows * dps)
    for which, weight_grad in enumerate(
        (dot(turned_all, low_all), dot(cot_turned_ref[...], active_all))
    ):
        weight_grad = weight_grad.astype(jnp.bfloat16)
        for r in range(rows):
            for d in range(dps):
                at = (d * rows + r) * cut
                grad_ref[r, 0, d, which * cut : (which + 1) * cut] = weight_grad[at : at + cut]


def hidden_grad_kernel(rows, dps, groups, *refs):
    lows, actives = refs[groups + 1 : 2 * groups + 1], refs[2 * groups + 1 : -1]
    low_all = jnp.concatenate([ref[0] for ref in lows], axis=0)
    active_all = jnp.concatenate([ref[0] for ref in actives], axis=0)
    store_grads(rows, dps, refs[:groups], refs[groups], low_all, active_all, refs[-1])


def hidden_grad(turned, cot_turned, low, active, dps, rows):
    groups = len(low)
    cols, span, local = low[0].shape
    tokens = groups * span
    model = cot_turned.shape[0]
    tile = min(HIDDEN_TILE, local)
    cut = model // (rows * dps)
    piece = pl.BlockSpec((1, span, tile), lambda c, i: (c, 0, i))
    return pl.pallas_call(
        functools.partial(hidden_grad_kernel, rows, dps, groups),
        grid=(cols, local // tile),
        in_specs=[fixed(part.shape) for part in turned]
        + [fixed(cot_turned.shape)]
        + [piece] * (2 * groups),
        out_specs=pl.BlockSpec((rows, 1, dps, 2 * cut, tile), lambda c, i: (0, c, 0, 0, i)),
        out_shape=jax.ShapeDtypeStruct(
            (rows, cols, dps, 2 * cut + cut // 2, local), jnp.bfloat16
        ),
        compiler_params=params(60),
        cost_estimate=cost(4 * tokens * model * cols * local, 8 * model * cols * local),
        name="hidden_grad",
    )(*turned, cot_turned, *low, *active)


def hidden_kernel(rows, dps, groups, first, *refs):
    normed_refs, refs = refs[:groups], refs[groups:]
    if first:
        turned_refs, cot_turned_ref, refs = refs[:groups], refs[groups], refs[groups + 1 :]
    cot_refs, refs = refs[:groups], refs[groups:]
    w_ref, fc_bias_ref = refs[:2]
    if first:
        starts = refs[2 : groups + 2]
        out_accs = refs[groups + 2 : 2 * groups + 2]
        back_accs = refs[2 * groups + 2 : 3 * groups + 2]
        grad_ref, bias_ref, sems = refs[3 * groups + 2 :]
        ends = out_accs
    else:
        proj_bias_ref = refs[4]
        out_ref, back_acc, low_ref, active_ref, bias_ref, out_acc, sems = refs[5:]
        starts, ends = refs[2:4], (out_acc, back_acc)
        out_accs, back_accs = (out_acc,), (back_acc,)
    step = pl.program_id(0) * pl.num_programs(1) + pl.program_id(1)
    last = pl.num_programs(0) * pl.num_programs(1) - 1
    model = normed_refs[0].shape[1]
    tile = w_ref.shape[3]
    depth = model // rows
    copies = [
        pltpu.make_async_copy(start, end, sems.at[at])
        for at, (start, end) in enumerate(zip(starts, ends))
    ]

    @pl.when(step == 0)
    def _():
        for copy in copies:
            copy.start()
        if first:
            for back_acc in back_accs:
                back_acc[...] = jnp.zeros_like(back_acc)

    fc_weight = w_ref[:, 0, :depth].reshape(model, tile)
    proj_turned = w_ref[:, 0, depth:].reshape(model, tile)
    root = 0.7978845608028654
    actives, lows = [], []
    for g in range(groups):
        hidden = dot(normed_refs[g][...], fc_weight) + fc_bias_ref[0]
        square = hidden * hidden
        inner = jnp.tanh(hidden * (root + (root * 0.044715) * square))
        plus = 0.5 + 0.5 * inner
        actives.append((hidden * plus).astype(jnp.bfloat16))
        bend = 0.5 - 0.5 * inner * inner
        slope = plus + hidden * bend * (root + (3 * root * 0.044715) * square)
        grad_active = dot(cot_refs[g][...], proj_turned)
        lows.append((grad_active * slope).astype(jnp.bfloat16))
    bias_ref[0] = functools.reduce(
        jnp.add, [jnp.sum(low.astype(jnp.float32), axis=0, keepdims=True) for low in lows]
    )
    if first:
        store_grads(
            rows,
            dps,
            turned_refs,
            cot_turned_ref,
            jnp.concatenate(lows, axis=0),
            jnp.concatenate(actives, axis=0),
            grad_ref,
        )
    else:
        low_ref[0] = lows[0]
        active_ref[0] = actives[0]

    @pl.when(step == 0)
    def _():
        for copy in copies:
            copy.wait()

    for g in range(groups):
        out_accs[g][...] += dot_nt(actives[g], proj_turned)
        back_accs[g][...] += dot_nt(lows[g], fc_weight)
    if not first:

        @pl.when(step == last)
        def _():
            out_ref[...] = (out_acc[...] + proj_bias_ref[...]).astype(out_ref.dtype)


def feed_forward(first, normed, turned, cot, weight, fc_bias, rest, dps):
    groups = len(normed)
    span, model = normed[0].shape
    tokens = groups * span
    rows, cols, _, local = weight.shape
    depth = model // rows
    tile = min(HIDDEN_TILE, local)
    cut = model // (rows * dps)
    acc_shape = jax.ShapeDtypeStruct((span, model), jnp.float32)
    anywhere = pl.BlockSpec(memory_space=pl.ANY)
    whole = fixed((span, model))
    if first:
        rest_specs = [anywhere] * groups
        out_shape = [acc_shape] * (2 * groups)
        scratch = [pltpu.SemaphoreType.DMA((groups,))]
        grad_specs = [pl.BlockSpec((rows, 1, dps, 2 * cut, tile), lambda c, i: (0, c, 0, 0, i))]
        grad_shapes = [jax.ShapeDtypeStruct((rows, cols, dps, 2 * cut, local), jnp.bfloat16)]
    else:
        rest_specs = [anywhere, anywhere, fixed((1, model))]
        out_shape = [jax.ShapeDtypeStruct((span, model), jnp.bfloat16), acc_shape]
        scratch = [pltpu.VMEM((span, model), jnp.float32), pltpu.SemaphoreType.DMA((2,))]
        grad_specs = [pl.BlockSpec((1, span, tile), lambda c, i: (c, 0, i))] * 2
        grad_shapes = [jax.ShapeDtypeStruct((cols, span, local), jnp.bfloat16)] * 2
    products = 12 if first else 8
    return pl.pallas_call(
        functools.partial(hidden_kernel, rows, dps, groups, first),
        grid=(cols, local // tile),
        in_specs=[whole] * groups
        + [fixed(part.shape) for part in turned]
        + [whole] * groups
        + [
            pl.BlockSpec((rows, 1, 2 * depth, tile), lambda c, i: (0, c, 0, i)),
            pl.BlockSpec((1, 1, tile), lambda c, i: (c, 0, i)),
        ]
        + rest_specs,
        out_specs=[whole] * len(out_shape)
        + grad_specs
        + [pl.BlockSpec((1, 1, tile), lambda c, i: (c, 0, i))],
        out_shape=out_shape
        + grad_shapes
        + [jax.ShapeDtypeStruct((cols, 1, local), jnp.float32)],
        scratch_shapes=scratch,
        compiler_params=params(60),
        cost_estimate=cost(
            products * tokens * model * cols * local,
            8 * model * cols * local,
            tokens * cols * local,
        ),
        name="feed_forward_first" if first else "feed_forward_second",
    )(*normed, *turned, *cot, weight, fc_bias, *rest)


def middle_back_kernel(
    rows, cols, grad_ref, middle_ref, cot_ref, w_ref, vec_ref, dx_ref, turned_ref, datt_ref, sum_ref
):
    grad = grad_ref[...]
    unit, inverse = centered(middle_ref[...])
    total = cot_ref[...].astype(jnp.float32) + norm_back(grad, vec_ref[1:2], unit, inverse)
    dx_ref[...] = total
    low = total.astype(jnp.bfloat16)
    turned_ref[...] = jnp.transpose(low)
    depth = w_ref.shape[3] // rows
    for c in range(cols):
        part = dot_nt(low[:, :depth], out_block(w_ref, 0, c, rows))
        for r in range(1, rows):
            part = part + dot_nt(low[:, r * depth : (r + 1) * depth], out_block(w_ref, r, c, rows))
        part = part.astype(jnp.bfloat16)
        for r in range(rows):
            datt_ref[r, c] = part[:, r * PAIR : (r + 1) * PAIR]

    @pl.when(pl.program_id(0) == 0)
    def _():
        sum_ref[...] = jnp.zeros_like(sum_ref)

    sum_ref[0:1] += jnp.sum(grad * unit, axis=0, keepdims=True)
    sum_ref[1:2] += jnp.sum(grad, axis=0, keepdims=True)
    sum_ref[2:3] += jnp.sum(low.astype(jnp.float32), axis=0, keepdims=True)


def middle_back(grad, middle, cot, weight, vectors):
    span, model = middle.shape
    rows, cols = weight.shape[:2]
    tile = min(256, span)
    return pl.pallas_call(
        functools.partial(middle_back_kernel, rows, cols),
        grid=(span // tile,),
        in_specs=[
            pl.BlockSpec((tile, model), lambda i: (i, 0)),
            pl.BlockSpec((tile, model), lambda i: (i, 0)),
            pl.BlockSpec((tile, model), lambda i: (i, 0)),
            out_weight_spec(weight),
            fixed(vectors.shape),
        ],
        out_specs=[
            pl.BlockSpec((tile, model), lambda i: (i, 0)),
            pl.BlockSpec((model, tile), lambda i: (0, i)),
            pl.BlockSpec((rows, cols, tile, PAIR), lambda i: (0, 0, i, 0)),
            pl.BlockSpec((8, model), lambda i: (0, 0)),
        ],
        out_shape=[
            jax.ShapeDtypeStruct((span, model), jnp.float32),
            jax.ShapeDtypeStruct((model, span), jnp.bfloat16),
            jax.ShapeDtypeStruct((rows, cols, span, PAIR), jnp.bfloat16),
            jax.ShapeDtypeStruct((8, model), jnp.float32),
        ],
        compiler_params=params(60),
        cost_estimate=cost(2 * span * model * model, 2 * model * model + 18 * span * model),
        name="out_norm_back",
    )(grad, middle, cot, weight, vectors)


def out_grad_kernel(rows, dps, groups, *refs):
    out_ref = refs[-1]
    total = None
    for g in range(groups):
        att = jnp.concatenate([refs[groups + g][r, 0] for r in range(rows)], axis=1)
        part = dot(refs[g][...], att)
        total = part if total is None else total + part
    total = total.astype(jnp.bfloat16)
    half = out_ref.shape[3]
    for r in range(rows):
        for d in range(dps):
            at = (d * rows + r) * 2 * half
            out_ref[r, 0, d] = jnp.concatenate(
                [total[at : at + half], total[at + half : at + 2 * half]], axis=1
            )


def out_grad(turned, att, before, dps):
    groups = len(turned)
    model, span = turned[0].shape
    rows, cols = att[0].shape[:2]
    cut = model // (rows * dps)
    return pl.pallas_call(
        functools.partial(out_grad_kernel, rows, dps, groups),
        grid=(cols,),
        in_specs=[fixed((model, span))] * groups
        + [pl.BlockSpec((rows, 1, span, PAIR), lambda c: (0, c, 0, 0))] * groups
        + [pl.BlockSpec(memory_space=pl.ANY)],
        out_specs=pl.BlockSpec(
            (rows, 1, dps, cut // 2, 2 * rows * PAIR), lambda c: (0, c, 0, 4, 0)
        ),
        out_shape=jax.ShapeDtypeStruct(before.shape, before.dtype),
        compiler_params=params(60),
        cost_estimate=cost(2 * groups * span * model * model, 2 * model * model),
        input_output_aliases={2 * groups: 0},
        name="out_grad",
    )(*turned, *att, before)


def qkv_grad_kernel(final, dqkv_ref, x_ref, *refs):
    grad_ref, bias_ref, acc = refs[-3:]
    step = pl.program_id(0)
    grads = dqkv_ref[...]
    rows = x_ref[...].reshape(grads.shape[0], x_ref.shape[2])
    part = lax.dot_general(grads, rows, TN, preferred_element_type=jnp.float32)
    sums = jnp.sum(grads.astype(jnp.float32), axis=0, keepdims=True)

    @pl.when(step == 0)
    def _():
        acc[...] = refs[0][...] + part if final else part
        bias_ref[...] = jnp.zeros_like(bias_ref)

    @pl.when(step > 0)
    def _():
        acc[...] += part

    bias_ref[0:1] += sums

    @pl.when(step == pl.num_programs(0) - 1)
    def _():
        grad_ref[...] = jnp.transpose(acc[...]).astype(grad_ref.dtype) if final else acc[...]


def qkv_grad(dqkv, normed, before):
    tokens, width = dqkv.shape
    members, _, model = normed.shape
    final = len(before) == 1
    tile = 2 * tokens // members
    grad_type = (
        jax.ShapeDtypeStruct((model, width), jnp.bfloat16)
        if final
        else jax.ShapeDtypeStruct((width, model), jnp.float32)
    )
    return pl.pallas_call(
        functools.partial(qkv_grad_kernel, final),
        grid=(tokens // tile,),
        in_specs=[
            pl.BlockSpec((tile, width), lambda i: (i, 0)),
            pl.BlockSpec((2, tile // 2, model), lambda i: (i, 0, 0)),
        ]
        + [fixed((width, model))] * len(before),
        out_specs=[fixed(grad_type.shape), fixed((8, width))],
        out_shape=[grad_type, jax.ShapeDtypeStruct((8, width), jnp.float32)],
        scratch_shapes=[pltpu.VMEM((width, model), jnp.float32)],
        compiler_params=params(60),
        cost_estimate=cost(2 * tokens * model * width, 2 * tokens * (model + width)),
        name="qkv_grad",
    )(dqkv, normed, *before)


def input_kernel(rows, dps, plane_ref, dqkv_ref, left_ref, right_ref, dx_ref, tok_ref, *refs):
    gain_ref = refs[0]
    out_ref, sum_ref, acc = refs[-3:]
    step = pl.program_id(0) * pl.num_programs(1) + pl.program_id(1)
    short = left_ref.shape[3] * 2 // 3
    grads = []
    for part in range(3):
        lanes = slice(part * PAIR, (part + 1) * PAIR)
        grads += [dqkv_ref[half, 0, :, lanes] for half in range(2)]
    pieces = []
    for r in range(rows):
        for d in range(dps):
            at = (plane_ref[0] - d) & (dps - 1)
            left, right = left_ref[at, r, 0], right_ref[at, r, 0]
            last = jnp.concatenate([left[short:], right[short:]], axis=0)
            pieces.append(jnp.concatenate([left[:short], right[:short], last], axis=1))
    weights = jnp.concatenate(pieces, axis=0)
    piece = dot_nt(jnp.concatenate(grads, axis=1), weights)

    @pl.when(step == 0)
    def _():
        acc[...] = piece

    @pl.when(step > 0)
    def _():
        acc[...] += piece

    @pl.when(step == pl.num_programs(0) * pl.num_programs(1) - 1)
    def _():
        grad = acc[...]
        unit, inverse = centered(tok_ref[0].astype(jnp.float32))
        out_ref[0] = dx_ref[...] + norm_back(grad, gain_ref[...], unit, inverse)
        sum_ref[0:1] = jnp.sum(grad * unit, axis=0, keepdims=True)
        sum_ref[1:2] = jnp.sum(grad, axis=0, keepdims=True)


def input_back(plane, dqkv, dx, tokens, weight, gain, before, g):
    dps, rows, cols, high, _ = weight.shape
    span, model = dx.shape
    return pl.pallas_call(
        functools.partial(input_kernel, rows, dps),
        grid=(rows // 2, cols),
        in_specs=[
            pl.BlockSpec(memory_space=pltpu.SMEM),
            pl.BlockSpec((2, 1, span, 3 * PAIR), lambda i, c: (i, c, 0, 0)),
            pl.BlockSpec((dps, rows, 1, high, 2 * PAIR), lambda i, c: (0, 0, c, 0, i)),
            pl.BlockSpec((dps, rows, 1, high, 2 * PAIR), lambda i, c: (0, 0, c, 0, rows // 2 + i)),
            fixed((span, model)),
            pl.BlockSpec((1, span, model), lambda i, c: (g, 0, 0), pipeline_mode=pl.Buffered(1)),
            fixed((1, model)),
        ]
        + [pl.BlockSpec(memory_space=pl.ANY)] * len(before),
        out_specs=[
            pl.BlockSpec((1, span, model), lambda i, c: (g, 0, 0), pipeline_mode=pl.Buffered(1)),
            fixed((8, model)),
        ],
        out_shape=[
            jax.ShapeDtypeStruct(tokens.shape, jnp.float32),
            jax.ShapeDtypeStruct((8, model), jnp.float32),
        ],
        scratch_shapes=[pltpu.VMEM((span, model), jnp.float32)],
        compiler_params=params(60),
        cost_estimate=cost(6 * span * model * model, 6 * model * model + 12 * span * model),
        input_output_aliases={7: 0} if before else {},
        name="input_back",
    )(plane, dqkv, weight, weight, dx, tokens, gain, *before)


def head_body(
    tokens,
    cotangent,
    branch,
    ln1_gain,
    ln1_bias,
    qkv_weight,
    qv_bias,
    out_weight,
    out_bias,
    ln2_gain,
    ln2_bias,
    fc_weight,
    fc_bias,
    proj_weight,
    proj_bias,
):
    groups, span, model = tokens.shape
    rows = lax.axis_size("row")
    cols = lax.axis_size("col")
    dps = lax.axis_size("dp")
    members = rows * cols
    count = groups * span
    head_cols = qv_bias.shape[1]
    hidden_cols = fc_bias.shape[0]

    def spread(shard):
        whole = lax.all_gather(shard, MESH_AXES, axis=0, tiled=False)
        return whole.reshape((rows, cols) + shard.shape)

    def swap(blocks):
        return lax.all_to_all(blocks, MESH_AXES, 0, 0, tiled=True)

    def collect_plane(partial):
        partial = partial.reshape((members,) + partial.shape[2:])
        partial = lax.psum_scatter(partial, MESH_AXES, scatter_dimension=0, tiled=True)
        return partial.reshape(partial.shape[1:])

    def exchange_dp(partial):
        me = lax.axis_index("dp")
        summed = lax.dynamic_index_in_dim(partial, me, 0, False).astype(jnp.float32)
        for shift in range(1, dps):
            piece = lax.dynamic_index_in_dim(partial, (me + shift) % dps, 0, False)
            pairs = [(i, (i + shift) % dps) for i in range(dps)]
            summed = summed + lax.ppermute(piece, "dp", pairs).astype(jnp.float32)
        return summed

    def collect_dp(partial):
        partial = lax.psum_scatter(partial, "dp", scatter_dimension=0, tiled=True)
        return partial[0].astype(jnp.float32)

    def total(values):
        for axis in ("row", "col", "dp"):
            size = lax.axis_size(axis)
            step = 1
            while step < size:
                partners = (step, 2 * step, 3 * step) if 4 * step <= size else (step,)
                parts = [values] + [
                    lax.ppermute(values, axis, [(i, i ^ other) for i in range(size)])
                    for other in partners
                ]
                values = parts[0] + parts[1]
                if len(parts) == 4:
                    values = values + (parts[2] + parts[3])
                step *= len(parts)
        return values

    half = hidden_cols // 2
    residual = tokens.astype(jnp.float32)
    normed = normalize(residual, ln1_gain, ln1_bias).astype(jnp.bfloat16)
    row = lax.axis_index("row")
    col = lax.axis_index("col")
    own = qkv_weight.reshape(-1, 3, rows, PAIR).transpose(2, 0, 1, 3)
    own = lax.all_to_all(own.reshape(rows, -1, 3 * PAIR), "row", 0, 0, tiled=True)
    own = own.reshape(model, 3 * PAIR)
    own_bias = lax.dynamic_slice_in_dim(qv_bias, row * PAIR, PAIR, 1)
    own_bias = jnp.concatenate([own_bias[0], jnp.zeros((PAIR,), jnp.float32), own_bias[1]])
    fc_full = lax.all_gather(fc_bias, "col", axis=0).reshape(cols, 1, hidden_cols)

    normed_all = [lax.all_gather(normed[0], MESH_AXES, axis=0, tiled=False)]
    cot_flat = cotangent.reshape(count, model)
    cot_turned = cot_flat.T
    toks = [tokens[g] for g in range(groups)]
    cots = [cotangent[g] for g in range(groups)]
    proj_bias_sum = jnp.sum(cot_flat.astype(jnp.float32), axis=0)
    plane = lax.axis_index("dp")
    short = qkv_weight.shape[0] // dps
    part = lax.dynamic_slice_in_dim(qkv_weight, plane * short, short, 0)
    last = jnp.concatenate([part[: short // 2, 2], part[short // 2 :, 2]], axis=1)
    part = jnp.concatenate([part[:, 0], part[:, 1]], axis=1)
    later = jnp.concatenate([normed[1], part, last], axis=0)
    shards = pack_weights(fc_weight, proj_weight, out_weight)
    normed_all[0], later, cot_turned, proj_bias_sum, shards, own, fc_full = (
        lax.optimization_barrier(
            (normed_all[0], later, cot_turned, proj_bias_sum, shards, own, fc_full)
        )
    )
    later = lax.all_gather(later, MESH_AXES, axis=0, tiled=False)
    normed_all.append(later)
    vectors = jnp.stack([out_bias, ln2_gain, ln2_bias] + [out_bias] * 5)
    gains = jnp.stack([ln2_gain] * 8)
    qkv, att, att_own, log_totals, middle, normed_two, turned_two = [], [], [], [], [], [], []
    w_first = spread(shards[0])
    w_second = spread(shards[1])
    def step_up(value):
        return lax.ppermute(value, "dp", [(i, i + 1) for i in range(dps - 1)])

    def step_down(value):
        return lax.ppermute(value, "dp", [(i + 1, i) for i in range(dps - 1)])

    for g in range(groups):
        qkv.append(project_qkv(normed_all[g], own, own_bias, span))
        mixed, totals = attend(branch[g], qkv[g])
        if g < groups - 1:
            mixed, normed_all[g + 1] = lax.optimization_barrier((mixed, normed_all[g + 1]))
        att_own.append(mixed)
        if g > 0:
            quarter = normed_all[1][:, span:].reshape(rows, cols, -1, model)
            ups, downs = [step_up(quarter)], [step_down(quarter)]
            mixed, att[g - 1], ups, downs = lax.optimization_barrier(
                (mixed, att[g - 1], ups, downs)
            )
            ups.append(step_up(ups[-1]))
            downs.append(step_down(downs[-1]))
        log_totals.append(totals)
        att.append(swap(mixed.reshape(members, span, PAIR)).reshape(rows, cols, span, PAIR))
    for g in range(groups):
        mid, low, turned = project_out(toks[g], att[g], w_first, vectors)
        middle.append(mid)
        normed_two.append(low)
        turned_two.append(turned)
    all_turned = turned_two + [cot_turned]
    normed_two[-1], ups, downs = lax.optimization_barrier((normed_two[-1], ups, downs))
    ups.append(step_up(ups[-1]))
    downs.append(step_down(downs[-1]))
    first_parts = feed_forward(
        True, normed_two, all_turned, cots, w_first, fc_full[:, :, :half], middle, dps
    )
    grad_first, fc_sum_first = first_parts[2 * groups :]
    plane_first = collect_plane(grad_first)
    block_out, low, active, fc_sums = [], [], [], []
    dx, dx_turned, grad_att, sums_two = [], [], [], []
    for g in range(groups):
        output_rows, grad_two, low_part, active_part, fc_part = feed_forward(
            False,
            [normed_two[g]],
            [],
            [cots[g]],
            w_second,
            fc_full[:, :, half:],
            (first_parts[g], first_parts[groups + g], proj_bias[None]),
            dps,
        )
        block_out.append(output_rows)
        low.append(low_part)
        active.append(active_part)
        fc_sums.append(fc_part)
        rows_grad, turned, datt, sums = middle_back(
            grad_two, middle[g], cots[g], w_first, gains
        )
        dx.append(rows_grad)
        dx_turned.append(turned)
        sums_two.append(sums)
        if g == 0:
            datt, normed_two[1] = lax.optimization_barrier((datt, normed_two[1]))
        grad_att.append(
            swap(datt.reshape(members, span, PAIR)).reshape(members * span, PAIR)
        )
    fc_sum_second = functools.reduce(jnp.add, fc_sums)
    grad_second = hidden_grad(turned_two, cot_turned, low, active, dps, rows)
    grad_att[0], grad_second = lax.optimization_barrier((grad_att[0], grad_second))
    plane_second = collect_plane(out_grad(dx_turned, att, grad_second, dps))
    rows_back, grads, bias_sums, before = [], [], [], []
    for g in range(groups):
        grad = attend_back(branch[g], qkv[g], att_own[g], grad_att[g], log_totals[g])
        if g == 0:
            grad, grad_att[1], plane_first = lax.optimization_barrier(
                (grad, grad_att[1], plane_first)
            )
            hidden_first = exchange_dp(plane_first)
        else:
            grad, rows_back[0], hidden_first, grads[0], ups, downs = lax.optimization_barrier(
                (grad, rows_back[0], hidden_first, grads[0], ups, downs)
            )
        rows_back.append(grad)
        grads.append(
            swap(grad.reshape(members, span, 3 * PAIR)).reshape(rows, cols, span, 3 * PAIR)
        )
    for g in range(groups):
        grad_qkv, bias_sum = qkv_grad(rows_back[g], normed_all[g], before)
        before = [grad_qkv]
        bias_sums.append(bias_sum[0])
        if g == 0:
            before[0], plane_second = lax.optimization_barrier((before[0], plane_second))
            hidden_second = collect_dp(plane_second)
    grads[0], grad_qkv = lax.optimization_barrier((grads[0], grad_qkv))
    grad_qkv = exchange_dp(grad_qkv.reshape(dps, rows, -1, 3 * PAIR))
    quarters = [quarter]
    for shift in range(1, dps):
        quarters.append(jnp.where(plane >= shift, ups[shift - 1], downs[dps - shift - 1]))
    w_qkv = jnp.stack(quarters)
    input_grads, sums_one = [], []
    for g in range(groups):
        rows_grad, sums = input_back(
            plane[None], grads[g], dx[g], tokens, w_qkv, ln1_gain[None], input_grads, g
        )
        input_grads = [rows_grad]
        sums_one.append(sums)
    sums_two = functools.reduce(jnp.add, sums_two)
    fc_sum = jnp.concatenate([fc_sum_first, fc_sum_second], axis=2).reshape(-1)
    sums_one = functools.reduce(jnp.add, sums_one)
    bias_sum = functools.reduce(jnp.add, bias_sums)
    qv_sum = jnp.zeros((2, model), jnp.float32)
    qv_sum = lax.dynamic_update_slice(
        qv_sum,
        jnp.stack([bias_sum[:PAIR], bias_sum[2 * PAIR :]]),
        (0, col * head_cols + row * PAIR),
    )
    small = (sums_two[2], sums_two[0], sums_two[1], fc_sum, proj_bias_sum)
    small += (sums_one[0], sums_one[1], qv_sum.reshape(-1))
    small = total(jnp.concatenate(small))
    grad_qkv = lax.all_to_all(grad_qkv, "row", 0, 0, tiled=True)
    d_qkv = grad_qkv.reshape(rows, -1, 3, PAIR).transpose(1, 2, 0, 3).reshape(-1, 3, head_cols)
    cut = model // (rows * dps)
    d_fc, d_proj = (
        jnp.concatenate([hidden_first[at : at + cut], hidden_second[at : at + cut]], axis=1)
        for at in (0, cut)
    )
    packed_out = hidden_second[2 * cut :]
    d_out = jnp.concatenate([packed_out[:, :head_cols], packed_out[:, head_cols:]], axis=0).T
    parts, at = [], 0
    for size in (model, model, model, hidden_cols * cols, model, model, model, 2 * model):
        parts.append(small[at : at + size])
        at += size
    s_out, s_gain_two, s_bias_two, s_fc, s_proj, s_gain_one, s_bias_one, s_qv = parts
    return (
        jnp.stack(block_out),
        input_grads[0],
        s_gain_one,
        s_bias_one,
        d_qkv,
        s_qv.reshape(2, model),
        d_out,
        s_out,
        s_gain_two,
        s_bias_two,
        d_fc,
        s_fc,
        d_proj.T,
        s_proj,
    )


def by_heads(mesh):
    rows, cols = mesh.shape["row"], mesh.shape["col"]

    def body(tokens, cotangent, branch, ln1_gain, ln1_bias, qkv_weight, *rest):
        width = qkv_weight.shape[2] * cols
        whole = tokens.shape[1] * rows * cols
        fits = width == rows * cols * PAIR and rows == 4 and mesh.shape["dp"] == 4 and tokens.shape[0] == 2
        fits = fits and qkv_weight.shape[0] * 4 == qkv_weight.shape[2] * cols
        fits = fits and rest[6].shape[0] == 4 * rows * PAIR
        fits = fits and all(size & (size - 1) == 0 for size in mesh.shape.values())
        fits = fits and whole == PLEN + CONTS * CLEN and tokens.shape[1] % BQ == 0
        chosen = head_body if fits else gathered_body
        return chosen(tokens, cotangent, branch, ln1_gain, ln1_bias, qkv_weight, *rest)

    return body


def solution(mesh):
    placed = (
        P("dp", ("row", "col"), None),
        P("dp", ("row", "col"), None),
        P("dp", None),
        P(),
        P(),
        P("row", None, "col"),
        P(None, "col"),
        P("col", "row"),
        P(),
        P(),
        P(),
        P("row", "col"),
        P("col"),
        P("col", "row"),
        P(),
    )
    return jax.shard_map(
        by_heads(mesh),
        mesh=mesh,
        in_specs=placed,
        out_specs=(
            P("dp", ("row", "col"), None),
            P("dp", ("row", "col"), None),
            P(),
            P(),
            P(("dp", "row"), None, "col"),
            P(),
            P("col", ("dp", "row")),
            P(),
            P(),
            P(),
            P(("dp", "row"), "col"),
            P(),
            P("col", ("dp", "row")),
            P(),
        ),
        check_vma=False,
    )
```
